128 devices in a mesh: seq: 16 (over z, y), head: 8 (over x, core).
Axes of the slice: x: 4, y: 4, z: 4, core: 2. Of those that a mesh axis runs over, the one named last changes fastest.
Arguments:
- ssd_input: bfloat16 [8192, 128, 128], P('seq', 'head'), may hold values from -3 to 3
- log_decay: float32 [8192, 128], P('seq', 'head'), may hold values from -1.6 to 0, as said below
- input_map: float32 [8192, 8, 128], P('seq', 'head'), may hold values from -0.18 to 0.18
- output_map: float32 [8192, 8, 128], P('seq', 'head'), may hold values from -0.18 to 0.18
- ssd_cotangent: bfloat16 [8192, 128, 128], P('seq', 'head'), may hold values from -3 to 3
- queries: bfloat16 [8192, 8, 128], P('seq', 'head'), may hold values from -100 to 100
- key_rows: bfloat16 [8192, 128], P('seq'), may hold values from -4 to 4
- value_rows: bfloat16 [8192, 128], P('seq'), may hold values from -6 to 6
- attn_cotangent: bfloat16 [8192, 8, 128], P('seq', 'head'), may hold values from -6 to 6
- pair_order: int32 [16], replicated, may hold values from 0 to 15, each once
Outputs:
- grad_input: bfloat16 [8192, 128, 128], P('seq', 'head')
- grad_decay: float32 [8192, 128], P('seq', 'head')
- grad_input_map: float32 [8192, 8, 128], P('seq', 'head')
- grad_output_map: float32 [8192, 8, 128], P('seq', 'head')
- grad_queries: bfloat16 [8192, 8, 128], P('seq', 'head')
- grad_keys: bfloat16 [8192, 128], P('seq')
- grad_values: bfloat16 [8192, 128], P('seq')
The draws below stay inside these ranges and needn't reach their ends.
Inputs may be any that keep to these rules, and one draw needn't show every extreme that they name: `pair_order`: a permutation of 0 to 15. `log_decay`: negative everywhere.
All inputs are finite; a program needn't handle non-finite values.
Results may differ from the reference program's by a relative error of at most 0.035.
Values may be sent and summed in bfloat16 or wider, within the bound.
No kernel may reach another device: no remote copies, remote signals or barrier semaphores. Data moves between devices by JAX's collectives and lax.ppermute only.
A program may use at most 192 MiB of HBM per device.

```python
import math
import jax
import jax.numpy as jnp
from jax import lax

SCAN_HEADS = 128
GROUPS = 8
HEAD_DIM = 128
STATE = 128
Q_HEADS = 8
ATT_DIM = 128
BLOCK = 128
TOK_DEV = 512
SEQUENCE_TOKENS = 8192
HALF = 256
N_SEQ = 16


def draw_log_decay(key, part):
    segments = jax.random.split(key, 7)
    fast_share = 0.5
    fast_heads = jax.random.uniform(segments[0], (SCAN_HEADS,)) < fast_share
    fast_rate = jnp.exp(jax.random.uniform(segments[1], (SCAN_HEADS,), minval=math.log(1.0 / 50.0), maxval=math.log(1.0 / 30.0)))
    slow_rate = jnp.exp(jax.random.uniform(segments[2], (SCAN_HEADS,), minval=math.log(0.1), maxval=math.log(0.4))) / SEQUENCE_TOKENS
    baseline_rate = jnp.where(fast_heads, fast_rate, slow_rate)
    block_multiplier = jnp.exp(jax.random.uniform(segments[3], (SEQUENCE_TOKENS // TOK_DEV, SCAN_HEADS), minval=math.log(0.5), maxval=math.log(2.0)))
    block_multiplier = jnp.repeat(block_multiplier, TOK_DEV, axis=0)
    token_multiplier = jax.random.uniform(segments[4], (SEQUENCE_TOKENS, SCAN_HEADS), minval=0.5, maxval=1.5)
    packet_rows = jax.random.randint(segments[5], (2,), 0, SEQUENCE_TOKENS)
    packet_size = jax.random.uniform(segments[6], (2, SCAN_HEADS), minval=0.22, maxval=0.69)
    row_position = jnp.arange(SEQUENCE_TOKENS)
    packets = jnp.where(row_position[:, None] == packet_rows[0], packet_size[0][None, :], 0.0)
    packets = packets + jnp.where(row_position[:, None] == packet_rows[1], packet_size[1][None, :], 0.0)
    return (-(baseline_rate[None, :] * block_multiplier * token_multiplier + packets)).astype(jnp.float32)


def attention_pair(key):
    base_key = jax.random.fold_in(key, 11)
    segments = jax.random.split(base_key, 2)
    key_draw = jnp.clip(jax.random.normal(segments[0], (SEQUENCE_TOKENS, ATT_DIM)), -4.0, 4.0)
    query_draw = jnp.clip(jax.random.normal(segments[1], (SEQUENCE_TOKENS, Q_HEADS, ATT_DIM)), -6.0, 6.0)
    return (query_draw, key_draw)


def draw_queries(key, part):
    return attention_pair(key)[0].astype(jnp.bfloat16)


def draw_key_rows(key, part):
    return attention_pair(key)[1].astype(jnp.bfloat16)


def steps_of(rng, dims, cuts, least, top_value):
    def one(axis_at, parts):
        heights = jax.random.uniform(jax.random.fold_in(jax.random.fold_in(rng, 6), axis_at), (parts,), jnp.float32, least / len(cuts), top_value / len(cuts))
        return jnp.repeat(jnp.exp(heights), dims[axis_at] // parts).reshape((-1,) + (1,) * (len(dims) - axis_at - 1))

    factor_of = one(*cuts[0])
    for cut in cuts[1:]:
        factor_of = factor_of * one(*cut)
    return factor_of


def normal_values(stream_key, extent, width, most, shards=(), held_as=jnp.bfloat16):
    array = jax.random.normal(stream_key, extent, jnp.float32) * width
    if len(shards) > 0:
        array = steps_of(stream_key, extent, shards, -0.22, 0.18) * array
    return jnp.clip(array, min=-most, max=most).astype(held_as)


def setup_inputs(seed: int = 0) -> dict:
    seeds = jax.random.split(jax.random.key(seed), 11)
    return {
        "ssd_input": normal_values(seeds[0], (SEQUENCE_TOKENS, SCAN_HEADS, HEAD_DIM), 0.5, 3.0, ((0, 16), (1, 8))),
        "log_decay": draw_log_decay(jax.random.fold_in(seeds[10], 71), 0),
        "input_map": normal_values(seeds[2], (SEQUENCE_TOKENS, GROUPS, STATE), 0.03, 0.18, ((0, 16), (1, 8)), jnp.float32),
        "output_map": normal_values(seeds[3], (SEQUENCE_TOKENS, GROUPS, STATE), 0.03, 0.18, ((0, 16), (1, 8)), jnp.float32),
        "ssd_cotangent": normal_values(seeds[4], (SEQUENCE_TOKENS, SCAN_HEADS, HEAD_DIM), 0.5, 3.0, ((0, 16), (1, 8))),
        "queries": draw_queries(jax.random.fold_in(seeds[10], 71), 0),
        "key_rows": draw_key_rows(jax.random.fold_in(seeds[10], 71), 0),
        "value_rows": normal_values(seeds[7], (SEQUENCE_TOKENS, ATT_DIM), 1.0, 6.0, ((0, 16),)),
        "attn_cotangent": normal_values(seeds[8], (SEQUENCE_TOKENS, Q_HEADS, ATT_DIM), 1.0, 6.0, ((0, 16), (1, 8))),
        "pair_order": jax.random.permutation(seeds[9], N_SEQ).astype(jnp.int32),
    }


HIGHEST = lax.Precision.HIGHEST
NEG_FILL = -1e+30

def through_bf16(values):
    return lax.optimization_barrier(values.astype(jnp.bfloat16)).astype(jnp.float32)

def block_advance(state_now, inputs):
    x_block, a_block, b_block, c_block = inputs
    cumulative = jnp.cumsum(a_block, axis=0)
    block_len = a_block.shape[0]
    causal_mask = (jnp.arange(block_len)[:, None] >= jnp.arange(block_len)[None, :])[:, :, None, None]
    decay_grid = jnp.exp(jnp.where(causal_mask, cumulative[:, None] - cumulative[None, :], NEG_FILL))
    inner_prod = jnp.einsum('tgn,sgn->tsg', c_block, b_block, precision=HIGHEST)
    weight_grid = through_bf16(inner_prod[:, :, :, None] * decay_grid)
    x_wide = x_block.astype(jnp.float32)
    local_part = jnp.einsum('tsge,sgep->tgep', weight_grid, x_wide, precision=HIGHEST)
    c_scaled = through_bf16(c_block[:, :, None, :] * jnp.exp(cumulative)[..., None])
    carried_part = jnp.einsum('tgen,genp->tgep', c_scaled, through_bf16(state_now), precision=HIGHEST)
    block_out = (local_part + carried_part).astype(jnp.bfloat16)
    tail_decay = jnp.exp(cumulative[-1][None] - cumulative)
    b_scaled = through_bf16(b_block[:, :, None, :] * tail_decay[..., None])
    fresh_state = jnp.einsum('tgen,tgep->genp', b_scaled, x_wide, precision=HIGHEST)
    return (jnp.exp(cumulative[-1])[..., None, None] * state_now + fresh_state, block_out)

def blocked(values):
    return values.reshape((values.shape[0] // BLOCK, BLOCK) + values.shape[1:])

def run_blocks(x_seq, a_seq, b_seq, c_seq, state_start):
    state_end, block_outs = lax.scan(block_advance, state_start, (blocked(x_seq), blocked(a_seq), blocked(b_seq), blocked(c_seq)))
    return (block_outs.reshape(x_seq.shape), state_end)

def group_backward(group_items):
    x_group, a_group, b_group, c_group, dy_group = group_items
    per_group = x_group.shape[1]

    def forward(x_values, a_values, b_values, c_values):
        state_zero = jnp.zeros((1, per_group, STATE, HEAD_DIM), jnp.float32)
        result, ignored = run_blocks(x_values[:, None], a_values[:, None], b_values[:, None], c_values[:, None], state_zero)
        return result[:, 0]
    primal, pullback = jax.vjp(forward, x_group, a_group, b_group, c_group)
    return pullback(dy_group)

def attention_grads(queries, key_rows, value_rows, attn_cotangent, pair_order):
    row_position = jnp.arange(SEQUENCE_TOKENS, dtype=jnp.int32)
    owner_dev = row_position // TOK_DEV
    within = row_position % TOK_DEV
    first_block = pair_order[owner_dev]
    block_id = jnp.where(within < HALF, first_block, 2 * N_SEQ - 1 - first_block)
    position = block_id * HALF + within % HALF
    keys_wide = key_rows.astype(jnp.float32)
    values_wide = value_rows.astype(jnp.float32)
    scale_factor = ATT_DIM ** (-0.5)

    def query_block(carried, block_index):
        key_grad, value_grad = carried
        start_row = (block_index * HALF).astype(jnp.int32)
        query_part = lax.dynamic_slice_in_dim(queries, start_row, HALF, 0).astype(jnp.float32)
        grad_part = lax.dynamic_slice_in_dim(attn_cotangent, start_row, HALF, 0).astype(jnp.float32)
        query_at = lax.dynamic_slice_in_dim(position, start_row, HALF, 0)
        visible = position[None, :] <= query_at[:, None]
        scores = jnp.einsum('rhd,kd->hrk', query_part, keys_wide, precision=HIGHEST) * scale_factor
        scores = jnp.where(visible[None], scores, NEG_FILL)
        row_top = lax.optimization_barrier(jnp.max(scores, axis=-1, keepdims=True))
        exp_scores = jnp.exp(scores - row_top)
        probs = exp_scores / lax.optimization_barrier(jnp.sum(exp_scores, axis=-1, keepdims=True))
        prob_b = through_bf16(probs)
        attn_out = through_bf16(jnp.einsum('hrk,kd->rhd', prob_b, values_wide, precision=HIGHEST))
        row_delta = lax.optimization_barrier(jnp.sum(grad_part * attn_out, axis=-1))
        prob_grad = jnp.einsum('rhd,kd->hrk', grad_part, values_wide, precision=HIGHEST)
        dscore = through_bf16(probs * (prob_grad - row_delta.T[:, :, None]))
        query_grad = (jnp.einsum('hrk,kd->rhd', dscore, keys_wide, precision=HIGHEST) * scale_factor).astype(jnp.bfloat16)
        key_grad = key_grad + jnp.einsum('hrk,rhd->kd', dscore, query_part, precision=HIGHEST) * scale_factor
        value_grad = value_grad + jnp.einsum('hrk,rhd->kd', prob_b, grad_part, precision=HIGHEST)
        return ((key_grad, value_grad), query_grad)
    zero_grad = jnp.zeros((SEQUENCE_TOKENS, ATT_DIM), jnp.float32)
    sums, query_blocks = lax.scan(query_block, (zero_grad, zero_grad), jnp.arange(SEQUENCE_TOKENS // HALF, dtype=jnp.int32))
    grad_queries = query_blocks.reshape(SEQUENCE_TOKENS, Q_HEADS, ATT_DIM)
    return (grad_queries, sums[0].astype(jnp.bfloat16), sums[1].astype(jnp.bfloat16))

def reference(ssd_input, log_decay, input_map, output_map, ssd_cotangent, queries, key_rows, value_rows, attn_cotangent, pair_order):
    per_group = SCAN_HEADS // GROUPS
    x_groups = ssd_input.reshape(SEQUENCE_TOKENS, GROUPS, per_group, HEAD_DIM).transpose(1, 0, 2, 3)
    a_groups = log_decay.reshape(SEQUENCE_TOKENS, GROUPS, per_group).transpose(1, 0, 2)
    b_groups = input_map.transpose(1, 0, 2)
    c_groups = output_map.transpose(1, 0, 2)
    dy_groups = ssd_cotangent.reshape(SEQUENCE_TOKENS, GROUPS, per_group, HEAD_DIM).transpose(1, 0, 2, 3)
    gradients = lax.map(group_backward, (x_groups, a_groups, b_groups, c_groups, dy_groups))
    grad_input = gradients[0].transpose(1, 0, 2, 3).reshape(SEQUENCE_TOKENS, SCAN_HEADS, HEAD_DIM)
    grad_decay = gradients[1].transpose(1, 0, 2).reshape(SEQUENCE_TOKENS, SCAN_HEADS)
    grad_input_map = gradients[2].transpose(1, 0, 2)
    grad_output_map = gradients[3].transpose(1, 0, 2)
    grad_queries, grad_keys, grad_values = attention_grads(queries, key_rows, value_rows, attn_cotangent, pair_order)
    return (grad_input, grad_decay, grad_input_map, grad_output_map, grad_queries, grad_keys, grad_values)
```

```python
import functools

import jax
import jax.numpy as jnp
from jax import lax
from jax.experimental import pallas as pl
from jax.experimental.pallas import tpu as pltpu
from jax.sharding import PartitionSpec as P

BLOCK = 128
BF = jnp.bfloat16
F32 = jnp.float32
HIGHEST = lax.Precision.HIGHEST
NEG = -1e30
LOG2E = 1.4426950408889634
STATE_ROWS = 256
TOTAL_ROWS = 16


def dot(a, b, ca, cb, precision=None):
    return lax.dot_general(
        a, b, (((ca,), (cb,)), ((), ())), precision=precision, preferred_element_type=F32
    )


def iota(shape, dim):
    return lax.broadcasted_iota(jnp.int32, shape, dim)


def pieces(v, count):
    out = []
    for _ in range(count):
        p = v.astype(BF)
        out.append(p)
        v = v - p.astype(F32)
    return out


def ssd_send_kernel(
    info, x_ref, y_ref, at_ref, b_ref, c_ref, k_ref, v_ref,
    send_ref, xh_ref, yh_ref, cum_ref, xs, ys, st, pu, run,
):
    k = pl.program_id(0)
    heads = x_ref.shape[1]

    @pl.when(k == 0)
    def _():
        st[...] = jnp.zeros_like(st)
        pu[...] = jnp.zeros_like(pu)
        run[...] = jnp.zeros_like(run)

    upto = (iota((BLOCK, BLOCK), 0) <= iota((BLOCK, BLOCK), 1)).astype(F32)
    cum = dot(at_ref[...], upto, 1, 0, HIGHEST)
    cum_ref[...] = cum
    total = cum[:, BLOCK - 1 :]
    grow = jnp.exp(cum)
    tail = jnp.exp(total - cum)
    keep = jnp.exp(total)
    before = run[:, :1]
    early = jnp.exp(before)
    run[...] = jnp.broadcast_to(before + total, run.shape)
    bt = b_ref[...].T
    ct = c_ref[...].T
    xs[...] = x_ref[...].astype(F32).reshape(xs.shape)
    ys[...] = y_ref[...].astype(F32).reshape(ys.shape)
    for h in range(heads):
        x = xs[pl.ds(h, BLOCK, stride=heads), :].astype(BF)
        y = ys[pl.ds(h, BLOCK, stride=heads), :].astype(BF)
        xh_ref[h] = x
        yh_ref[h] = y
        bs = (bt * tail[h : h + 1, :]).astype(BF)
        cs = (ct * grow[h : h + 1, :]).astype(BF)
        st[h] = keep[h : h + 1, :] * st[h] + dot(bs, x, 1, 0)
        pu[h] = pu[h] + early[h : h + 1, :] * dot(cs, y, 1, 0).astype(BF).astype(F32)

    @pl.when(k == pl.num_programs(0) - 1)
    def _():
        at = pl.multiple_of(info[1] * 32, 32)
        half = k_ref.shape[0] // 2
        subs = [r[pl.ds(at + o, 32), :] for r in (k_ref, v_ref) for o in (0, half)]
        three = pieces(run[...], 3)
        for h in range(heads):
            send_ref[h, 0:128, :] = st[h].astype(BF)
            send_ref[h, 128:256, :] = pu[h].astype(BF)
            for i, s in enumerate(subs):
                send_ref[h, 256 + 32 * i : 288 + 32 * i, :] = s
            rows = iota((TOTAL_ROWS, 128), 0)
            t = jnp.zeros((TOTAL_ROWS, 128), F32)
            for i, p in enumerate(three):
                t = jnp.where(rows == i, p[h : h + 1, :].astype(F32), t)
            send_ref[h, 384:400, :] = t.astype(BF)


def ssd_send(info, x, y, at, b, c, keys, values):
    tok, heads, width = x.shape
    nb = tok // BLOCK
    blk = pl.BlockSpec((BLOCK, heads, width), lambda k, i: (k, 0, 0))
    mat = pl.BlockSpec((BLOCK, 128), lambda k, i: (k, 0))
    row = pl.BlockSpec((heads, BLOCK), lambda k, i: (0, k))
    hm = pl.BlockSpec((heads, BLOCK, width), lambda k, i: (0, k, 0))
    whole = pl.BlockSpec((tok, 128), lambda k, i: (0, 0))
    rows = STATE_ROWS + 128 + TOTAL_ROWS
    return pl.pallas_call(
        ssd_send_kernel,
        grid_spec=pltpu.PrefetchScalarGridSpec(
            num_scalar_prefetch=1,
            grid=(nb,),
            in_specs=[blk, blk, row, mat, mat, whole, whole],
            out_specs=[pl.BlockSpec((heads, rows, 128), lambda k, i: (0, 0, 0)), hm, hm, row],
            scratch_shapes=[
                pltpu.VMEM((BLOCK * heads, width), F32),
                pltpu.VMEM((BLOCK * heads, width), F32),
                pltpu.VMEM((heads, 128, 128), F32),
                pltpu.VMEM((heads, 128, 128), F32),
                pltpu.VMEM((heads, 128), F32),
            ],
        ),
        out_shape=[
            jax.ShapeDtypeStruct((heads, rows, 128), BF),
            jax.ShapeDtypeStruct((heads, tok, width), BF),
            jax.ShapeDtypeStruct((heads, tok, width), BF),
            jax.ShapeDtypeStruct((heads, tok), F32),
        ],
        compiler_params=pltpu.CompilerParams(vmem_limit_bytes=48 << 20),
        name="ssd_send",
    )(info, x, y, at, b, c, keys, values)


def sort_keys(info, recv, ks, vs):
    for b in range(32):
        src = info[2 + (b if b < 16 else 31 - b)]
        o = 0 if b < 16 else 32
        ks[32 * b : 32 * b + 32, :] = recv[src, 256 + o : 288 + o, :]
        vs[32 * b : 32 * b + 32, :] = recv[src, 320 + o : 352 + o, :]


def item_at(info, i):
    first = info[0]
    n0 = (first + 4) // 4
    late = (i >= n0).astype(jnp.int32)
    g = i - late * n0
    block = jnp.where(late == 1, 31 - first, first)
    kr = iota((128, 256), 0)
    key_at = (g * 4 + kr // 32) * 256 + info[1] * 32 + kr % 32
    bias = jnp.where(key_at <= block * 256 + iota((128, 256), 1), 0.0, NEG)
    return pl.multiple_of(g * 128, 128), pl.multiple_of(late * 256, 256), bias


def attn_stat_kernel(info, recv, qd, stat, ks, vs):
    heads = qd.shape[0]
    scale = LOG2E * 128**-0.5
    sort_keys(info, recv, ks, vs)
    stat[0:heads, :] = jnp.full((heads, 512), NEG, F32)
    stat[heads:, :] = jnp.zeros((2 * heads, 512), F32)

    def item(i, carry):
        kat, rat, bias = item_at(info, i)
        kg = ks[pl.ds(kat, 128), :]
        vg = vs[pl.ds(kat, 128), :]
        for h in range(heads):
            s = dot(kg, qd[h, 0, pl.ds(rat, 256), :], 1, 1) * scale + bias
            dp = dot(vg, qd[h, 1, pl.ds(rat, 256), :], 1, 1)
            old = stat[h : h + 1, pl.ds(rat, 256)]
            top = jnp.maximum(old, jnp.max(s, axis=0, keepdims=True))
            p = jnp.exp2(s - top)
            fix = jnp.exp2(old - top)
            l = heads + h
            d = 2 * heads + h
            stat[h : h + 1, pl.ds(rat, 256)] = top
            stat[l : l + 1, pl.ds(rat, 256)] = fix * stat[
                l : l + 1, pl.ds(rat, 256)
            ] + jnp.sum(p, axis=0, keepdims=True)
            stat[d : d + 1, pl.ds(rat, 256)] = fix * stat[
                d : d + 1, pl.ds(rat, 256)
            ] + jnp.sum(p * dp, axis=0, keepdims=True)
        return carry

    lax.fori_loop(0, 9, item, 0)


VM = pl.BlockSpec(memory_space=pltpu.VMEM)
SM = pl.BlockSpec(memory_space=pltpu.SMEM)


def attn_stat(info, recv, qd):
    heads = qd.shape[0]
    return pl.pallas_call(
        attn_stat_kernel,
        in_specs=[SM, VM, VM],
        out_specs=VM,
        out_shape=jax.ShapeDtypeStruct((3 * heads, 512), F32),
        scratch_shapes=[pltpu.VMEM((1024, 128), BF), pltpu.VMEM((1024, 128), BF)],
        compiler_params=pltpu.CompilerParams(vmem_limit_bytes=48 << 20),
        name="attn_stat",
    )(info, recv, qd)


def attn_grad_kernel(info, recv, qd, stats, send, dqt, ks, vs, dk, dv, lse, delta, dqs):
    heads = qd.shape[0]
    scale = 128**-0.5
    sort_keys(info, recv, ks, vs)
    top = stats[0, 0:heads, :]
    for j in range(1, stats.shape[0]):
        top = jnp.maximum(top, stats[j, 0:heads, :])
    total = jnp.zeros_like(top)
    dsum = jnp.zeros_like(top)
    for j in range(stats.shape[0]):
        f = jnp.exp2(stats[j, 0:heads, :] - top)
        total = total + f * stats[j, heads : 2 * heads, :]
        dsum = dsum + f * stats[j, 2 * heads :, :]
    lse[...] = top + jnp.log2(total)
    delta[...] = dsum / total
    dk[...] = jnp.zeros_like(dk)
    dv[...] = jnp.zeros_like(dv)
    dqs[...] = jnp.zeros_like(dqs)

    def item(i, carry):
        kat, rat, bias = item_at(info, i)
        kg = ks[pl.ds(kat, 128), :]
        vg = vs[pl.ds(kat, 128), :]
        kt = kg.astype(F32).T.astype(BF)
        dkg = dk[pl.ds(kat, 128), :]
        dvg = dv[pl.ds(kat, 128), :]
        for h in range(heads):
            q = qd[h, 0, pl.ds(rat, 256), :]
            do = qd[h, 1, pl.ds(rat, 256), :]
            s = dot(kg, q, 1, 1) * (scale * LOG2E) + bias
            dp = dot(vg, do, 1, 1)
            p = jnp.exp2(s - lse[h : h + 1, pl.ds(rat, 256)])
            ds = (p * (dp - delta[h : h + 1, pl.ds(rat, 256)])).astype(BF)
            dvg = dvg + dot(p.astype(BF), do, 1, 0)
            dkg = dkg + dot(ds, q, 1, 0)
            dqs[h, :, pl.ds(rat, 256)] += dot(kt, ds, 1, 0)
        dk[pl.ds(kat, 128), :] = dkg
        dv[pl.ds(kat, 128), :] = dvg
        return carry

    lax.fori_loop(0, 9, item, 0)
    dqt[...] = (dqs[...] * scale).astype(BF)
    for e in range(16):
        b = info[18 + e]
        for j, (r, f) in enumerate(((dk, scale), (dv, 1.0))):
            lo = r[pl.ds(pl.multiple_of(b * 32, 32), 32), :]
            hi = r[pl.ds(pl.multiple_of((31 - b) * 32, 32), 32), :]
            send[e, 256 + 64 * j : 288 + 64 * j, :] = (lo * f).astype(BF)
            send[e, 288 + 64 * j : 320 + 64 * j, :] = (hi * f).astype(BF)
    n = recv.shape[0]
    state = jnp.zeros((128, 128), F32)
    for e in range(n):
        send[e, 0:128, :] = state.astype(BF)
        if e < n - 1:
            t = recv[e, 384:400, :].astype(F32)
            keep = jnp.exp(t[0:1] + t[1:2] + t[2:3])
            state = keep * state + recv[e, 0:128, :].astype(F32)
    pull = jnp.zeros((128, 128), F32)
    for e in reversed(range(n)):
        send[e, 128:256, :] = pull.astype(BF)
        if e > 0:
            t = recv[e, 384:400, :].astype(F32)
            keep = jnp.exp(t[0:1] + t[1:2] + t[2:3])
            pull = keep * pull + recv[e, 128:256, :].astype(F32)


def attn_grad(info, recv, qd, stats):
    heads = qd.shape[0]
    n = recv.shape[0]
    return pl.pallas_call(
        attn_grad_kernel,
        in_specs=[SM, VM, VM, VM],
        out_specs=[VM, VM],
        out_shape=[
            jax.ShapeDtypeStruct((n, 384, 128), BF),
            jax.ShapeDtypeStruct((heads, 128, 512), BF),
        ],
        scratch_shapes=[
            pltpu.VMEM((1024, 128), BF),
            pltpu.VMEM((1024, 128), BF),
            pltpu.VMEM((1024, 128), F32),
            pltpu.VMEM((1024, 128), F32),
            pltpu.VMEM((heads, 512), F32),
            pltpu.VMEM((heads, 512), F32),
            pltpu.VMEM((heads, 128, 512), F32),
        ],
        compiler_params=pltpu.CompilerParams(vmem_limit_bytes=48 << 20),
        name="attn_grad",
    )(info, recv, qd, stats)


def ssd_grad_kernel(
    xh, yh, states, cum, b_ref, c_ref,
    dx_ref, da_ref, db_ref, dc_ref,
    g_s, dg_s, dct, dbt, bt_s, ct_s, colp, dcol, drow, dxs,
):
    h = pl.program_id(0)
    heads = pl.num_programs(0)
    nb = xh.shape[1] // BLOCK
    rows = iota((BLOCK, BLOCK), 0)
    lanes = iota((BLOCK, BLOCK), 1)

    @pl.when(h == 0)
    def _():
        dg_s[...] = jnp.zeros_like(dg_s)
        dct[...] = jnp.zeros_like(dct)
        dbt[...] = jnp.zeros_like(dbt)
        dcol[...] = jnp.zeros_like(dcol)
        drow[...] = jnp.zeros_like(drow)
        for k in range(nb):
            sl = slice(k * BLOCK, (k + 1) * BLOCK)
            b = b_ref[sl, :]
            c = c_ref[sl, :]
            g_s[k] = jnp.where(rows <= lanes, dot(b, c, 1, 1, HIGHEST), 0.0)
            bt_s[k] = b.T
            ct_s[k] = c.T
            cm = cum[:, sl]
            tl = jnp.exp(cm[:, BLOCK - 1 :] - cm)
            parts = [p.astype(F32) for p in pieces(cm, 3) + pieces(tl, 2)]
            parts.append(jnp.zeros((BLOCK - 5 * heads_of(cum), BLOCK), F32))
            colp[k] = jnp.concatenate(parts, axis=0).T.astype(BF)

    nh = heads_of(cum)
    pr = iota((BLOCK, 2 * BLOCK), 0)
    pc = iota((BLOCK, 2 * BLOCK), 1)
    mine = (pr % nh) == h
    left = jnp.logical_and(pr < 3 * nh, pc < BLOCK)
    right = jnp.logical_and(jnp.logical_and(pr >= 3 * nh, pr < 5 * nh), pc >= BLOCK)
    pick = jnp.where(jnp.logical_and(mine, jnp.logical_or(left, right)), 1.0, 0.0).astype(BF)

    crow = cum[pl.ds(h, 1), :]
    x = [xh[0, k * BLOCK : (k + 1) * BLOCK, :] for k in range(nb)]
    y = [yh[0, k * BLOCK : (k + 1) * BLOCK, :] for k in range(nb)]
    c = [crow[:, k * BLOCK : (k + 1) * BLOCK] for k in range(nb)]
    total = [v[:, BLOCK - 1 :] for v in c]
    keep = [jnp.exp(t) for t in total]
    tail = [jnp.exp(t - v) for t, v in zip(total, c)]
    grow = [jnp.exp(v) for v in c]
    state = [states[0, 0:128, :].astype(F32)]
    for k in range(nb - 1):
        bs = (bt_s[k] * tail[k]).astype(BF)
        state.append(keep[k] * state[k] + dot(bs, x[k], 1, 0))
    pull = states[0, 128:256, :].astype(F32)
    for k in reversed(range(nb)):
        cols = dot(colp[k], pick, 1, 0)
        decay = jnp.exp(jnp.minimum(c[k] - cols[:, :BLOCK], 0.0))
        w = g_s[k] * decay
        dw = dot(x[k], y[k], 1, 1)
        t = dw * decay
        dg_s[k] += t
        z = t * g_s[k]
        sb = state[k].astype(BF)
        pb = pull.astype(BF)
        bs = (b_ref[k * BLOCK : (k + 1) * BLOCK, :] * cols[:, BLOCK:]).astype(BF)
        dx = dot(w.astype(BF), y[k], 1, 0) + dot(bs, pb, 1, 0)
        dxs[pl.ds(k * BLOCK * heads + h, BLOCK, stride=nh), :] = dx
        dcs = dot(sb, y[k], 1, 1) * grow[k]
        dct[k] += dcs
        q = dcs * ct_s[k]
        dbs = dot(pb, x[k], 1, 1) * tail[k]
        dbt[k] += dbs
        v = dbs * bt_s[k]
        vs = jnp.sum(v, axis=0, keepdims=True)
        line = jnp.sum(z + q, axis=0, keepdims=True) - vs
        cross = keep[k] * jnp.sum(state[k] * pull, axis=0, keepdims=True)
        last = jnp.sum(vs + cross, axis=1, keepdims=True)
        line = jnp.where(iota((1, BLOCK), 1) == BLOCK - 1, line + last, line)
        at = slice(k * BLOCK, (k + 1) * BLOCK)
        drow[:, at] = jnp.where(iota((nh, BLOCK), 0) == h, line, drow[:, at])
        zc = jnp.sum(z, axis=1, keepdims=True)
        dcol[k] = jnp.where(lanes == h, zc, dcol[k])
        if k > 0:
            cs = (ct_s[k] * grow[k]).astype(BF)
            pull = keep[k] * pull + dot(cs, y[k], 1, 0).astype(BF).astype(F32)

    @pl.when(h == heads - 1)
    def _():
        late = (rows <= lanes).astype(F32)
        for k in range(nb):
            sl = slice(k * BLOCK, (k + 1) * BLOCK)
            dg = jnp.where(rows <= lanes, dg_s[k], 0.0)
            db_ref[sl, :] = dbt[k].T + dot(dg, c_ref[sl, :], 1, 0, HIGHEST)
            dc_ref[sl, :] = dct[k].T + dot(dg.T, b_ref[sl, :], 1, 0, HIGHEST)
            line = jnp.concatenate(
                [drow[:, sl], jnp.zeros((BLOCK - nh, BLOCK), F32)], axis=0
            ).T - dcol[k]
            da_ref[sl, :] = dot(late, line, 1, 0, HIGHEST)[:, :nh]
            dx_ref[sl] = (
                dxs[k * BLOCK * nh : (k + 1) * BLOCK * nh, :]
                .reshape(BLOCK, nh, 128)
                .astype(BF)
            )


def heads_of(cum):
    return cum.shape[0]


def ssd_grad(xh, yh, states, cum, b, c):
    heads, tok, width = xh.shape
    nb = tok // BLOCK
    rows = states.shape[1]
    per = pl.BlockSpec((1, tok, width), lambda h: (h, 0, 0))
    whole = lambda *s: pl.BlockSpec(s, lambda h: (0,) * len(s))
    sq = pltpu.VMEM((nb, 128, 128), F32)
    return pl.pallas_call(
        ssd_grad_kernel,
        grid=(heads,),
        in_specs=[
            per,
            per,
            pl.BlockSpec((1, rows, 128), lambda h: (h, 0, 0)),
            whole(heads, tok),
            whole(tok, 128),
            whole(tok, 128),
        ],
        out_specs=[
            whole(tok, heads, width),
            whole(tok, heads),
            whole(tok, 128),
            whole(tok, 128),
        ],
        out_shape=[
            jax.ShapeDtypeStruct((tok, heads, width), BF),
            jax.ShapeDtypeStruct((tok, heads), F32),
            jax.ShapeDtypeStruct((tok, 128), F32),
            jax.ShapeDtypeStruct((tok, 128), F32),
        ],
        scratch_shapes=[
            sq, sq, sq, sq, sq, sq,
            pltpu.VMEM((nb, 128, 128), BF),
            sq,
            pltpu.VMEM((heads, tok), F32),
            pltpu.VMEM((tok * heads, width), F32),
        ],
        compiler_params=pltpu.CompilerParams(vmem_limit_bytes=48 << 20),
        name="ssd_grad",
    )(xh, yh, states, cum, b, c)


def per_device(
    ssd_input, log_decay, input_map, output_map, ssd_cotangent,
    queries, key_rows, value_rows, attn_cotangent, pair_order,
):
    tok, heads, width = ssd_input.shape
    b = input_map.reshape(tok, 128)
    c = output_map.reshape(tok, 128)
    own = lax.axis_index("seq")
    place = lax.axis_index("head")
    inverse = jnp.sum(
        jnp.where(pair_order[None, :] == jnp.arange(16)[:, None], jnp.arange(16)[None, :], 0),
        axis=1,
    )
    info = jnp.concatenate(
        [
            jnp.stack([pair_order[own], place.astype(jnp.int32)]),
            inverse.astype(jnp.int32),
            pair_order,
        ]
    )
    qd = lax.all_gather(
        jnp.stack([queries.reshape(tok, 128), attn_cotangent.reshape(tok, 128)]), "head"
    )
    send, xh, yh, cum = ssd_send(
        info, ssd_input, ssd_cotangent, log_decay.T, b, c, key_rows, value_rows
    )
    recv = lax.all_to_all(send, "seq", 0, 0)
    stats = lax.all_gather(attn_stat(info, recv, qd), "head")
    back, dqt = attn_grad(info, recv, qd, stats)
    dq = lax.psum_scatter(dqt, "head", scatter_dimension=0)
    states = lax.all_to_all(back, "seq", 0, 0)
    dkv = jnp.sum(states[:, 256:, :].astype(F32), axis=0).astype(BF)
    dkv = lax.all_gather(dkv, "head").reshape(8, 2, 2, 32, 128).transpose(1, 2, 0, 3, 4)
    dx, da, db, dc = ssd_grad(xh, yh, states, cum, b, c)
    return (
        dx,
        da,
        db.reshape(tok, 1, 128),
        dc.reshape(tok, 1, 128),
        dq.T.reshape(tok, 1, 128),
        dkv[0].reshape(tok, 128),
        dkv[1].reshape(tok, 128),
    )


def solution(mesh):
    tok = P("seq", "head", None)
    return jax.shard_map(
        per_device,
        mesh=mesh,
        in_specs=(
            tok, P("seq", "head"), tok, tok, tok, tok,
            P("seq", None), P("seq", None), tok, P(),
        ),
        out_specs=(tok, P("seq", "head"), tok, tok, tok, P("seq", None), P("seq", None)),
        check_vma=False,
    )
```

```python
import functools

import jax
import jax.numpy as jnp
from jax import lax
from jax.experimental import pallas as pl
from jax.experimental.pallas import tpu as pltpu
from jax.sharding import PartitionSpec as P

BLOCK = 128
BF = jnp.bfloat16
F32 = jnp.float32
HIGHEST = lax.Precision.HIGHEST
NEG = -1e30
LOG2E = 1.4426950408889634
STATE_ROWS = 256
TOTAL_ROWS = 16


def dot(a, b, ca, cb, precision=None):
    return lax.dot_general(
        a, b, (((ca,), (cb,)), ((), ())), precision=precision, preferred_element_type=F32
    )


def iota(shape, dim):
    return lax.broadcasted_iota(jnp.int32, shape, dim)


def pieces(v, count):
    out = []
    for _ in range(count):
        p = v.astype(BF)
        out.append(p)
        v = v - p.astype(F32)
    return out


def ssd_send_kernel(
    x_ref, y_ref, at_ref, b_ref, c_ref, k_ref, v_ref, q_ref, do_ref,
    send_ref, xh_ref, yh_ref, cum_ref, qd_ref, xs, ys, st, pu, run,
):
    k = pl.program_id(0)
    heads = x_ref.shape[1]

    @pl.when(k == 0)
    def _():
        st[...] = jnp.zeros_like(st)
        pu[...] = jnp.zeros_like(pu)
        run[...] = jnp.zeros_like(run)

    upto = (iota((BLOCK, BLOCK), 0) <= iota((BLOCK, BLOCK), 1)).astype(F32)
    cum = dot(at_ref[...], upto, 1, 0, HIGHEST)
    cum_ref[...] = cum
    total = cum[:, BLOCK - 1 :]
    grow = jnp.exp(cum)
    tail = jnp.exp(total - cum)
    keep = jnp.exp(total)
    before = run[:, :1]
    early = jnp.exp(before)
    run[...] = jnp.broadcast_to(before + total, run.shape)
    bt = b_ref[...].T
    ct = c_ref[...].T
    xs[...] = x_ref[...].astype(F32).reshape(xs.shape)
    ys[...] = y_ref[...].astype(F32).reshape(ys.shape)
    for h in range(heads):
        x = xs[pl.ds(h, BLOCK, stride=heads), :].astype(BF)
        y = ys[pl.ds(h, BLOCK, stride=heads), :].astype(BF)
        xh_ref[h] = x
        yh_ref[h] = y
        bs = (bt * tail[h : h + 1, :]).astype(BF)
        cs = (ct * grow[h : h + 1, :]).astype(BF)
        st[h] = keep[h : h + 1, :] * st[h] + dot(bs, x, 1, 0)
        pu[h] = pu[h] + early[h : h + 1, :] * dot(cs, y, 1, 0).astype(BF).astype(F32)

    @pl.when(k == pl.num_programs(0) - 1)
    def _():
        qd_ref[0] = q_ref[...]
        qd_ref[1] = do_ref[...]
        at = pl.multiple_of(lax.axis_index("head") * 32, 32)
        half = k_ref.shape[0] // 2
        subs = [r[pl.ds(at + o, 32), :] for r in (k_ref, v_ref) for o in (0, half)]
        three = pieces(run[...], 3)
        for h in range(heads):
            send_ref[h, 0:128, :] = st[h].astype(BF)
            send_ref[h, 128:256, :] = pu[h].astype(BF)
            for i, s in enumerate(subs):
                send_ref[h, 256 + 32 * i : 288 + 32 * i, :] = s
            rows = iota((TOTAL_ROWS, 128), 0)
            t = jnp.zeros((TOTAL_ROWS, 128), F32)
            for i, p in enumerate(three):
                t = jnp.where(rows == i, p[h : h + 1, :].astype(F32), t)
            send_ref[h, 384:400, :] = t.astype(BF)


def ssd_send(x, y, at, b, c, keys, values, q, do):
    tok, heads, width = x.shape
    nb = tok // BLOCK
    blk = pl.BlockSpec((BLOCK, heads, width), lambda k: (k, 0, 0))
    mat = pl.BlockSpec((BLOCK, 128), lambda k: (k, 0))
    row = pl.BlockSpec((heads, BLOCK), lambda k: (0, k))
    hm = pl.BlockSpec((heads, BLOCK, width), lambda k: (0, k, 0))
    whole = pl.BlockSpec((tok, 128), lambda k: (0, 0))
    rows = STATE_ROWS + 128 + TOTAL_ROWS
    return pl.pallas_call(
        ssd_send_kernel,
        grid_spec=pltpu.PrefetchScalarGridSpec(
            num_scalar_prefetch=0,
            grid=(nb,),
            in_specs=[blk, blk, row, mat, mat, whole, whole, whole, whole],
            out_specs=[
                pl.BlockSpec((heads, rows, 128), lambda k: (0, 0, 0)),
                hm,
                hm,
                row,
                pl.BlockSpec((2, tok, 128), lambda k: (0, 0, 0)),
            ],
            scratch_shapes=[
                pltpu.VMEM((BLOCK * heads, width), F32),
                pltpu.VMEM((BLOCK * heads, width), F32),
                pltpu.VMEM((heads, 128, 128), F32),
                pltpu.VMEM((heads, 128, 128), F32),
                pltpu.VMEM((heads, 128), F32),
            ],
        ),
        out_shape=[
            jax.ShapeDtypeStruct((heads, rows, 128), BF),
            jax.ShapeDtypeStruct((heads, tok, width), BF),
            jax.ShapeDtypeStruct((heads, tok, width), BF),
            jax.ShapeDtypeStruct((heads, tok), F32),
            jax.ShapeDtypeStruct((2, tok, 128), BF),
        ],
        compiler_params=pltpu.CompilerParams(vmem_limit_bytes=60 << 20),
        name="ssd_send",
    )(x, y, at, b, c, keys, values, q, do)


def sort_keys(order, inverse, recv, ks, vs):
    for e in range(16):
        inverse[order[e]] = e
    for b in range(32):
        src = inverse[b if b < 16 else 31 - b]
        o = 0 if b < 16 else 32
        ks[32 * b : 32 * b + 32, :] = recv[src, 256 + o : 288 + o, :]
        vs[32 * b : 32 * b + 32, :] = recv[src, 320 + o : 352 + o, :]


def item_at(order, i):
    first = order[lax.axis_index("seq")]
    n0 = (first + 4) // 4
    late = (i >= n0).astype(jnp.int32)
    g = i - late * n0
    block = jnp.where(late == 1, 31 - first, first)
    kr = iota((128, 256), 0)
    key_at = (g * 4 + kr // 32) * 256 + lax.axis_index("head") * 32 + kr % 32
    bias = jnp.where(key_at <= block * 256 + iota((128, 256), 1), 0.0, NEG)
    return pl.multiple_of(g * 128, 128), pl.multiple_of(late * 256, 256), bias


def attn_stat_kernel(order, recv, qd, stat, ks, vs, inverse):
    heads = qd.shape[0]
    scale = LOG2E * 128**-0.5
    sort_keys(order, inverse, recv, ks, vs)
    stat[0:heads, :] = jnp.full((heads, 512), NEG, F32)
    stat[heads:, :] = jnp.zeros((2 * heads, 512), F32)

    def item(i, carry):
        kat, rat, bias = item_at(order, i)
        kg = ks[pl.ds(kat, 128), :]
        vg = vs[pl.ds(kat, 128), :]
        for h in range(heads):
            s = dot(kg, qd[h, 0, pl.ds(rat, 256), :], 1, 1) * scale + bias
            dp = dot(vg, qd[h, 1, pl.ds(rat, 256), :], 1, 1)
            old = stat[h : h + 1, pl.ds(rat, 256)]
            top = jnp.maximum(old, jnp.max(s, axis=0, keepdims=True))
            p = jnp.exp2(s - top)
            fix = jnp.exp2(old - top)
            l = heads + h
            d = 2 * heads + h
            stat[h : h + 1, pl.ds(rat, 256)] = top
            stat[l : l + 1, pl.ds(rat, 256)] = fix * stat[
                l : l + 1, pl.ds(rat, 256)
            ] + jnp.sum(p, axis=0, keepdims=True)
            stat[d : d + 1, pl.ds(rat, 256)] = fix * stat[
                d : d + 1, pl.ds(rat, 256)
            ] + jnp.sum(p * dp, axis=0, keepdims=True)
        return carry

    lax.fori_loop(0, 9, item, 0)


VM = pl.BlockSpec(memory_space=pltpu.VMEM)
SM = pl.BlockSpec(memory_space=pltpu.SMEM)
HB = pl.BlockSpec(memory_space=pltpu.HBM)


def attn_stat(order, recv, qd):
    heads = qd.shape[0]
    return pl.pallas_call(
        attn_stat_kernel,
        in_specs=[SM, VM, VM],
        out_specs=VM,
        out_shape=jax.ShapeDtypeStruct((3 * heads, 512), F32),
        scratch_shapes=[
            pltpu.VMEM((1024, 128), BF),
            pltpu.VMEM((1024, 128), BF),
            pltpu.SMEM((16,), jnp.int32),
        ],
        compiler_params=pltpu.CompilerParams(vmem_limit_bytes=20 << 20),
        name="attn_stat",
    )(order, recv, qd)


def attn_grad_kernel(
    order, recv, qd, stats, send, dqt, ks, vs, dk, dv, lse, delta, dqs, inverse, dqo, buf, sem
):
    heads = qd.shape[0]
    scale = 128**-0.5
    sort_keys(order, inverse, recv, ks, vs)
    n = recv.shape[0]
    state = jnp.zeros((128, 128), F32)
    for e in range(n):
        buf[e, 0:128, :] = state.astype(BF)
        if e < n - 1:
            t = recv[e, 384:400, :].astype(F32)
            keep = jnp.exp(t[0:1] + t[1:2] + t[2:3])
            state = keep * state + recv[e, 0:128, :].astype(F32)
    moves = [pltpu.make_async_copy(buf.at[:, 0:128], send.at[:, 0:128], sem.at[0])]
    moves[0].start()
    pull = jnp.zeros((128, 128), F32)
    for e in reversed(range(n)):
        buf[e, 128:256, :] = pull.astype(BF)
        if e > 0:
            t = recv[e, 384:400, :].astype(F32)
            keep = jnp.exp(t[0:1] + t[1:2] + t[2:3])
            pull = keep * pull + recv[e, 128:256, :].astype(F32)
    moves.append(pltpu.make_async_copy(buf.at[:, 128:256], send.at[:, 128:256], sem.at[1]))
    moves[1].start()
    top = stats[0, 0:heads, :]
    for j in range(1, stats.shape[0]):
        top = jnp.maximum(top, stats[j, 0:heads, :])
    total = jnp.zeros_like(top)
    dsum = jnp.zeros_like(top)
    for j in range(stats.shape[0]):
        f = jnp.exp2(stats[j, 0:heads, :] - top)
        total = total + f * stats[j, heads : 2 * heads, :]
        dsum = dsum + f * stats[j, 2 * heads :, :]
    lse[...] = top + jnp.log2(total)
    delta[...] = dsum / total
    dk[...] = jnp.zeros_like(dk)
    dv[...] = jnp.zeros_like(dv)
    dqs[...] = jnp.zeros_like(dqs)

    def item(i, carry):
        kat, rat, bias = item_at(order, i)
        kg = ks[pl.ds(kat, 128), :]
        vg = vs[pl.ds(kat, 128), :]
        kt = kg.astype(F32).T.astype(BF)
        dkg = dk[pl.ds(kat, 128), :]
        dvg = dv[pl.ds(kat, 128), :]
        for h in range(heads):
            q = qd[h, 0, pl.ds(rat, 256), :]
            do = qd[h, 1, pl.ds(rat, 256), :]
            s = dot(kg, q, 1, 1) * (scale * LOG2E) + bias
            dp = dot(vg, do, 1, 1)
            p = jnp.exp2(s - lse[h : h + 1, pl.ds(rat, 256)])
            ds = (p * (dp - delta[h : h + 1, pl.ds(rat, 256)])).astype(BF)
            dvg = dvg + dot(p.astype(BF), do, 1, 0)
            dkg = dkg + dot(ds, q, 1, 0)
            dqs[h, :, pl.ds(rat, 256)] += dot(kt, ds, 1, 0)
        dk[pl.ds(kat, 128), :] = dkg
        dv[pl.ds(kat, 128), :] = dvg
        return carry

    lax.fori_loop(0, 9, item, 0)
    dqo[...] = (dqs[...] * scale).astype(BF)
    moves.append(pltpu.make_async_copy(dqo, dqt, sem.at[2]))
    moves[2].start()
    for e in range(16):
        b = order[e]
        for j, (r, f) in enumerate(((dk, scale), (dv, 1.0))):
            lo = r[pl.ds(pl.multiple_of(b * 32, 32), 32), :]
            hi = r[pl.ds(pl.multiple_of((31 - b) * 32, 32), 32), :]
            buf[e, 256 + 64 * j : 288 + 64 * j, :] = (lo * f).astype(BF)
            buf[e, 288 + 64 * j : 320 + 64 * j, :] = (hi * f).astype(BF)
    moves.append(pltpu.make_async_copy(buf.at[:, 256:384], send.at[:, 256:384], sem.at[3]))
    moves[3].start()
    for m in moves:
        m.wait()


def attn_grad(order, recv, qd, stats):
    heads = qd.shape[0]
    n = recv.shape[0]
    return pl.pallas_call(
        attn_grad_kernel,
        in_specs=[SM, VM, VM, VM],
        out_specs=[HB, HB],
        out_shape=[
            pltpu.HBM((n, 384, 128), BF),
            pltpu.HBM((heads, 128, 512), BF),
        ],
        scratch_shapes=[
            pltpu.VMEM((1024, 128), BF),
            pltpu.VMEM((1024, 128), BF),
            pltpu.VMEM((1024, 128), F32),
            pltpu.VMEM((1024, 128), F32),
            pltpu.VMEM((heads, 512), F32),
            pltpu.VMEM((heads, 512), F32),
            pltpu.VMEM((heads, 128, 512), F32),
            pltpu.SMEM((16,), jnp.int32),
            pltpu.VMEM((heads, 128, 512), BF),
            pltpu.VMEM((n, 384, 128), BF),
            pltpu.SemaphoreType.DMA((4,)),
        ],
        compiler_params=pltpu.CompilerParams(vmem_limit_bytes=20 << 20),
        name="attn_grad",
    )(order, recv, qd, stats)


def ssd_grad_kernel(
    xh, yh, states, cum, b_ref, c_ref,
    dx_ref, da_ref, db_ref, dc_ref,
    g_s, dg_s, dct, dbt, bt_s, ct_s, colp, dcol, drow, dxs,
):
    h = pl.program_id(0)
    heads = pl.num_programs(0)
    nb = xh.shape[1] // BLOCK
    rows = iota((BLOCK, BLOCK), 0)
    lanes = iota((BLOCK, BLOCK), 1)

    @pl.when(h == 0)
    def _():
        dg_s[...] = jnp.zeros_like(dg_s)
        dct[...] = jnp.zeros_like(dct)
        dbt[...] = jnp.zeros_like(dbt)
        dcol[...] = jnp.zeros_like(dcol)
        drow[...] = jnp.zeros_like(drow)
        for k in range(nb):
            sl = slice(k * BLOCK, (k + 1) * BLOCK)
            b = b_ref[sl, :]
            c = c_ref[sl, :]
            g_s[k] = jnp.where(rows <= lanes, dot(b, c, 1, 1, HIGHEST), 0.0)
            bt_s[k] = b.T
            ct_s[k] = c.T
            cm = cum[:, sl]
            tl = jnp.exp(cm[:, BLOCK - 1 :] - cm)
            parts = [p.astype(F32) for p in pieces(cm, 3) + pieces(tl, 2)]
            parts.append(jnp.zeros((BLOCK - 5 * heads_of(cum), BLOCK), F32))
            colp[k] = jnp.concatenate(parts, axis=0).T.astype(BF)

    nh = heads_of(cum)
    pr = iota((BLOCK, 2 * BLOCK), 0)
    pc = iota((BLOCK, 2 * BLOCK), 1)
    mine = (pr % nh) == h
    left = jnp.logical_and(pr < 3 * nh, pc < BLOCK)
    right = jnp.logical_and(jnp.logical_and(pr >= 3 * nh, pr < 5 * nh), pc >= BLOCK)
    pick = jnp.where(jnp.logical_and(mine, jnp.logical_or(left, right)), 1.0, 0.0).astype(BF)

    crow = cum[pl.ds(h, 1), :]
    x = [xh[0, k * BLOCK : (k + 1) * BLOCK, :] for k in range(nb)]
    y = [yh[0, k * BLOCK : (k + 1) * BLOCK, :] for k in range(nb)]
    c = [crow[:, k * BLOCK : (k + 1) * BLOCK] for k in range(nb)]
    total = [v[:, BLOCK - 1 :] for v in c]
    keep = [jnp.exp(t) for t in total]
    tail = [jnp.exp(t - v) for t, v in zip(total, c)]
    grow = [jnp.exp(v) for v in c]
    state = [states[0, 0:128, :].astype(F32)]
    for k in range(nb - 1):
        bs = (bt_s[k] * tail[k]).astype(BF)
        state.append(keep[k] * state[k] + dot(bs, x[k], 1, 0))
    pull = states[0, 128:256, :].astype(F32)
    for k in reversed(range(nb)):
        cols = dot(colp[k], pick, 1, 0)
        decay = jnp.exp(jnp.minimum(c[k] - cols[:, :BLOCK], 0.0))
        w = g_s[k] * decay
        dw = dot(x[k], y[k], 1, 1)
        t = dw * decay
        dg_s[k] += t
        z = t * g_s[k]
        sb = state[k].astype(BF)
        pb = pull.astype(BF)
        bs = (b_ref[k * BLOCK : (k + 1) * BLOCK, :] * cols[:, BLOCK:]).astype(BF)
        dx = dot(w.astype(BF), y[k], 1, 0) + dot(bs, pb, 1, 0)
        dxs[pl.ds(k * BLOCK * heads + h, BLOCK, stride=nh), :] = dx
        dcs = dot(sb, y[k], 1, 1) * grow[k]
        dct[k] += dcs
        q = dcs * ct_s[k]
        dbs = dot(pb, x[k], 1, 1) * tail[k]
        dbt[k] += dbs
        v = dbs * bt_s[k]
        vs = jnp.sum(v, axis=0, keepdims=True)
        line = jnp.sum(z + q, axis=0, keepdims=True) - vs
        cross = keep[k] * jnp.sum(state[k] * pull, axis=0, keepdims=True)
        last = jnp.sum(vs + cross, axis=1, keepdims=True)
        line = jnp.where(iota((1, BLOCK), 1) == BLOCK - 1, line + last, line)
        at = slice(k * BLOCK, (k + 1) * BLOCK)
        drow[:, at] = jnp.where(iota((nh, BLOCK), 0) == h, line, drow[:, at])
        zc = jnp.sum(z, axis=1, keepdims=True)
        dcol[k] = jnp.where(lanes == h, zc, dcol[k])
        if k > 0:
            cs = (ct_s[k] * grow[k]).astype(BF)
            pull = keep[k] * pull + dot(cs, y[k], 1, 0).astype(BF).astype(F32)

    @pl.when(h == heads - 1)
    def _():
        late = (rows >= lanes).astype(F32)
        for k in range(nb):
            sl = slice(k * BLOCK, (k + 1) * BLOCK)
            dg = jnp.where(rows <= lanes, dg_s[k], 0.0)
            db_ref[sl, :] = dbt[k].T + dot(dg, c_ref[sl, :], 1, 0, HIGHEST)
            dc_ref[sl, :] = dct[k].T + dot(dg.T, b_ref[sl, :], 1, 0, HIGHEST)
            da_ref[:, sl] = dot(drow[:, sl] - dcol[k].T[:nh], late, 1, 0, HIGHEST)
            dx_ref[sl] = (
                dxs[k * BLOCK * nh : (k + 1) * BLOCK * nh, :]
                .reshape(BLOCK, nh, 128)
                .astype(BF)
            )


def heads_of(cum):
    return cum.shape[0]


def ssd_grad(xh, yh, states, cum, b, c):
    heads, tok, width = xh.shape
    nb = tok // BLOCK
    rows = states.shape[1]
    per = pl.BlockSpec((1, tok, width), lambda h: (h, 0, 0))
    whole = lambda *s: pl.BlockSpec(s, lambda h: (0,) * len(s))
    sq = pltpu.VMEM((nb, 128, 128), F32)
    return pl.pallas_call(
        ssd_grad_kernel,
        grid=(heads,),
        in_specs=[
            per,
            per,
            pl.BlockSpec((1, rows, 128), lambda h: (h, 0, 0)),
            whole(heads, tok),
            whole(tok, 128),
            whole(tok, 128),
        ],
        out_specs=[
            whole(tok, heads, width),
            whole(heads, tok),
            whole(tok, 128),
            whole(tok, 128),
        ],
        out_shape=[
            jax.ShapeDtypeStruct((tok, heads, width), BF),
            jax.ShapeDtypeStruct((heads, tok), F32),
            jax.ShapeDtypeStruct((tok, 128), F32),
            jax.ShapeDtypeStruct((tok, 128), F32),
        ],
        scratch_shapes=[
            sq, sq, sq, sq, sq, sq,
            pltpu.VMEM((nb, 128, 128), BF),
            sq,
            pltpu.VMEM((heads, tok), F32),
            pltpu.VMEM((tok * heads, width), F32),
        ],
        compiler_params=pltpu.CompilerParams(vmem_limit_bytes=48 << 20),
        name="ssd_grad",
    )(xh, yh, states, cum, b, c)


def finish_kernel(dqt, dkv, dq, dk, dv):
    dq[...] = dqt[0].astype(F32).T.astype(BF)
    for h in range(dkv.shape[0]):
        for j in range(2):
            to = slice(256 * j + 32 * h, 256 * j + 32 * h + 32)
            dk[to, :] = dkv[h, 32 * j : 32 * j + 32, :]
            dv[to, :] = dkv[h, 64 + 32 * j : 96 + 32 * j, :]


def finish(dqt, dkv):
    out = jax.ShapeDtypeStruct((512, 128), BF)
    return pl.pallas_call(
        finish_kernel,
        in_specs=[VM, VM],
        out_specs=[VM, VM, VM],
        out_shape=[out, out, out],
        name="finish",
    )(dqt, dkv)


def per_device(
    ssd_input, log_decay, input_map, output_map, ssd_cotangent,
    queries, key_rows, value_rows, attn_cotangent, pair_order,
):
    tok, heads, width = ssd_input.shape
    b = input_map.reshape(tok, 128)
    c = output_map.reshape(tok, 128)
    send, xh, yh, cum, qd = ssd_send(
        ssd_input, ssd_cotangent, log_decay.T, b, c, key_rows, value_rows,
        queries.reshape(tok, 128), attn_cotangent.reshape(tok, 128),
    )
    qd = lax.all_gather(qd, "head")
    recv = lax.all_to_all(send, "seq", 0, 0)
    stats = lax.all_gather(attn_stat(pair_order, recv, qd), "head")
    back, dqt = attn_grad(pair_order, recv, qd, stats)
    dqt = lax.psum_scatter(dqt, "head", scatter_dimension=0, tiled=True)
    states = lax.all_to_all(back, "seq", 0, 0)
    dkv = jnp.sum(states[:, 256:, :].astype(F32), axis=0).astype(BF)
    dkv = lax.all_gather(dkv, "head")
    dx, da, db, dc = ssd_grad(xh, yh, states, cum, b, c)
    dq, dk, dv = finish(dqt, dkv)
    return (
        dx,
        da.T,
        db.reshape(tok, 1, 128),
        dc.reshape(tok, 1, 128),
        dq.reshape(tok, 1, 128),
        dk,
        dv,
    )


def solution(mesh):
    tok = P("seq", "head", None)
    return jax.shard_map(
        per_device,
        mesh=mesh,
        in_specs=(
            tok, P("seq", "head"), tok, tok, tok, tok,
            P("seq", None), P("seq", None), tok, P(),
        ),
        out_specs=(tok, P("seq", "head"), tok, tok, tok, P("seq", None), P("seq", None)),
        check_vma=False,
    )
```

```python
import functools

import jax
import jax.numpy as jnp
from jax import lax
from jax.experimental import pallas as pl
from jax.experimental.pallas import tpu as pltpu
from jax.sharding import PartitionSpec as P

BLOCK = 128
BF = jnp.bfloat16
F32 = jnp.float32
HIGHEST = lax.Precision.HIGHEST
NEG = -1e30
LOG2E = 1.4426950408889634
STATE_ROWS = 256
TOTAL_ROWS = 16


def dot(a, b, ca, cb, precision=None):
    return lax.dot_general(
        a, b, (((ca,), (cb,)), ((), ())), precision=precision, preferred_element_type=F32
    )


def iota(shape, dim):
    return lax.broadcasted_iota(jnp.int32, shape, dim)


def pieces(v, count):
    out = []
    for _ in range(count):
        p = v.astype(BF)
        out.append(p)
        v = v - p.astype(F32)
    return out


def ssd_send_kernel(
    x_ref, y_ref, at_ref, b_ref, c_ref, k_ref, v_ref, q_ref, do_ref,
    send_ref, xh_ref, yh_ref, cum_ref, qd_ref, st, pu, run,
):
    k = pl.program_id(0)
    heads = x_ref.shape[1]

    @pl.when(k == 0)
    def _():
        st[...] = jnp.zeros_like(st)
        pu[...] = jnp.zeros_like(pu)
        run[...] = jnp.zeros_like(run)

    upto = (iota((BLOCK, BLOCK), 0) <= iota((BLOCK, BLOCK), 1)).astype(F32)
    cum = dot(at_ref[...], upto, 1, 0, HIGHEST)
    cum_ref[...] = cum
    total = cum[:, BLOCK - 1 :]
    grow = jnp.exp(cum)
    tail = jnp.exp(total - cum)
    keep = jnp.exp(total)
    before = run[:, :1]
    early = jnp.exp(before)
    run[...] = jnp.broadcast_to(before + total, run.shape)
    bt = b_ref[...].T
    ct = c_ref[...].T
    xt = jnp.swapaxes(x_ref[...], 0, 1)
    yt = jnp.swapaxes(y_ref[...], 0, 1)
    for h in range(heads):
        x = xt[h]
        y = yt[h]
        xh_ref[h] = x
        yh_ref[h] = y
        bs = (bt * tail[h : h + 1, :]).astype(BF)
        cs = (ct * grow[h : h + 1, :]).astype(BF)
        st[h] = keep[h : h + 1, :] * st[h] + dot(bs, x, 1, 0)
        pu[h] = pu[h] + early[h : h + 1, :] * dot(cs, y, 1, 0).astype(BF).astype(F32)

    @pl.when(k == pl.num_programs(0) - 1)
    def _():
        qd_ref[0] = q_ref[...]
        qd_ref[1] = do_ref[...]
        at = pl.multiple_of(lax.axis_index("head") * 32, 32)
        half = k_ref.shape[0] // 2
        subs = [r[pl.ds(at + o, 32), :] for r in (k_ref, v_ref) for o in (0, half)]
        three = pieces(run[...], 3)
        for h in range(heads):
            send_ref[h, 0:128, :] = st[h].astype(BF)
            send_ref[h, 128:256, :] = pu[h].astype(BF)
            for i, s in enumerate(subs):
                send_ref[h, 256 + 32 * i : 288 + 32 * i, :] = s
            rows = iota((TOTAL_ROWS, 128), 0)
            t = jnp.zeros((TOTAL_ROWS, 128), F32)
            for i, p in enumerate(three):
                t = jnp.where(rows == i, p[h : h + 1, :].astype(F32), t)
            send_ref[h, 384:400, :] = t.astype(BF)


def ssd_send(x, y, at, b, c, keys, values, q, do):
    tok, heads, width = x.shape
    nb = tok // BLOCK
    blk = pl.BlockSpec((BLOCK, heads, width), lambda k: (k, 0, 0))
    mat = pl.BlockSpec((BLOCK, 128), lambda k: (k, 0))
    row = pl.BlockSpec((heads, BLOCK), lambda k: (0, k))
    hm = pl.BlockSpec((heads, BLOCK, width), lambda k: (0, k, 0))
    whole = pl.BlockSpec((tok, 128), lambda k: (0, 0))
    rows = STATE_ROWS + 128 + TOTAL_ROWS
    return pl.pallas_call(
        ssd_send_kernel,
        grid_spec=pltpu.PrefetchScalarGridSpec(
            num_scalar_prefetch=0,
            grid=(nb,),
            in_specs=[blk, blk, row, mat, mat, whole, whole, whole, whole],
            out_specs=[
                pl.BlockSpec((heads, rows, 128), lambda k: (0, 0, 0)),
                hm,
                hm,
                row,
                pl.BlockSpec((2, tok, 128), lambda k: (0, 0, 0)),
            ],
            scratch_shapes=[
                pltpu.VMEM((heads, 128, 128), F32),
                pltpu.VMEM((heads, 128, 128), F32),
                pltpu.VMEM((heads, 128), F32),
            ],
        ),
        out_shape=[
            jax.ShapeDtypeStruct((heads, rows, 128), BF),
            jax.ShapeDtypeStruct((heads, tok, width), BF),
            jax.ShapeDtypeStruct((heads, tok, width), BF),
            jax.ShapeDtypeStruct((heads, tok), F32),
            jax.ShapeDtypeStruct((2, tok, 128), BF),
        ],
        compiler_params=pltpu.CompilerParams(vmem_limit_bytes=60 << 20),
        name="ssd_send",
    )(x, y, at, b, c, keys, values, q, do)


def sort_keys(order, inverse, recv, ks, vs):
    for e in range(16):
        inverse[order[e]] = e
    for b in range(32):
        src = inverse[b if b < 16 else 31 - b]
        o = 0 if b < 16 else 32
        ks[32 * b : 32 * b + 32, :] = recv[src, 256 + o : 288 + o, :]
        vs[32 * b : 32 * b + 32, :] = recv[src, 320 + o : 352 + o, :]


def item_at(order, size, i):
    first = order[lax.axis_index("seq")]
    per = size // 32
    n0 = (first + per) // per
    late = (i >= n0).astype(jnp.int32)
    g = i - late * n0
    block = jnp.where(late == 1, 31 - first, first)
    kr = iota((size, 256), 0)
    key_at = (g * per + kr // 32) * 256 + lax.axis_index("head") * 32 + kr % 32
    bias = jnp.where(key_at <= block * 256 + iota((size, 256), 1), 0.0, NEG)
    return pl.multiple_of(g * size, size), pl.multiple_of(late * 256, 256), bias


def attn_stat_kernel(order, recv, qd, stat, ks, vs, inverse):
    heads = qd.shape[0]
    scale = LOG2E * 128**-0.5
    sort_keys(order, inverse, recv, ks, vs)
    stat[0] = jnp.full((heads, 512), NEG, F32)
    stat[1:] = jnp.zeros((2, heads, 512), F32)

    def item(i, carry):
        kat, rat, bias = item_at(order, 256, i)
        kg = ks[pl.ds(kat, 256), :]
        vg = vs[pl.ds(kat, 256), :]
        for h in range(heads):
            s = dot(kg, qd[h, 0, pl.ds(rat, 256), :], 1, 1) * scale + bias
            dp = dot(vg, qd[h, 1, pl.ds(rat, 256), :], 1, 1)
            at = (slice(h, h + 1), pl.ds(rat, 256))
            old = stat[0, *at]
            top = jnp.maximum(old, jnp.max(s, axis=0, keepdims=True))
            p = jnp.exp2(s - top)
            fix = jnp.exp2(old - top)
            stat[0, *at] = top
            stat[1, *at] = fix * stat[1, *at] + jnp.sum(p, axis=0, keepdims=True)
            stat[2, *at] = fix * stat[2, *at] + jnp.sum(p * dp, axis=0, keepdims=True)
        return carry

    lax.fori_loop(0, 5, item, 0)


VM = pl.BlockSpec(memory_space=pltpu.VMEM)
SM = pl.BlockSpec(memory_space=pltpu.SMEM)
HB = pl.BlockSpec(memory_space=pltpu.HBM)


def attn_stat(order, recv, qd):
    heads = qd.shape[0]
    return pl.pallas_call(
        attn_stat_kernel,
        in_specs=[SM, VM, VM],
        out_specs=VM,
        out_shape=jax.ShapeDtypeStruct((3, heads, 512), F32),
        scratch_shapes=[
            pltpu.VMEM((1024, 128), BF),
            pltpu.VMEM((1024, 128), BF),
            pltpu.SMEM((16,), jnp.int32),
        ],
        compiler_params=pltpu.CompilerParams(vmem_limit_bytes=20 << 20),
        name="attn_stat",
    )(order, recv, qd)


def attn_grad_kernel(
    order, recv, qd, s0, s1, s2, s3, send, dqt, ks, vs, dk, dv, lse, delta, dqs, inverse, dqo, buf, sem
):
    heads = qd.shape[0]
    scale = 128**-0.5
    sort_keys(order, inverse, recv, ks, vs)
    n = recv.shape[0]
    state = jnp.zeros((128, 128), F32)
    for e in range(n):
        buf[e, 0:128, :] = state.astype(BF)
        if e < n - 1:
            t = recv[e, 384:400, :].astype(F32)
            keep = jnp.exp(t[0:1] + t[1:2] + t[2:3])
            state = keep * state + recv[e, 0:128, :].astype(F32)
    moves = [pltpu.make_async_copy(buf.at[:, 0:128], send.at[:, 0:128], sem.at[0])]
    moves[0].start()
    pull = jnp.zeros((128, 128), F32)
    for e in reversed(range(n)):
        buf[e, 128:256, :] = pull.astype(BF)
        if e > 0:
            t = recv[e, 384:400, :].astype(F32)
            keep = jnp.exp(t[0:1] + t[1:2] + t[2:3])
            pull = keep * pull + recv[e, 128:256, :].astype(F32)
    moves.append(pltpu.make_async_copy(buf.at[:, 128:256], send.at[:, 128:256], sem.at[1]))
    moves[1].start()
    stats = (s0, s1, s2, s3)
    top = functools.reduce(jnp.maximum, [r[0] for r in stats])
    total = jnp.zeros_like(top)
    dsum = jnp.zeros_like(top)
    for r in stats:
        f = jnp.exp2(r[0] - top)
        total = total + f * r[1]
        dsum = dsum + f * r[2]
    lse[...] = top + jnp.log2(total)
    delta[...] = dsum / total
    dk[...] = jnp.zeros_like(dk)
    dv[...] = jnp.zeros_like(dv)
    dqs[...] = jnp.zeros_like(dqs)

    def item(i, carry):
        kat, rat, bias = item_at(order, 512, i)
        kg = ks[pl.ds(kat, 512), :]
        vg = vs[pl.ds(kat, 512), :]
        kt = kg.astype(F32).T.astype(BF)
        dkg = dk[pl.ds(kat, 512), :]
        dvg = dv[pl.ds(kat, 512), :]
        for h in range(heads):
            q = qd[h, 0, pl.ds(rat, 256), :]
            do = qd[h, 1, pl.ds(rat, 256), :]
            s = dot(kg, q, 1, 1) * (scale * LOG2E) + bias
            dp = dot(vg, do, 1, 1)
            p = jnp.exp2(s - lse[h : h + 1, pl.ds(rat, 256)])
            ds = (p * (dp - delta[h : h + 1, pl.ds(rat, 256)])).astype(BF)
            dvg = dvg + dot(p.astype(BF), do, 1, 0)
            dkg = dkg + dot(ds, q, 1, 0)
            dqs[h, :, pl.ds(rat, 256)] += dot(kt, ds, 1, 0)
        dk[pl.ds(kat, 512), :] = dkg
        dv[pl.ds(kat, 512), :] = dvg
        return carry

    lax.fori_loop(0, 3, item, 0)
    dqo[...] = (dqs[...] * scale).astype(BF)
    moves.append(pltpu.make_async_copy(dqo, dqt, sem.at[2]))
    moves[2].start()
    for e in range(16):
        b = order[e]
        for j, (r, f) in enumerate(((dk, scale), (dv, 1.0))):
            lo = r[pl.ds(pl.multiple_of(b * 32, 32), 32), :]
            hi = r[pl.ds(pl.multiple_of((31 - b) * 32, 32), 32), :]
            buf[e, 256 + 64 * j : 288 + 64 * j, :] = (lo * f).astype(BF)
            buf[e, 288 + 64 * j : 320 + 64 * j, :] = (hi * f).astype(BF)
    moves.append(pltpu.make_async_copy(buf.at[:, 256:384], send.at[:, 256:384], sem.at[3]))
    moves[3].start()
    for m in moves:
        m.wait()


def attn_grad(order, recv, qd, *stats):
    heads = qd.shape[0]
    n = recv.shape[0]
    return pl.pallas_call(
        attn_grad_kernel,
        in_specs=[SM] + [VM] * 6,
        out_specs=[HB, HB],
        out_shape=[
            pltpu.HBM((n, 384, 128), BF),
            pltpu.HBM((heads, 128, 512), BF),
        ],
        scratch_shapes=[
            pltpu.VMEM((1024, 128), BF),
            pltpu.VMEM((1024, 128), BF),
            pltpu.VMEM((1024, 128), F32),
            pltpu.VMEM((1024, 128), F32),
            pltpu.VMEM((heads, 512), F32),
            pltpu.VMEM((heads, 512), F32),
            pltpu.VMEM((heads, 128, 512), F32),
            pltpu.SMEM((16,), jnp.int32),
            pltpu.VMEM((heads, 128, 512), BF),
            pltpu.VMEM((n, 384, 128), BF),
            pltpu.SemaphoreType.DMA((4,)),
        ],
        compiler_params=pltpu.CompilerParams(vmem_limit_bytes=20 << 20),
        name="attn_grad",
    )(order, recv, qd, *stats)


def ssd_grad_kernel(
    xh, yh, states, cum, b_ref, c_ref,
    dx_ref, da_ref, db_ref, dc_ref,
    g_s, dg_s, dct, dbt, bt_s, ct_s, colp, dcol, drow, dxs,
):
    base = pl.program_id(0) * 8
    heads = pl.num_programs(0) * 8
    nb = xh.shape[1] // BLOCK
    rows = iota((BLOCK, BLOCK), 0)
    lanes = iota((BLOCK, BLOCK), 1)

    @pl.when(base == 0)
    def _():
        dg_s[...] = jnp.zeros_like(dg_s)
        dct[...] = jnp.zeros_like(dct)
        dbt[...] = jnp.zeros_like(dbt)
        dcol[...] = jnp.zeros_like(dcol)
        drow[...] = jnp.zeros_like(drow)
        for k in range(nb):
            sl = slice(k * BLOCK, (k + 1) * BLOCK)
            b = b_ref[sl, :]
            c = c_ref[sl, :]
            g_s[k] = jnp.where(rows <= lanes, dot(b, c, 1, 1, HIGHEST), 0.0)
            bt_s[k] = b.T
            ct_s[k] = c.T
            cm = cum[:, sl]
            tl = jnp.exp(cm[:, BLOCK - 1 :] - cm)
            gap = jnp.zeros((BLOCK // 2 - heads_of(cum), BLOCK), F32)
            colp[k] = jnp.concatenate([cm, gap, tl, gap], axis=0).T

    nh = heads_of(cum)
    turned = [pltpu.roll(colp[k], lax.rem(BLOCK - base, BLOCK), 1) for k in range(nb)]
    for hh in range(8):
        h = base + hh
        crow = cum[pl.ds(h, 1), :]
        x = [xh[hh, k * BLOCK : (k + 1) * BLOCK, :] for k in range(nb)]
        y = [yh[hh, k * BLOCK : (k + 1) * BLOCK, :] for k in range(nb)]
        c = [crow[:, k * BLOCK : (k + 1) * BLOCK] for k in range(nb)]
        total = [v[:, BLOCK - 1 :] for v in c]
        keep = [jnp.exp(t) for t in total]
        tail = [jnp.exp(t - v) for t, v in zip(total, c)]
        grow = [jnp.exp(v) for v in c]
        state = [states[hh, 0:128, :].astype(F32)]
        for k in range(nb - 1):
            bs = (bt_s[k] * tail[k]).astype(BF)
            state.append(keep[k] * state[k] + dot(bs, x[k], 1, 0))
        pull = states[hh, 128:256, :].astype(F32)
        for k in reversed(range(nb)):
            decay = jnp.exp(jnp.minimum(c[k] - turned[k][:, hh : hh + 1], 0.0))
            w = g_s[k] * decay
            sb = state[k].astype(BF)
            xy = dot(jnp.concatenate([x[k], sb], axis=0), y[k], 1, 1)
            dw = xy[:BLOCK]
            t = dw * decay
            dg_s[k] += t
            z = t * g_s[k]
            pb = pull.astype(BF)
            bs = (b_ref[k * BLOCK : (k + 1) * BLOCK, :] * turned[k][:, 64 + hh : 65 + hh]).astype(BF)
            cs = (ct_s[k] * grow[k]).astype(BF)
            wy = dot(jnp.concatenate([w.astype(BF), cs], axis=0), y[k], 1, 0)
            dx = wy[:BLOCK] + dot(bs, pb, 1, 0)
            dxs[pl.ds(k * BLOCK * heads + h, BLOCK, stride=nh), :] = dx
            dcs = xy[BLOCK:] * grow[k]
            dct[k] += dcs
            q = dcs * ct_s[k]
            dbs = dot(pb, x[k], 1, 1) * tail[k]
            dbt[k] += dbs
            v = dbs * bt_s[k]
            vs = jnp.sum(v, axis=0, keepdims=True)
            line = jnp.sum(z + q, axis=0, keepdims=True) - vs
            cross = keep[k] * jnp.sum(state[k] * pull, axis=0, keepdims=True)
            last = jnp.sum(vs + cross, axis=1, keepdims=True)
            line = jnp.where(iota((1, BLOCK), 1) == BLOCK - 1, line + last, line)
            at = slice(k * BLOCK, (k + 1) * BLOCK)
            drow[:, at] = jnp.where(iota((nh, BLOCK), 0) == h, line, drow[:, at])
            zc = jnp.sum(z, axis=1, keepdims=True)
            dcol[k] = jnp.where(lanes == h, zc, dcol[k])
            if k > 0:
                pull = keep[k] * pull + wy[BLOCK:].astype(BF).astype(F32)

    @pl.when(base == heads - 8)
    def _():
        late = (rows >= lanes).astype(F32)
        for k in range(nb):
            sl = slice(k * BLOCK, (k + 1) * BLOCK)
            dg = jnp.where(rows <= lanes, dg_s[k], 0.0)
            db_ref[sl, :] = dbt[k].T + dot(dg, c_ref[sl, :], 1, 0, HIGHEST)
            dc_ref[sl, :] = dct[k].T + dot(dg.T, b_ref[sl, :], 1, 0, HIGHEST)
            da_ref[:, sl] = dot(drow[:, sl] - dcol[k].T[:nh], late, 1, 0, HIGHEST)
            dx_ref[sl] = (
                dxs[k * BLOCK * nh : (k + 1) * BLOCK * nh, :]
                .reshape(BLOCK, nh, 128)
                .astype(BF)
            )


def heads_of(cum):
    return cum.shape[0]


def ssd_grad(xh, yh, states, cum, b, c):
    heads, tok, width = xh.shape
    nb = tok // BLOCK
    rows = states.shape[1]
    per = pl.BlockSpec((8, tok, width), lambda h: (h, 0, 0))
    whole = lambda *s: pl.BlockSpec(s, lambda h: (0,) * len(s))
    sq = pltpu.VMEM((nb, 128, 128), F32)
    return pl.pallas_call(
        ssd_grad_kernel,
        grid=(heads // 8,),
        in_specs=[
            per,
            per,
            pl.BlockSpec((8, rows, 128), lambda h: (h, 0, 0)),
            whole(heads, tok),
            whole(tok, 128),
            whole(tok, 128),
        ],
        out_specs=[
            whole(tok, heads, width),
            whole(heads, tok),
            whole(tok, 128),
            whole(tok, 128),
        ],
        out_shape=[
            jax.ShapeDtypeStruct((tok, heads, width), BF),
            jax.ShapeDtypeStruct((heads, tok), F32),
            jax.ShapeDtypeStruct((tok, 128), F32),
            jax.ShapeDtypeStruct((tok, 128), F32),
        ],
        scratch_shapes=[
            sq, sq, sq, sq, sq, sq,
            sq,
            sq,
            pltpu.VMEM((heads, tok), F32),
            pltpu.VMEM((tok * heads, width), F32),
        ],
        compiler_params=pltpu.CompilerParams(vmem_limit_bytes=48 << 20),
        cost_estimate=pl.CostEstimate(
            flops=6 * 10**9, bytes_accessed=10**7, transcendentals=10**6
        ),
        name="ssd_grad",
    )(xh, yh, states, cum, b, c)


def finish_kernel(dqt, *refs):
    parts, (dq, dk, dv) = refs[:8], refs[8:]
    dq[...] = dqt[0].astype(F32).T.astype(BF)
    place = lax.axis_index("head")
    for m, r in enumerate(parts):
        h = place ^ m
        for j in range(2):
            to = pl.ds(pl.multiple_of(256 * j + 32 * h, 32), 32)
            dk[to, :] = r[32 * j : 32 * j + 32, :]
            dv[to, :] = r[64 + 32 * j : 96 + 32 * j, :]


def finish(dqt, parts):
    out = jax.ShapeDtypeStruct((512, 128), BF)
    return pl.pallas_call(
        finish_kernel,
        in_specs=[VM] * 9,
        out_specs=[VM, VM, VM],
        out_shape=[out, out, out],
        name="finish",
    )(dqt, *parts)


def swap(v, m):
    return lax.ppermute(v, "head", [(i, i ^ m) for i in range(8)])


def join(a, b):
    top = jnp.maximum(a[0], b[0])
    f, g = jnp.exp2(a[0] - top), jnp.exp2(b[0] - top)
    return jnp.stack([top, f * a[1] + g * b[1], f * a[2] + g * b[2]])


def per_device(
    ssd_input, log_decay, input_map, output_map, ssd_cotangent,
    queries, key_rows, value_rows, attn_cotangent, pair_order,
):
    tok, heads, width = ssd_input.shape
    b = input_map.reshape(tok, 128)
    c = output_map.reshape(tok, 128)
    send, xh, yh, cum, qd = ssd_send(
        ssd_input, ssd_cotangent, log_decay.T, b, c, key_rows, value_rows,
        queries.reshape(tok, 128), attn_cotangent.reshape(tok, 128),
    )
    qd = lax.all_gather(qd, "head")
    recv = lax.all_to_all(send, "seq", 0, 0)
    stat = attn_stat(pair_order, recv, qd)
    stat = join(stat, swap(stat, 1))
    back, dqt = attn_grad(pair_order, recv, qd, stat, *[swap(stat, m) for m in (2, 6, 4)])
    dqt = lax.psum_scatter(dqt, "head", scatter_dimension=0, tiled=True)
    states = lax.all_to_all(back, "seq", 0, 0)
    dkv = jnp.sum(states[:, 256:, :].astype(F32), axis=0).astype(BF)
    parts = [dkv] + [swap(dkv, m) for m in range(1, 8)]
    dx, da, db, dc = ssd_grad(xh, yh, states, cum, b, c)
    dq, dk, dv = finish(dqt, parts)
    return (
        dx,
        da.T,
        db.reshape(tok, 1, 128),
        dc.reshape(tok, 1, 128),
        dq.reshape(tok, 1, 128),
        dk,
        dv,
    )


def solution(mesh):
    tok = P("seq", "head", None)
    return jax.shard_map(
        per_device,
        mesh=mesh,
        in_specs=(
            tok, P("seq", "head"), tok, tok, tok, tok,
            P("seq", None), P("seq", None), tok, P(),
        ),
        out_specs=(tok, P("seq", "head"), tok, tok, tok, P("seq", None), P("seq", None)),
        check_vma=False,
    )
```

```python
import functools

import jax
import jax.numpy as jnp
from jax import lax
from jax.experimental import pallas as pl
from jax.experimental.pallas import tpu as pltpu
from jax.sharding import PartitionSpec as P

BLOCK = 128
BF = jnp.bfloat16
F32 = jnp.float32
HIGHEST = lax.Precision.HIGHEST
NEG = -1e30
LOG2E = 1.4426950408889634
STATE_ROWS = 256
TOTAL_ROWS = 16


def dot(a, b, ca, cb, precision=None):
    return lax.dot_general(
        a, b, (((ca,), (cb,)), ((), ())), precision=precision, preferred_element_type=F32
    )


def iota(shape, dim):
    return lax.broadcasted_iota(jnp.int32, shape, dim)


def pieces(v, count):
    out = []
    for _ in range(count):
        p = v.astype(BF)
        out.append(p)
        v = v - p.astype(F32)
    return out


def ssd_send_kernel(
    x_ref, y_ref, at_ref, b_ref, c_ref, k_ref, v_ref, q_ref, do_ref,
    send_ref, xh_ref, yh_ref, cum_ref, qd_ref, st, pu, run,
):
    k = pl.program_id(0)
    heads = x_ref.shape[1]

    @pl.when(k == 0)
    def _():
        st[...] = jnp.zeros_like(st)
        pu[...] = jnp.zeros_like(pu)
        run[...] = jnp.zeros_like(run)

    upto = (iota((BLOCK, BLOCK), 0) <= iota((BLOCK, BLOCK), 1)).astype(F32)
    cum = dot(at_ref[...], upto, 1, 0, HIGHEST)
    cum_ref[...] = cum
    total = cum[:, BLOCK - 1 :]
    grow = jnp.exp(cum)
    tail = jnp.exp(total - cum)
    keep = jnp.exp(total)
    before = run[:, :1]
    early = jnp.exp(before)
    run[...] = jnp.broadcast_to(before + total, run.shape)
    bt = b_ref[...].T
    ct = c_ref[...].T
    xt = jnp.swapaxes(x_ref[...], 0, 1)
    yt = jnp.swapaxes(y_ref[...], 0, 1)
    for h in range(heads):
        x = xt[h]
        y = yt[h]
        xh_ref[h] = x
        yh_ref[h] = y
        bs = (bt * tail[h : h + 1, :]).astype(BF)
        cs = (ct * grow[h : h + 1, :]).astype(BF)
        st[h] = keep[h : h + 1, :] * st[h] + dot(bs, x, 1, 0)
        pu[h] = pu[h] + early[h : h + 1, :] * dot(cs, y, 1, 0).astype(BF).astype(F32)

    @pl.when(k == pl.num_programs(0) - 1)
    def _():
        qd_ref[0] = q_ref[...]
        qd_ref[1] = do_ref[...]
        at = pl.multiple_of(lax.axis_index("head") * 32, 32)
        half = k_ref.shape[0] // 2
        subs = [r[pl.ds(at + o, 32), :] for r in (k_ref, v_ref) for o in (0, half)]
        three = pieces(run[...], 3)
        for h in range(heads):
            send_ref[h, 0:128, :] = st[h].astype(BF)
            send_ref[h, 128:256, :] = pu[h].astype(BF)
            for i, s in enumerate(subs):
                send_ref[h, 256 + 32 * i : 288 + 32 * i, :] = s
            rows = iota((TOTAL_ROWS, 128), 0)
            t = jnp.zeros((TOTAL_ROWS, 128), F32)
            for i, p in enumerate(three):
                t = jnp.where(rows == i, p[h : h + 1, :].astype(F32), t)
            send_ref[h, 384:400, :] = t.astype(BF)


def ssd_send(x, y, at, b, c, keys, values, q, do):
    tok, heads, width = x.shape
    nb = tok // BLOCK
    blk = pl.BlockSpec((BLOCK, heads, width), lambda k: (k, 0, 0))
    mat = pl.BlockSpec((BLOCK, 128), lambda k: (k, 0))
    row = pl.BlockSpec((heads, BLOCK), lambda k: (0, k))
    hm = pl.BlockSpec((heads, BLOCK, width), lambda k: (0, k, 0))
    whole = pl.BlockSpec((tok, 128), lambda k: (0, 0))
    rows = STATE_ROWS + 128 + TOTAL_ROWS
    return pl.pallas_call(
        ssd_send_kernel,
        grid_spec=pltpu.PrefetchScalarGridSpec(
            num_scalar_prefetch=0,
            grid=(nb,),
            in_specs=[blk, blk, row, mat, mat, whole, whole, whole, whole],
            out_specs=[
                pl.BlockSpec((heads, rows, 128), lambda k: (0, 0, 0)),
                hm,
                hm,
                row,
                pl.BlockSpec((2, tok, 128), lambda k: (0, 0, 0)),
            ],
            scratch_shapes=[
                pltpu.VMEM((heads, 128, 128), F32),
                pltpu.VMEM((heads, 128, 128), F32),
                pltpu.VMEM((heads, 128), F32),
            ],
        ),
        out_shape=[
            jax.ShapeDtypeStruct((heads, rows, 128), BF),
            jax.ShapeDtypeStruct((heads, tok, width), BF),
            jax.ShapeDtypeStruct((heads, tok, width), BF),
            jax.ShapeDtypeStruct((heads, tok), F32),
            jax.ShapeDtypeStruct((2, tok, 128), BF),
        ],
        compiler_params=pltpu.CompilerParams(vmem_limit_bytes=60 << 20),
        cost_estimate=pl.CostEstimate(
            flops=3 * 10**9, bytes_accessed=10**7, transcendentals=10**5
        ),
        name="ssd_send",
    )(x, y, at, b, c, keys, values, q, do)


VM = pl.BlockSpec(memory_space=pltpu.VMEM)
SM = pl.BlockSpec(memory_space=pltpu.SMEM)
HB = pl.BlockSpec(memory_space=pltpu.HBM)


def scan_kernel(recv, back):
    n = recv.shape[0]
    state = jnp.zeros((128, 128), F32)
    for e in range(n):
        back[e, 0:128, :] = state.astype(BF)
        if e < n - 1:
            t = recv[e, 384:400, :].astype(F32)
            keep = jnp.exp(t[0:1] + t[1:2] + t[2:3])
            state = keep * state + recv[e, 0:128, :].astype(F32)
    pull = jnp.zeros((128, 128), F32)
    for e in reversed(range(n)):
        back[e, 128:256, :] = pull.astype(BF)
        if e > 0:
            t = recv[e, 384:400, :].astype(F32)
            keep = jnp.exp(t[0:1] + t[1:2] + t[2:3])
            pull = keep * pull + recv[e, 128:256, :].astype(F32)


def scan(recv):
    n = recv.shape[0]
    return pl.pallas_call(
        scan_kernel,
        in_specs=[VM],
        out_specs=VM,
        out_shape=jax.ShapeDtypeStruct((n, 256, 128), BF),
        compiler_params=pltpu.CompilerParams(vmem_limit_bytes=20 << 20),
        name="scan",
    )(recv)


def sort_keys(order, inverse, recv, ks, vs):
    for e in range(16):
        inverse[order[e]] = e
    for b in range(32):
        src = inverse[b if b < 16 else 31 - b]
        o = 0 if b < 16 else 32
        ks[32 * b : 32 * b + 32, :] = recv[src, 256 + o : 288 + o, :]
        vs[32 * b : 32 * b + 32, :] = recv[src, 320 + o : 352 + o, :]


def item_at(order, size, i):
    first = order[lax.axis_index("seq")]
    per = size // 32
    n0 = (first + per) // per
    late = (i >= n0).astype(jnp.int32)
    g = i - late * n0
    block = jnp.where(late == 1, 31 - first, first)
    kr = iota((size, 256), 0)
    key_at = (g * per + kr // 32) * 256 + lax.axis_index("head") * 32 + kr % 32
    bias = jnp.where(key_at <= block * 256 + iota((size, 256), 1), 0.0, NEG)
    return pl.multiple_of(g * size, size), pl.multiple_of(late * 256, 256), bias


def attn_stat_kernel(order, recv, *refs):
    qd, (stat, ks, vs, inverse) = refs[:8], refs[8:]
    heads = len(qd)
    scale = LOG2E * 128**-0.5
    sort_keys(order, inverse, recv, ks, vs)
    stat[0] = jnp.full((heads, 512), NEG, F32)
    stat[1:] = jnp.zeros((2, heads, 512), F32)

    def item(i, carry):
        kat, rat, bias = item_at(order, 256, i)
        kg = ks[pl.ds(kat, 256), :]
        vg = vs[pl.ds(kat, 256), :]
        for h in range(heads):
            s = dot(kg, qd[h][0, pl.ds(rat, 256), :], 1, 1) * scale + bias
            dp = dot(vg, qd[h][1, pl.ds(rat, 256), :], 1, 1)
            at = (slice(h, h + 1), pl.ds(rat, 256))
            old = stat[0, *at]
            top = jnp.maximum(old, jnp.max(s, axis=0, keepdims=True))
            p = jnp.exp2(s - top)
            fix = jnp.exp2(old - top)
            stat[0, *at] = top
            stat[1, *at] = fix * stat[1, *at] + jnp.sum(p, axis=0, keepdims=True)
            stat[2, *at] = fix * stat[2, *at] + jnp.sum(p * dp, axis=0, keepdims=True)
        return carry

    lax.fori_loop(0, 5, item, 0)


def attn_stat(order, recv, qd):
    heads = len(qd)
    return pl.pallas_call(
        attn_stat_kernel,
        in_specs=[SM] + [VM] * 9,
        out_specs=VM,
        out_shape=jax.ShapeDtypeStruct((3, heads, 512), F32),
        scratch_shapes=[
            pltpu.VMEM((1024, 128), BF),
            pltpu.VMEM((1024, 128), BF),
            pltpu.SMEM((16,), jnp.int32),
        ],
        compiler_params=pltpu.CompilerParams(vmem_limit_bytes=20 << 20),
        cost_estimate=pl.CostEstimate(
            flops=4 * 10**9, bytes_accessed=5 * 10**6, transcendentals=10**6
        ),
        name="attn_stat",
    )(order, recv, *qd)


def attn_grad_kernel(order, recv, *refs):
    qd, stats, send, dqt = refs[:8], refs[8:12], refs[12], refs[13:21]
    ks, vs, dk, dv, lse, delta, dqs, inverse, dqo, buf, sem = refs[21:]
    heads = len(qd)
    scale = 128**-0.5
    sort_keys(order, inverse, recv, ks, vs)
    tables = [[r[i] for i in range(3)] for r in stats]
    for m, v in zip((2, 6, 4), tables[1:]):
        v[:] = [turn_rows(x, m) for x in v]
    top = functools.reduce(jnp.maximum, [v[0] for v in tables])
    total = jnp.zeros_like(top)
    dsum = jnp.zeros_like(top)
    for v in tables:
        f = jnp.exp2(v[0] - top)
        total = total + f * v[1]
        dsum = dsum + f * v[2]
    lse[...] = top + jnp.log2(total)
    delta[...] = dsum / total
    dk[...] = jnp.zeros_like(dk)
    dv[...] = jnp.zeros_like(dv)
    dqs[...] = jnp.zeros_like(dqs)

    def item(i, carry):
        kat, rat, bias = item_at(order, 512, i)
        kg = ks[pl.ds(kat, 512), :]
        vg = vs[pl.ds(kat, 512), :]
        kt = kg.astype(F32).T.astype(BF)
        dkg = dk[pl.ds(kat, 512), :]
        dvg = dv[pl.ds(kat, 512), :]
        for h in range(heads):
            q = qd[h][0, pl.ds(rat, 256), :]
            do = qd[h][1, pl.ds(rat, 256), :]
            s = dot(kg, q, 1, 1) * (scale * LOG2E) + bias
            dp = dot(vg, do, 1, 1)
            p = jnp.exp2(s - lse[h : h + 1, pl.ds(rat, 256)])
            ds = (p * (dp - delta[h : h + 1, pl.ds(rat, 256)])).astype(BF)
            dvg = dvg + dot(p.astype(BF), do, 1, 0)
            dkg = dkg + dot(ds, q, 1, 0)
            dqs[h, :, pl.ds(rat, 256)] += dot(kt, ds, 1, 0)
        dk[pl.ds(kat, 512), :] = dkg
        dv[pl.ds(kat, 512), :] = dvg
        return carry

    lax.fori_loop(0, 3, item, 0)
    dqo[...] = (dqs[...] * scale).astype(BF)
    moves = [pltpu.make_async_copy(dqo.at[h], dqt[h], sem.at[h]) for h in range(heads)]
    for m in moves:
        m.start()
    for e in range(16):
        b = order[e]
        for j, (r, f) in enumerate(((dk, scale), (dv, 1.0))):
            lo = r[pl.ds(pl.multiple_of(b * 32, 32), 32), :]
            hi = r[pl.ds(pl.multiple_of((31 - b) * 32, 32), 32), :]
            buf[e, 64 * j : 32 + 64 * j, :] = (lo * f).astype(BF)
            buf[e, 32 + 64 * j : 64 + 64 * j, :] = (hi * f).astype(BF)
    moves.append(pltpu.make_async_copy(buf, send, sem.at[heads]))
    moves[-1].start()
    for m in moves:
        m.wait()


def attn_grad(order, recv, qd, *stats):
    heads = len(qd)
    n = recv.shape[0]
    return pl.pallas_call(
        attn_grad_kernel,
        in_specs=[SM] + [VM] * 13,
        out_specs=[HB] * 9,
        out_shape=[pltpu.HBM((n, 128, 128), BF)] + [pltpu.HBM((128, 512), BF)] * 8,
        scratch_shapes=[
            pltpu.VMEM((1024, 128), BF),
            pltpu.VMEM((1024, 128), BF),
            pltpu.VMEM((1024, 128), F32),
            pltpu.VMEM((1024, 128), F32),
            pltpu.VMEM((heads, 512), F32),
            pltpu.VMEM((heads, 512), F32),
            pltpu.VMEM((heads, 128, 512), F32),
            pltpu.SMEM((16,), jnp.int32),
            pltpu.VMEM((heads, 128, 512), BF),
            pltpu.VMEM((n, 128, 128), BF),
            pltpu.SemaphoreType.DMA((heads + 1,)),
        ],
        compiler_params=pltpu.CompilerParams(vmem_limit_bytes=20 << 20),
        cost_estimate=pl.CostEstimate(
            flops=8 * 10**9, bytes_accessed=6 * 10**6, transcendentals=10**6
        ),
        name="attn_grad",
    )(order, recv, *qd, *stats)


def ssd_grad_kernel(
    xh, yh, states, cum, b_ref, c_ref,
    dx_ref, da_ref, db_ref, dc_ref,
    g_s, dg_s, dct, dbt, bt_s, ct_s, colp, dcol, drow, dxs,
):
    base = pl.program_id(0) * 8
    heads = pl.num_programs(0) * 8
    nb = xh.shape[1] // BLOCK
    rows = iota((BLOCK, BLOCK), 0)
    lanes = iota((BLOCK, BLOCK), 1)

    @pl.when(base == 0)
    def _():
        dg_s[...] = jnp.zeros_like(dg_s)
        dct[...] = jnp.zeros_like(dct)
        dbt[...] = jnp.zeros_like(dbt)
        dcol[...] = jnp.zeros_like(dcol)
        drow[...] = jnp.zeros_like(drow)
        for k in range(nb):
            sl = slice(k * BLOCK, (k + 1) * BLOCK)
            b = b_ref[sl, :]
            c = c_ref[sl, :]
            g_s[k] = jnp.where(rows <= lanes, dot(b, c, 1, 1, HIGHEST), 0.0)
            bt_s[k] = b.T
            ct_s[k] = c.T
            cm = cum[:, sl]
            tl = jnp.exp(cm[:, BLOCK - 1 :] - cm)
            gap = jnp.zeros((BLOCK // 2 - heads_of(cum), BLOCK), F32)
            colp[k] = jnp.concatenate([cm, gap, tl, gap], axis=0).T

    nh = heads_of(cum)
    turned = [pltpu.roll(colp[k], lax.rem(BLOCK - base, BLOCK), 1) for k in range(nb)]
    for hh in range(8):
        h = base + hh
        crow = cum[pl.ds(h, 1), :]
        x = [xh[hh, k * BLOCK : (k + 1) * BLOCK, :] for k in range(nb)]
        y = [yh[hh, k * BLOCK : (k + 1) * BLOCK, :] for k in range(nb)]
        c = [crow[:, k * BLOCK : (k + 1) * BLOCK] for k in range(nb)]
        total = [v[:, BLOCK - 1 :] for v in c]
        keep = [jnp.exp(t) for t in total]
        tail = [jnp.exp(t - v) for t, v in zip(total, c)]
        grow = [jnp.exp(v) for v in c]
        state = [states[hh, 0:128, :].astype(F32)]
        for k in range(nb - 1):
            bs = (bt_s[k] * tail[k]).astype(BF)
            state.append(keep[k] * state[k] + dot(bs, x[k], 1, 0))
        pull = states[hh, 128:256, :].astype(F32)
        for k in reversed(range(nb)):
            decay = jnp.exp(jnp.minimum(c[k] - turned[k][:, hh : hh + 1], 0.0))
            w = g_s[k] * decay
            sb = state[k].astype(BF)
            xy = dot(jnp.concatenate([x[k], sb], axis=0), y[k], 1, 1)
            dw = xy[:BLOCK]
            t = dw * decay
            dg_s[k] += t
            z = t * g_s[k]
            pb = pull.astype(BF)
            bs = (b_ref[k * BLOCK : (k + 1) * BLOCK, :] * turned[k][:, 64 + hh : 65 + hh]).astype(BF)
            cs = (ct_s[k] * grow[k]).astype(BF)
            wy = dot(jnp.concatenate([w.astype(BF), cs], axis=0), y[k], 1, 0)
            dx = wy[:BLOCK] + dot(bs, pb, 1, 0)
            dxs[pl.ds(k * BLOCK * heads + h, BLOCK, stride=nh), :] = dx
            dcs = xy[BLOCK:] * grow[k]
            dct[k] += dcs
            q = dcs * ct_s[k]
            dbs = dot(pb, x[k], 1, 1) * tail[k]
            dbt[k] += dbs
            v = dbs * bt_s[k]
            vs = jnp.sum(v, axis=0, keepdims=True)
            line = jnp.sum(z + q, axis=0, keepdims=True) - vs
            cross = keep[k] * jnp.sum(state[k] * pull, axis=0, keepdims=True)
            last = jnp.sum(vs + cross, axis=1, keepdims=True)
            line = jnp.where(iota((1, BLOCK), 1) == BLOCK - 1, line + last, line)
            at = slice(k * BLOCK, (k + 1) * BLOCK)
            drow[:, at] = jnp.where(iota((nh, BLOCK), 0) == h, line, drow[:, at])
            zc = jnp.sum(z, axis=1, keepdims=True)
            dcol[k] = jnp.where(lanes == h, zc, dcol[k])
            if k > 0:
                pull = keep[k] * pull + wy[BLOCK:].astype(BF).astype(F32)

    @pl.when(base == heads - 8)
    def _():
        late = (rows >= lanes).astype(F32)
        for k in range(nb):
            sl = slice(k * BLOCK, (k + 1) * BLOCK)
            dg = jnp.where(rows <= lanes, dg_s[k], 0.0)
            db_ref[sl, :] = dbt[k].T + dot(dg, c_ref[sl, :], 1, 0, HIGHEST)
            dc_ref[sl, :] = dct[k].T + dot(dg.T, b_ref[sl, :], 1, 0, HIGHEST)
            da_ref[:, sl] = dot(drow[:, sl] - dcol[k].T[:nh], late, 1, 0, HIGHEST)
            dx_ref[sl] = (
                dxs[k * BLOCK * nh : (k + 1) * BLOCK * nh, :]
                .reshape(BLOCK, nh, 128)
                .astype(BF)
            )


def heads_of(cum):
    return cum.shape[0]


def ssd_grad(xh, yh, states, cum, b, c):
    heads, tok, width = xh.shape
    nb = tok // BLOCK
    rows = states.shape[1]
    per = pl.BlockSpec((8, tok, width), lambda h: (h, 0, 0))
    whole = lambda *s: pl.BlockSpec(s, lambda h: (0,) * len(s))
    sq = pltpu.VMEM((nb, 128, 128), F32)
    return pl.pallas_call(
        ssd_grad_kernel,
        grid=(heads // 8,),
        in_specs=[
            per,
            per,
            pl.BlockSpec((8, rows, 128), lambda h: (h, 0, 0)),
            whole(heads, tok),
            whole(tok, 128),
            whole(tok, 128),
        ],
        out_specs=[
            whole(tok, heads, width),
            whole(heads, tok),
            whole(tok, 128),
            whole(tok, 128),
        ],
        out_shape=[
            jax.ShapeDtypeStruct((tok, heads, width), BF),
            jax.ShapeDtypeStruct((heads, tok), F32),
            jax.ShapeDtypeStruct((tok, 128), F32),
            jax.ShapeDtypeStruct((tok, 128), F32),
        ],
        scratch_shapes=[
            sq, sq, sq, sq, sq, sq,
            sq,
            sq,
            pltpu.VMEM((heads, tok), F32),
            pltpu.VMEM((tok * heads, width), F32),
        ],
        compiler_params=pltpu.CompilerParams(vmem_limit_bytes=48 << 20),
        cost_estimate=pl.CostEstimate(
            flops=6 * 10**9, bytes_accessed=10**7, transcendentals=10**6
        ),
        name="ssd_grad",
    )(xh, yh, states, cum, b, c)


def finish_kernel(*refs):
    dqt, parts, (dq, dk, dv) = refs[:8], refs[8:16], refs[16:]
    total = functools.reduce(jnp.add, [r[...].astype(F32) for r in dqt])
    dq[...] = total.T.astype(BF)
    place = lax.axis_index("head")
    for m, r in enumerate(parts):
        h = place ^ m
        for j in range(2):
            to = pl.ds(pl.multiple_of(256 * j + 32 * h, 32), 32)
            dk[to, :] = r[32 * j : 32 * j + 32, :]
            dv[to, :] = r[64 + 32 * j : 96 + 32 * j, :]


def finish(dqt, parts):
    out = jax.ShapeDtypeStruct((512, 128), BF)
    return pl.pallas_call(
        finish_kernel,
        in_specs=[VM] * 16,
        out_specs=[VM, VM, VM],
        out_shape=[out, out, out],
        name="finish",
    )(*dqt, *parts)


def swap(v, m):
    return lax.ppermute(v, "head", [(i, i ^ m) for i in range(8)])


def turn_rows(v, m):
    return jnp.concatenate([v[j ^ m : (j ^ m) + 1] for j in range(v.shape[0])], axis=0)


def join_kernel(a, b, o):
    other = [turn_rows(b[i], 1) for i in range(3)]
    top = jnp.maximum(a[0], other[0])
    f, g = jnp.exp2(a[0] - top), jnp.exp2(other[0] - top)
    o[0] = top
    o[1] = f * a[1] + g * other[1]
    o[2] = f * a[2] + g * other[2]


def join(a, b):
    return pl.pallas_call(
        join_kernel,
        in_specs=[VM, VM],
        out_specs=VM,
        out_shape=jax.ShapeDtypeStruct(a.shape, F32),
        name="join",
    )(a, b)


def after(value, other):
    return lax.optimization_barrier((value, other))[0]


def per_device(
    ssd_input, log_decay, input_map, output_map, ssd_cotangent,
    queries, key_rows, value_rows, attn_cotangent, pair_order,
):
    tok, heads, width = ssd_input.shape
    b = input_map.reshape(tok, 128)
    c = output_map.reshape(tok, 128)
    send, xh, yh, cum, qd = ssd_send(
        ssd_input, ssd_cotangent, log_decay.T, b, c, key_rows, value_rows,
        queries.reshape(tok, 128), attn_cotangent.reshape(tok, 128),
    )
    recv = lax.all_to_all(send, "seq", 0, 0)
    qds = [qd] + [swap(qd, m) for m in range(1, 8)]
    turned = scan(recv)
    states = lax.all_to_all(turned, "seq", 0, 0)
    first = attn_stat(pair_order, after(recv, turned), qds)
    stat = join(first, swap(first, 1))
    back, *dqt = attn_grad(pair_order, recv, qds, stat, *[swap(stat, m) for m in (2, 6, 4)])
    back = after(back, states)
    dx, da, db, dc = ssd_grad(after(xh, back), yh, states, cum, b, c)
    back = lax.all_to_all(back, "seq", 0, 0)
    dqt = [dqt[0]] + [swap(dqt[m], m) for m in range(1, 8)]
    dkv = jnp.sum(after(back, da).astype(F32), axis=0).astype(BF)
    parts = [dkv] + [swap(dkv, m) for m in range(1, 8)]
    dq, dk, dv = finish(dqt, parts)
    return (
        dx,
        da.T,
        db.reshape(tok, 1, 128),
        dc.reshape(tok, 1, 128),
        dq.reshape(tok, 1, 128),
        dk,
        dv,
    )


def solution(mesh):
    tok = P("seq", "head", None)
    return jax.shard_map(
        per_device,
        mesh=mesh,
        in_specs=(
            tok, P("seq", "head"), tok, tok, tok, tok,
            P("seq", None), P("seq", None), tok, P(),
        ),
        out_specs=(tok, P("seq", "head"), tok, tok, tok, P("seq", None), P("seq", None)),
        check_vma=False,
    )
```

```python
import functools

import jax
import jax.numpy as jnp
from jax import lax
from jax.experimental import pallas as pl
from jax.experimental.pallas import tpu as pltpu
from jax.sharding import PartitionSpec as P

BLOCK = 128
BF = jnp.bfloat16
F32 = jnp.float32
HIGHEST = lax.Precision.HIGHEST
NEG = -1e30
LOG2E = 1.4426950408889634
STATE_ROWS = 256
TOTAL_ROWS = 16


def dot(a, b, ca, cb, precision=None):
    return lax.dot_general(
        a, b, (((ca,), (cb,)), ((), ())), precision=precision, preferred_element_type=F32
    )


def iota(shape, dim):
    return lax.broadcasted_iota(jnp.int32, shape, dim)


def pieces(v, count):
    out = []
    for _ in range(count):
        p = v.astype(BF)
        out.append(p)
        v = v - p.astype(F32)
    return out


def ssd_send_kernel(
    x_ref, y_ref, at_ref, b_ref, c_ref, k_ref, v_ref, q_ref, do_ref,
    send_ref, xh_ref, yh_ref, cum_ref, qd_ref, st, pu, run,
):
    k = pl.program_id(0)
    heads = x_ref.shape[1]

    @pl.when(k == 0)
    def _():
        st[...] = jnp.zeros_like(st)
        pu[...] = jnp.zeros_like(pu)
        run[...] = jnp.zeros_like(run)

    upto = (iota((BLOCK, BLOCK), 0) <= iota((BLOCK, BLOCK), 1)).astype(F32)
    cum = dot(at_ref[...], upto, 1, 0, HIGHEST)
    cum_ref[...] = cum
    total = cum[:, BLOCK - 1 :]
    grow = jnp.exp(cum)
    tail = jnp.exp(total - cum)
    keep = jnp.exp(total)
    before = run[:, :1]
    early = jnp.exp(before)
    run[...] = jnp.broadcast_to(before + total, run.shape)
    bt = b_ref[...].T
    ct = c_ref[...].T
    xt = jnp.swapaxes(x_ref[...], 0, 1)
    yt = jnp.swapaxes(y_ref[...], 0, 1)
    for h in range(heads):
        x = xt[h]
        y = yt[h]
        xh_ref[h] = x
        yh_ref[h] = y
        bs = (bt * tail[h : h + 1, :]).astype(BF)
        cs = (ct * grow[h : h + 1, :]).astype(BF)
        st[h] = keep[h : h + 1, :] * st[h] + dot(bs, x, 1, 0)
        pu[h] = pu[h] + early[h : h + 1, :] * dot(cs, y, 1, 0).astype(BF).astype(F32)

    @pl.when(k == pl.num_programs(0) - 1)
    def _():
        qd_ref[0] = q_ref[...]
        qd_ref[1] = do_ref[...]
        at = pl.multiple_of(lax.axis_index("head") * 32, 32)
        half = k_ref.shape[0] // 2
        subs = [r[pl.ds(at + o, 32), :] for r in (k_ref, v_ref) for o in (0, half)]
        three = pieces(run[...], 3)
        for h in range(heads):
            send_ref[h, 0:128, :] = st[h].astype(BF)
            send_ref[h, 128:256, :] = pu[h].astype(BF)
            for i, s in enumerate(subs):
                send_ref[h, 256 + 32 * i : 288 + 32 * i, :] = s
            rows = iota((TOTAL_ROWS, 128), 0)
            t = jnp.zeros((TOTAL_ROWS, 128), F32)
            for i, p in enumerate(three):
                t = jnp.where(rows == i, p[h : h + 1, :].astype(F32), t)
            send_ref[h, 384:400, :] = t.astype(BF)


def ssd_send(x, y, at, b, c, keys, values, q, do):
    tok, heads, width = x.shape
    nb = tok // BLOCK
    blk = pl.BlockSpec((BLOCK, heads, width), lambda k: (k, 0, 0))
    mat = pl.BlockSpec((BLOCK, 128), lambda k: (k, 0))
    row = pl.BlockSpec((heads, BLOCK), lambda k: (0, k))
    hm = pl.BlockSpec((heads, BLOCK, width), lambda k: (0, k, 0))
    whole = pl.BlockSpec((tok, 128), lambda k: (0, 0))
    rows = STATE_ROWS + 128 + TOTAL_ROWS
    return pl.pallas_call(
        ssd_send_kernel,
        grid_spec=pltpu.PrefetchScalarGridSpec(
            num_scalar_prefetch=0,
            grid=(nb,),
            in_specs=[blk, blk, row, mat, mat, whole, whole, whole, whole],
            out_specs=[
                pl.BlockSpec((heads, rows, 128), lambda k: (0, 0, 0)),
                hm,
                hm,
                row,
                pl.BlockSpec((2, tok, 128), lambda k: (0, 0, 0)),
            ],
            scratch_shapes=[
                pltpu.VMEM((heads, 128, 128), F32),
                pltpu.VMEM((heads, 128, 128), F32),
                pltpu.VMEM((heads, 128), F32),
            ],
        ),
        out_shape=[
            jax.ShapeDtypeStruct((heads, rows, 128), BF),
            jax.ShapeDtypeStruct((heads, tok, width), BF),
            jax.ShapeDtypeStruct((heads, tok, width), BF),
            jax.ShapeDtypeStruct((heads, tok), F32),
            jax.ShapeDtypeStruct((2, tok, 128), BF),
        ],
        compiler_params=pltpu.CompilerParams(vmem_limit_bytes=60 << 20),
        cost_estimate=pl.CostEstimate(
            flops=3 * 10**9, bytes_accessed=10**7, transcendentals=10**5
        ),
        name="ssd_send",
    )(x, y, at, b, c, keys, values, q, do)


VM = pl.BlockSpec(memory_space=pltpu.VMEM)
SM = pl.BlockSpec(memory_space=pltpu.SMEM)
HB = pl.BlockSpec(memory_space=pltpu.HBM)


def scan_kernel(recv, back):
    n = recv.shape[0]
    state = jnp.zeros((128, 128), F32)
    for e in range(n):
        back[e, 0:128, :] = state.astype(BF)
        if e < n - 1:
            t = recv[e, 384:400, :].astype(F32)
            keep = jnp.exp(t[0:1] + t[1:2] + t[2:3])
            state = keep * state + recv[e, 0:128, :].astype(F32)
    pull = jnp.zeros((128, 128), F32)
    for e in reversed(range(n)):
        back[e, 128:256, :] = pull.astype(BF)
        if e > 0:
            t = recv[e, 384:400, :].astype(F32)
            keep = jnp.exp(t[0:1] + t[1:2] + t[2:3])
            pull = keep * pull + recv[e, 128:256, :].astype(F32)


def scan(recv):
    n = recv.shape[0]
    return pl.pallas_call(
        scan_kernel,
        in_specs=[VM],
        out_specs=VM,
        out_shape=jax.ShapeDtypeStruct((n, 256, 128), BF),
        compiler_params=pltpu.CompilerParams(vmem_limit_bytes=20 << 20),
        name="scan",
    )(recv)


def sort_keys(order, inverse, recv, ks, vs):
    for e in range(16):
        inverse[order[e]] = e
    for b in range(32):
        src = inverse[b if b < 16 else 31 - b]
        o = 0 if b < 16 else 32
        ks[32 * b : 32 * b + 32, :] = recv[src, 256 + o : 288 + o, :]
        vs[32 * b : 32 * b + 32, :] = recv[src, 320 + o : 352 + o, :]


def item_at(order, size, i):
    first = order[lax.axis_index("seq")]
    per = size // 32
    n0 = (first + per) // per
    late = (i >= n0).astype(jnp.int32)
    g = i - late * n0
    block = jnp.where(late == 1, 31 - first, first)
    kr = iota((size, 256), 0)
    key_at = (g * per + kr // 32) * 256 + lax.axis_index("head") * 32 + kr % 32
    bias = jnp.where(key_at <= block * 256 + iota((size, 256), 1), 0.0, NEG)
    return pl.multiple_of(g * size, size), pl.multiple_of(late * 256, 256), bias


def attn_stat_kernel(order, recv, *refs):
    qd, (stat, mate, ks, vs, inverse) = refs[:8], refs[8:]
    heads = len(qd)
    scale = LOG2E * 128**-0.5
    sort_keys(order, inverse, recv, ks, vs)
    stat[0] = jnp.full((heads, 512), NEG, F32)
    stat[1:] = jnp.zeros((2, heads, 512), F32)

    def item(i, carry):
        kat, rat, bias = item_at(order, 256, i)
        kg = ks[pl.ds(kat, 256), :]
        vg = vs[pl.ds(kat, 256), :]
        for h in range(heads):
            s = dot(kg, qd[h][0, pl.ds(rat, 256), :], 1, 1) * scale + bias
            dp = dot(vg, qd[h][1, pl.ds(rat, 256), :], 1, 1)
            at = (slice(h, h + 1), pl.ds(rat, 256))
            old = stat[0, *at]
            top = jnp.maximum(old, jnp.max(s, axis=0, keepdims=True))
            p = jnp.exp2(s - top)
            fix = jnp.exp2(old - top)
            stat[0, *at] = top
            stat[1, *at] = fix * stat[1, *at] + jnp.sum(p, axis=0, keepdims=True)
            stat[2, *at] = fix * stat[2, *at] + jnp.sum(p * dp, axis=0, keepdims=True)
        return carry

    lax.fori_loop(0, 5, item, 0)
    for i in range(3):
        mate[i] = turn_rows(stat[i], 1)


def attn_stat(order, recv, qd):
    heads = len(qd)
    return pl.pallas_call(
        attn_stat_kernel,
        in_specs=[SM] + [VM] * 9,
        out_specs=[VM, VM],
        out_shape=[jax.ShapeDtypeStruct((3, heads, 512), F32)] * 2,
        scratch_shapes=[
            pltpu.VMEM((1024, 128), BF),
            pltpu.VMEM((1024, 128), BF),
            pltpu.SMEM((16,), jnp.int32),
        ],
        compiler_params=pltpu.CompilerParams(vmem_limit_bytes=20 << 20),
        cost_estimate=pl.CostEstimate(
            flops=4 * 10**9, bytes_accessed=5 * 10**6, transcendentals=10**6
        ),
        name="attn_stat",
    )(order, recv, *qd)


def attn_grad_kernel(order, recv, *refs):
    qd, stats, send, dqt = refs[:8], refs[8:12], refs[12], refs[13:21]
    ks, vs, dk, dv, lse, delta, dqs, inverse, dqo, buf, sem = refs[21:]
    heads = len(qd)
    scale = 128**-0.5
    sort_keys(order, inverse, recv, ks, vs)
    tables = [[r[i] for i in range(3)] for r in stats]
    for m, v in zip((2, 6, 4), tables[1:]):
        v[:] = [turn_rows(x, m) for x in v]
    top = functools.reduce(jnp.maximum, [v[0] for v in tables])
    total = jnp.zeros_like(top)
    dsum = jnp.zeros_like(top)
    for v in tables:
        f = jnp.exp2(v[0] - top)
        total = total + f * v[1]
        dsum = dsum + f * v[2]
    lse[...] = top + jnp.log2(total)
    delta[...] = dsum / total
    dk[...] = jnp.zeros_like(dk)
    dv[...] = jnp.zeros_like(dv)
    dqs[...] = jnp.zeros_like(dqs)

    def item(i, carry):
        kat, rat, bias = item_at(order, 512, i)
        kg = ks[pl.ds(kat, 512), :]
        vg = vs[pl.ds(kat, 512), :]
        kt = kg.astype(F32).T.astype(BF)
        dkg = dk[pl.ds(kat, 512), :]
        dvg = dv[pl.ds(kat, 512), :]
        for h in range(heads):
            q = qd[h][0, pl.ds(rat, 256), :]
            do = qd[h][1, pl.ds(rat, 256), :]
            s = dot(kg, q, 1, 1) * (scale * LOG2E) + bias
            dp = dot(vg, do, 1, 1)
            p = jnp.exp2(s - lse[h : h + 1, pl.ds(rat, 256)])
            ds = (p * (dp - delta[h : h + 1, pl.ds(rat, 256)])).astype(BF)
            dvg = dvg + dot(p.astype(BF), do, 1, 0)
            dkg = dkg + dot(ds, q, 1, 0)
            dqs[h, :, pl.ds(rat, 256)] += dot(kt, ds, 1, 0)
        dk[pl.ds(kat, 512), :] = dkg
        dv[pl.ds(kat, 512), :] = dvg
        return carry

    lax.fori_loop(0, 3, item, 0)
    dqo[...] = (dqs[...] * scale).astype(BF)
    moves = [pltpu.make_async_copy(dqo.at[h], dqt[h], sem.at[h]) for h in range(heads)]
    for m in moves:
        m.start()
    for e in range(16):
        b = order[e]
        for j, (r, f) in enumerate(((dk, scale), (dv, 1.0))):
            lo = r[pl.ds(pl.multiple_of(b * 32, 32), 32), :]
            hi = r[pl.ds(pl.multiple_of((31 - b) * 32, 32), 32), :]
            buf[e, 64 * j : 32 + 64 * j, :] = (lo * f).astype(BF)
            buf[e, 32 + 64 * j : 64 + 64 * j, :] = (hi * f).astype(BF)
    moves.append(pltpu.make_async_copy(buf, send, sem.at[heads]))
    moves[-1].start()
    for m in moves:
        m.wait()


def attn_grad(order, recv, qd, *stats):
    heads = len(qd)
    n = recv.shape[0]
    return pl.pallas_call(
        attn_grad_kernel,
        in_specs=[SM] + [VM] * 13,
        out_specs=[HB] * 9,
        out_shape=[pltpu.HBM((n, 128, 128), BF)] + [pltpu.HBM((128, 512), BF)] * 8,
        scratch_shapes=[
            pltpu.VMEM((1024, 128), BF),
            pltpu.VMEM((1024, 128), BF),
            pltpu.VMEM((1024, 128), F32),
            pltpu.VMEM((1024, 128), F32),
            pltpu.VMEM((heads, 512), F32),
            pltpu.VMEM((heads, 512), F32),
            pltpu.VMEM((heads, 128, 512), F32),
            pltpu.SMEM((16,), jnp.int32),
            pltpu.VMEM((heads, 128, 512), BF),
            pltpu.VMEM((n, 128, 128), BF),
            pltpu.SemaphoreType.DMA((heads + 1,)),
        ],
        compiler_params=pltpu.CompilerParams(vmem_limit_bytes=20 << 20),
        cost_estimate=pl.CostEstimate(
            flops=8 * 10**9, bytes_accessed=6 * 10**6, transcendentals=10**6
        ),
        name="attn_grad",
    )(order, recv, *qd, *stats)


def ssd_grad_kernel(
    xh, yh, states, cum, b_ref, c_ref,
    dx_ref, da_ref, db_ref, dc_ref,
    g_s, dg_s, dct, dbt, bt_s, ct_s, colp, dcol, drow, dxs,
):
    base = pl.program_id(0) * 8
    heads = pl.num_programs(0) * 8
    nb = xh.shape[1] // BLOCK
    rows = iota((BLOCK, BLOCK), 0)
    lanes = iota((BLOCK, BLOCK), 1)

    @pl.when(base == 0)
    def _():
        dg_s[...] = jnp.zeros_like(dg_s)
        dct[...] = jnp.zeros_like(dct)
        dbt[...] = jnp.zeros_like(dbt)
        dcol[...] = jnp.zeros_like(dcol)
        drow[...] = jnp.zeros_like(drow)
        for k in range(nb):
            sl = slice(k * BLOCK, (k + 1) * BLOCK)
            b = b_ref[sl, :]
            c = c_ref[sl, :]
            g_s[k] = jnp.where(rows <= lanes, dot(b, c, 1, 1, HIGHEST), 0.0)
            bt_s[k] = b.T
            ct_s[k] = c.T
            cm = cum[:, sl]
            tl = jnp.exp(cm[:, BLOCK - 1 :] - cm)
            gap = jnp.zeros((BLOCK // 2 - heads_of(cum), BLOCK), F32)
            colp[k] = jnp.concatenate([cm, gap, tl, gap], axis=0).T

    nh = heads_of(cum)
    turned = [pltpu.roll(colp[k], lax.rem(BLOCK - base, BLOCK), 1) for k in range(nb)]
    for hh in range(8):
        h = base + hh
        crow = cum[pl.ds(h, 1), :]
        x = [xh[hh, k * BLOCK : (k + 1) * BLOCK, :] for k in range(nb)]
        y = [yh[hh, k * BLOCK : (k + 1) * BLOCK, :] for k in range(nb)]
        c = [crow[:, k * BLOCK : (k + 1) * BLOCK] for k in range(nb)]
        total = [v[:, BLOCK - 1 :] for v in c]
        keep = [jnp.exp(t) for t in total]
        tail = [jnp.exp(t - v) for t, v in zip(total, c)]
        grow = [jnp.exp(v) for v in c]
        state = [states[hh, 0:128, :].astype(F32)]
        for k in range(nb - 1):
            bs = (bt_s[k] * tail[k]).astype(BF)
            state.append(keep[k] * state[k] + dot(bs, x[k], 1, 0))
        pull = states[hh, 128:256, :].astype(F32)
        for k in reversed(range(nb)):
            decay = jnp.exp(jnp.minimum(c[k] - turned[k][:, hh : hh + 1], 0.0))
            w = g_s[k] * decay
            sb = state[k].astype(BF)
            xy = dot(jnp.concatenate([x[k], sb], axis=0), y[k], 1, 1)
            dw = xy[:BLOCK]
            t = dw * decay
            dg_s[k] += t
            z = t * g_s[k]
            pb = pull.astype(BF)
            bs = (b_ref[k * BLOCK : (k + 1) * BLOCK, :] * turned[k][:, 64 + hh : 65 + hh]).astype(BF)
            cs = (ct_s[k] * grow[k]).astype(BF)
            wy = dot(jnp.concatenate([w.astype(BF), cs], axis=0), y[k], 1, 0)
            dx = wy[:BLOCK] + dot(bs, pb, 1, 0)
            dxs[pl.ds(k * BLOCK * heads + h, BLOCK, stride=nh), :] = dx
            dcs = xy[BLOCK:] * grow[k]
            dct[k] += dcs
            q = dcs * ct_s[k]
            dbs = dot(pb, x[k], 1, 1) * tail[k]
            dbt[k] += dbs
            v = dbs * bt_s[k]
            vs = jnp.sum(v, axis=0, keepdims=True)
            line = jnp.sum(z + q, axis=0, keepdims=True) - vs
            cross = keep[k] * jnp.sum(state[k] * pull, axis=0, keepdims=True)
            last = jnp.sum(vs + cross, axis=1, keepdims=True)
            line = jnp.where(iota((1, BLOCK), 1) == BLOCK - 1, line + last, line)
            at = slice(k * BLOCK, (k + 1) * BLOCK)
            drow[:, at] = jnp.where(iota((nh, BLOCK), 0) == h, line, drow[:, at])
            zc = jnp.sum(z, axis=1, keepdims=True)
            dcol[k] = jnp.where(lanes == h, zc, dcol[k])
            if k > 0:
                pull = keep[k] * pull + wy[BLOCK:].astype(BF).astype(F32)

    @pl.when(base == heads - 8)
    def _():
        late = (rows >= lanes).astype(F32)
        for k in range(nb):
            sl = slice(k * BLOCK, (k + 1) * BLOCK)
            dg = jnp.where(rows <= lanes, dg_s[k], 0.0)
            db_ref[sl, :] = dbt[k].T + dot(dg, c_ref[sl, :], 1, 0, HIGHEST)
            dc_ref[sl, :] = dct[k].T + dot(dg.T, b_ref[sl, :], 1, 0, HIGHEST)
            da_ref[:, sl] = dot(drow[:, sl] - dcol[k].T[:nh], late, 1, 0, HIGHEST)
            dx_ref[sl] = (
                dxs[k * BLOCK * nh : (k + 1) * BLOCK * nh, :]
                .reshape(BLOCK, nh, 128)
                .astype(BF)
            )


def heads_of(cum):
    return cum.shape[0]


def ssd_grad(xh, yh, states, cum, b, c):
    heads, tok, width = xh.shape
    nb = tok // BLOCK
    rows = states.shape[1]
    per = pl.BlockSpec((8, tok, width), lambda h: (h, 0, 0))
    whole = lambda *s: pl.BlockSpec(s, lambda h: (0,) * len(s))
    sq = pltpu.VMEM((nb, 128, 128), F32)
    return pl.pallas_call(
        ssd_grad_kernel,
        grid=(heads // 8,),
        in_specs=[
            per,
            per,
            pl.BlockSpec((8, rows, 128), lambda h: (h, 0, 0)),
            whole(heads, tok),
            whole(tok, 128),
            whole(tok, 128),
        ],
        out_specs=[
            whole(tok, heads, width),
            whole(heads, tok),
            whole(tok, 128),
            whole(tok, 128),
        ],
        out_shape=[
            jax.ShapeDtypeStruct((tok, heads, width), BF),
            jax.ShapeDtypeStruct((heads, tok), F32),
            jax.ShapeDtypeStruct((tok, 128), F32),
            jax.ShapeDtypeStruct((tok, 128), F32),
        ],
        scratch_shapes=[
            sq, sq, sq, sq, sq, sq,
            sq,
            sq,
            pltpu.VMEM((heads, tok), F32),
            pltpu.VMEM((tok * heads, width), F32),
        ],
        compiler_params=pltpu.CompilerParams(vmem_limit_bytes=60 << 20),
        cost_estimate=pl.CostEstimate(
            flops=6 * 10**9, bytes_accessed=10**7, transcendentals=10**6
        ),
        name="ssd_grad",
    )(xh, yh, states, cum, b, c)


def finish_kernel(*refs):
    dqt, parts, (dq, dk, dv) = refs[:4], refs[4:12], refs[12:]
    total = functools.reduce(jnp.add, [r[...].astype(F32) for r in dqt])
    dq[...] = total.T.astype(BF)
    place = lax.axis_index("head")
    for m, r in enumerate(parts):
        h = place ^ m
        for j in range(2):
            to = pl.ds(pl.multiple_of(256 * j + 32 * h, 32), 32)
            dk[to, :] = r[32 * j : 32 * j + 32, :]
            dv[to, :] = r[64 + 32 * j : 96 + 32 * j, :]


def finish(dqt, parts):
    out = jax.ShapeDtypeStruct((512, 128), BF)
    return pl.pallas_call(
        finish_kernel,
        in_specs=[VM] * 12,
        out_specs=[VM, VM, VM],
        out_shape=[out, out, out],
        compiler_params=pltpu.CompilerParams(vmem_limit_bytes=16 << 20),
        name="finish",
    )(*dqt, *parts)


def swap(v, m):
    return lax.ppermute(v, "head", [(i, i ^ m) for i in range(8)])


def turn_rows(v, m):
    return jnp.concatenate([v[j ^ m : (j ^ m) + 1] for j in range(v.shape[0])], axis=0)


def join(a, b):
    top = jnp.maximum(a[0], b[0])
    f, g = jnp.exp2(a[0] - top), jnp.exp2(b[0] - top)
    return jnp.stack([top, f * a[1] + g * b[1], f * a[2] + g * b[2]])


def gather_heads(v):
    out = [v] + [None] * 7
    for m in (2, 6, 4):
        out[m] = swap(v, m)
    for m in (0, 2, 6, 4):
        out[m + 1] = swap(out[m], 1)
    return out


def pair_sums(parts):
    return [
        (parts[m].astype(F32) + swap(parts[m + 1], 1).astype(F32)).astype(BF)
        for m in (0, 2, 4, 6)
    ]


def after(value, other):
    return lax.optimization_barrier((value, other))[0]


def per_device(
    ssd_input, log_decay, input_map, output_map, ssd_cotangent,
    queries, key_rows, value_rows, attn_cotangent, pair_order,
):
    tok, heads, width = ssd_input.shape
    b = input_map.reshape(tok, 128)
    c = output_map.reshape(tok, 128)
    send, xh, yh, cum, qd = ssd_send(
        ssd_input, ssd_cotangent, log_decay.T, b, c, key_rows, value_rows,
        queries.reshape(tok, 128), attn_cotangent.reshape(tok, 128),
    )
    recv = lax.all_to_all(send, "seq", 0, 0)
    qds = gather_heads(qd)
    turned = scan(recv)
    states = lax.all_to_all(turned, "seq", 0, 0)
    first, mate = attn_stat(pair_order, after(recv, turned), qds)
    stat = join(first, swap(mate, 1))
    rest = [swap(stat, m) for m in (2, 6, 4)]
    back, *dqt = attn_grad(pair_order, after(recv, states), qds, stat, *rest)
    pair = pair_sums(dqt)
    dx, da, db, dc = ssd_grad(after(xh, (back, *pair)), yh, states, cum, b, c)
    back = lax.all_to_all(back, "seq", 0, 0)
    dqt = [pair[0]] + [swap(pair[i], m) for i, m in ((1, 2), (3, 6), (2, 4))]
    dkv = jnp.sum(after(back, da).astype(F32), axis=0).astype(BF)
    parts = gather_heads(dkv)
    dq, dk, dv = finish(dqt, parts)
    return (
        dx,
        da.T,
        db.reshape(tok, 1, 128),
        dc.reshape(tok, 1, 128),
        dq.reshape(tok, 1, 128),
        dk,
        dv,
    )


def solution(mesh):
    tok = P("seq", "head", None)
    return jax.shard_map(
        per_device,
        mesh=mesh,
        in_specs=(
            tok, P("seq", "head"), tok, tok, tok, tok,
            P("seq", None), P("seq", None), tok, P(),
        ),
        out_specs=(tok, P("seq", "head"), tok, tok, tok, P("seq", None), P("seq", None)),
        check_vma=False,
    )
```

```python
import functools

import jax
import jax.numpy as jnp
from jax import lax
from jax.experimental import pallas as pl
from jax.experimental.pallas import tpu as pltpu
from jax.sharding import PartitionSpec as P

BLOCK = 128
BF = jnp.bfloat16
F32 = jnp.float32
HIGHEST = lax.Precision.HIGHEST
NEG = -1e30
LOG2E = 1.4426950408889634
STATE_ROWS = 256
TOTAL_ROWS = 16


def dot(a, b, ca, cb, precision=None):
    return lax.dot_general(
        a, b, (((ca,), (cb,)), ((), ())), precision=precision, preferred_element_type=F32
    )


def iota(shape, dim):
    return lax.broadcasted_iota(jnp.int32, shape, dim)


def pieces(v, count):
    out = []
    for _ in range(count):
        p = v.astype(BF)
        out.append(p)
        v = v - p.astype(F32)
    return out


def ssd_send_kernel(
    x_ref, y_ref, at_ref, b_ref, c_ref, k_ref, v_ref, q_ref, do_ref,
    send_ref, xh_ref, yh_ref, cum_ref, qd_ref, st, pu, run,
):
    k = pl.program_id(0)
    heads = x_ref.shape[1]

    @pl.when(k == 0)
    def _():
        st[...] = jnp.zeros_like(st)
        pu[...] = jnp.zeros_like(pu)
        run[...] = jnp.zeros_like(run)

    upto = (iota((BLOCK, BLOCK), 0) <= iota((BLOCK, BLOCK), 1)).astype(F32)
    cum = dot(at_ref[...], upto, 1, 0, HIGHEST)
    cum_ref[...] = cum
    total = cum[:, BLOCK - 1 :]
    grow = jnp.exp(cum)
    tail = jnp.exp(total - cum)
    keep = jnp.exp(total)
    before = run[:, :1]
    early = jnp.exp(before)
    run[...] = jnp.broadcast_to(before + total, run.shape)
    bt = b_ref[...].T
    ct = c_ref[...].T
    xt = jnp.swapaxes(x_ref[...], 0, 1)
    yt = jnp.swapaxes(y_ref[...], 0, 1)
    for h in range(heads):
        x = xt[h]
        y = yt[h]
        xh_ref[h] = x
        yh_ref[h] = y
        bs = (bt * tail[h : h + 1, :]).astype(BF)
        cs = (ct * grow[h : h + 1, :]).astype(BF)
        st[h] = keep[h : h + 1, :] * st[h] + dot(bs, x, 1, 0)
        pu[h] = pu[h] + early[h : h + 1, :] * dot(cs, y, 1, 0).astype(BF).astype(F32)

    @pl.when(k == pl.num_programs(0) - 1)
    def _():
        qd_ref[0] = q_ref[...]
        qd_ref[1] = do_ref[...]
        at = pl.multiple_of(lax.axis_index("head") * 32, 32)
        half = k_ref.shape[0] // 2
        subs = [r[pl.ds(at + o, 32), :] for r in (k_ref, v_ref) for o in (0, half)]
        three = pieces(run[...], 3)
        for h in range(heads):
            send_ref[h, 0:128, :] = st[h].astype(BF)
            send_ref[h, 128:256, :] = pu[h].astype(BF)
            for i, s in enumerate(subs):
                send_ref[h, 256 + 32 * i : 288 + 32 * i, :] = s
            rows = iota((TOTAL_ROWS, 128), 0)
            t = jnp.zeros((TOTAL_ROWS, 128), F32)
            for i, p in enumerate(three):
                t = jnp.where(rows == i, p[h : h + 1, :].astype(F32), t)
            send_ref[h, 384:400, :] = t.astype(BF)


def ssd_send(x, y, at, b, c, keys, values, q, do):
    tok, heads, width = x.shape
    nb = tok // BLOCK
    blk = pl.BlockSpec((BLOCK, heads, width), lambda k: (k, 0, 0))
    mat = pl.BlockSpec((BLOCK, 128), lambda k: (k, 0))
    row = pl.BlockSpec((heads, BLOCK), lambda k: (0, k))
    hm = pl.BlockSpec((heads, BLOCK, width), lambda k: (0, k, 0))
    whole = pl.BlockSpec((tok, 128), lambda k: (0, 0))
    rows = STATE_ROWS + 128 + TOTAL_ROWS
    return pl.pallas_call(
        ssd_send_kernel,
        grid_spec=pltpu.PrefetchScalarGridSpec(
            num_scalar_prefetch=0,
            grid=(nb,),
            in_specs=[blk, blk, row, mat, mat, whole, whole, whole, whole],
            out_specs=[
                pl.BlockSpec((heads, rows, 128), lambda k: (0, 0, 0)),
                hm,
                hm,
                row,
                pl.BlockSpec((2, tok, 128), lambda k: (0, 0, 0)),
            ],
            scratch_shapes=[
                pltpu.VMEM((heads, 128, 128), F32),
                pltpu.VMEM((heads, 128, 128), F32),
                pltpu.VMEM((heads, 128), F32),
            ],
        ),
        out_shape=[
            jax.ShapeDtypeStruct((heads, rows, 128), BF),
            jax.ShapeDtypeStruct((heads, tok, width), BF),
            jax.ShapeDtypeStruct((heads, tok, width), BF),
            jax.ShapeDtypeStruct((heads, tok), F32),
            jax.ShapeDtypeStruct((2, tok, 128), BF),
        ],
        compiler_params=pltpu.CompilerParams(vmem_limit_bytes=60 << 20),
        cost_estimate=pl.CostEstimate(
            flops=3 * 10**9, bytes_accessed=10**7, transcendentals=10**5
        ),
        name="ssd_send",
    )(x, y, at, b, c, keys, values, q, do)


VM = pl.BlockSpec(memory_space=pltpu.VMEM)
SM = pl.BlockSpec(memory_space=pltpu.SMEM)
HB = pl.BlockSpec(memory_space=pltpu.HBM)


def scan_kernel(recv, back):
    n = recv.shape[0]
    state = jnp.zeros((128, 128), F32)
    for e in range(n):
        back[e, 0:128, :] = state.astype(BF)
        if e < n - 1:
            t = recv[e, 384:400, :].astype(F32)
            keep = jnp.exp(t[0:1] + t[1:2] + t[2:3])
            state = keep * state + recv[e, 0:128, :].astype(F32)
    pull = jnp.zeros((128, 128), F32)
    for e in reversed(range(n)):
        back[e, 128:256, :] = pull.astype(BF)
        if e > 0:
            t = recv[e, 384:400, :].astype(F32)
            keep = jnp.exp(t[0:1] + t[1:2] + t[2:3])
            pull = keep * pull + recv[e, 128:256, :].astype(F32)


def scan(recv):
    n = recv.shape[0]
    return pl.pallas_call(
        scan_kernel,
        in_specs=[VM],
        out_specs=VM,
        out_shape=jax.ShapeDtypeStruct((n, 256, 128), BF),
        compiler_params=pltpu.CompilerParams(vmem_limit_bytes=20 << 20),
        name="scan",
    )(recv)


def sort_keys(order, inverse, recv, ks, vs):
    for e in range(16):
        inverse[order[e]] = e
    for b in range(32):
        src = inverse[b if b < 16 else 31 - b]
        o = 0 if b < 16 else 32
        ks[32 * b : 32 * b + 32, :] = recv[src, 256 + o : 288 + o, :]
        vs[32 * b : 32 * b + 32, :] = recv[src, 320 + o : 352 + o, :]


def item_at(order, size, i):
    first = order[lax.axis_index("seq")]
    per = size // 32
    n0 = (first + per) // per
    late = (i >= n0).astype(jnp.int32)
    g = i - late * n0
    block = jnp.where(late == 1, 31 - first, first)
    kr = iota((size, 256), 0)
    key_at = (g * per + kr // 32) * 256 + lax.axis_index("head") * 32 + kr % 32
    bias = jnp.where(key_at <= block * 256 + iota((size, 256), 1), 0.0, NEG)
    return pl.multiple_of(g * size, size), pl.multiple_of(late * 256, 256), bias


def attn_stat_kernel(order, recv, *refs):
    qd, (stat, mate, ks, vs, inverse) = refs[:8], refs[8:]
    heads = len(qd)
    scale = LOG2E * 128**-0.5
    sort_keys(order, inverse, recv, ks, vs)
    stat[0] = jnp.full((heads, 512), NEG, F32)
    stat[1:] = jnp.zeros((2, heads, 512), F32)

    def item(i, carry):
        kat, rat, bias = item_at(order, 256, i)
        kg = ks[pl.ds(kat, 256), :]
        vg = vs[pl.ds(kat, 256), :]
        for h in range(heads):
            s = dot(kg, qd[h][0, pl.ds(rat, 256), :], 1, 1) * scale + bias
            dp = dot(vg, qd[h][1, pl.ds(rat, 256), :], 1, 1)
            at = (slice(h, h + 1), pl.ds(rat, 256))
            old = stat[0, *at]
            top = jnp.maximum(old, jnp.max(s, axis=0, keepdims=True))
            p = jnp.exp2(s - top)
            fix = jnp.exp2(old - top)
            stat[0, *at] = top
            stat[1, *at] = fix * stat[1, *at] + jnp.sum(p, axis=0, keepdims=True)
            stat[2, *at] = fix * stat[2, *at] + jnp.sum(p * dp, axis=0, keepdims=True)
        return carry

    lax.fori_loop(0, 5, item, 0)
    for i in range(3):
        mate[i] = turn_rows(stat[i], 1)


def attn_stat(order, recv, qd):
    heads = len(qd)
    return pl.pallas_call(
        attn_stat_kernel,
        in_specs=[SM] + [VM] * 9,
        out_specs=[VM, VM],
        out_shape=[jax.ShapeDtypeStruct((3, heads, 512), F32)] * 2,
        scratch_shapes=[
            pltpu.VMEM((1024, 128), BF),
            pltpu.VMEM((1024, 128), BF),
            pltpu.SMEM((16,), jnp.int32),
        ],
        compiler_params=pltpu.CompilerParams(vmem_limit_bytes=20 << 20),
        cost_estimate=pl.CostEstimate(
            flops=4 * 10**9, bytes_accessed=5 * 10**6, transcendentals=10**6
        ),
        name="attn_stat",
    )(order, recv, *qd)


def attn_grad_kernel(order, recv, *refs):
    qd, stats, send, dqt = refs[:8], refs[8:12], refs[12], refs[13:21]
    ks, vs, dk, dv, lse, delta, dqs, inverse, dqo, buf, sem = refs[21:]
    heads = len(qd)
    scale = 128**-0.5
    sort_keys(order, inverse, recv, ks, vs)
    tables = [[r[i] for i in range(3)] for r in stats]
    for m, v in zip((2, 6, 4), tables[1:]):
        v[:] = [turn_rows(x, m) for x in v]
    top = functools.reduce(jnp.maximum, [v[0] for v in tables])
    total = jnp.zeros_like(top)
    dsum = jnp.zeros_like(top)
    for v in tables:
        f = jnp.exp2(v[0] - top)
        total = total + f * v[1]
        dsum = dsum + f * v[2]
    lse[...] = top + jnp.log2(total)
    delta[...] = dsum / total
    dk[...] = jnp.zeros_like(dk)
    dv[...] = jnp.zeros_like(dv)
    dqs[...] = jnp.zeros_like(dqs)

    def item(i, carry):
        kat, rat, bias = item_at(order, 512, i)
        kg = ks[pl.ds(kat, 512), :]
        vg = vs[pl.ds(kat, 512), :]
        kt = kg.astype(F32).T.astype(BF)
        dkg = dk[pl.ds(kat, 512), :]
        dvg = dv[pl.ds(kat, 512), :]
        for h in range(heads):
            q = qd[h][0, pl.ds(rat, 256), :]
            do = qd[h][1, pl.ds(rat, 256), :]
            s = dot(kg, q, 1, 1) * (scale * LOG2E) + bias
            dp = dot(vg, do, 1, 1)
            p = jnp.exp2(s - lse[h : h + 1, pl.ds(rat, 256)])
            ds = (p * (dp - delta[h : h + 1, pl.ds(rat, 256)])).astype(BF)
            dvg = dvg + dot(p.astype(BF), do, 1, 0)
            dkg = dkg + dot(ds, q, 1, 0)
            dqs[h, :, pl.ds(rat, 256)] += dot(kt, ds, 1, 0)
        dk[pl.ds(kat, 512), :] = dkg
        dv[pl.ds(kat, 512), :] = dvg
        return carry

    lax.fori_loop(0, 3, item, 0)
    dqo[...] = (dqs[...] * scale).astype(BF)
    moves = [pltpu.make_async_copy(dqo.at[h], dqt[h], sem.at[h]) for h in range(heads)]
    for m in moves:
        m.start()
    for e in range(16):
        b = order[e]
        for j, (r, f) in enumerate(((dk, scale), (dv, 1.0))):
            lo = r[pl.ds(pl.multiple_of(b * 32, 32), 32), :]
            hi = r[pl.ds(pl.multiple_of((31 - b) * 32, 32), 32), :]
            buf[e, 64 * j : 32 + 64 * j, :] = (lo * f).astype(BF)
            buf[e, 32 + 64 * j : 64 + 64 * j, :] = (hi * f).astype(BF)
    moves.append(pltpu.make_async_copy(buf, send, sem.at[heads]))
    moves[-1].start()
    for m in moves:
        m.wait()


def attn_grad(order, recv, qd, *stats):
    heads = len(qd)
    n = recv.shape[0]
    return pl.pallas_call(
        attn_grad_kernel,
        in_specs=[SM] + [VM] * 13,
        out_specs=[HB] * 9,
        out_shape=[pltpu.HBM((n, 128, 128), BF)] + [pltpu.HBM((128, 512), BF)] * 8,
        scratch_shapes=[
            pltpu.VMEM((1024, 128), BF),
            pltpu.VMEM((1024, 128), BF),
            pltpu.VMEM((1024, 128), F32),
            pltpu.VMEM((1024, 128), F32),
            pltpu.VMEM((heads, 512), F32),
            pltpu.VMEM((heads, 512), F32),
            pltpu.VMEM((heads, 128, 512), F32),
            pltpu.SMEM((16,), jnp.int32),
            pltpu.VMEM((heads, 128, 512), BF),
            pltpu.VMEM((n, 128, 128), BF),
            pltpu.SemaphoreType.DMA((heads + 1,)),
        ],
        compiler_params=pltpu.CompilerParams(vmem_limit_bytes=20 << 20),
        cost_estimate=pl.CostEstimate(
            flops=8 * 10**9, bytes_accessed=6 * 10**6, transcendentals=10**6
        ),
        name="attn_grad",
    )(order, recv, *qd, *stats)


STEP_HEADS = 4


def turned_columns(cum, k, table):
    cm = cum[:, k * BLOCK : (k + 1) * BLOCK]
    tl = jnp.exp(cm[:, BLOCK - 1 :] - cm)
    gap = jnp.zeros((BLOCK // 2 - cm.shape[0], BLOCK), F32)
    table[k] = jnp.concatenate([cm, gap, tl, gap], axis=0).T


def head_vectors(cum, h, nb):
    row = cum[pl.ds(h, 1), :]
    c = [row[:, k * BLOCK : (k + 1) * BLOCK] for k in range(nb)]
    total = [v[:, BLOCK - 1 :] for v in c]
    keep = [jnp.exp(t) for t in total]
    tail = [jnp.exp(t - v) for t, v in zip(total, c)]
    grow = [jnp.exp(v) for v in c]
    return c, keep, tail, grow


def ssd_local_kernel(
    xh, yh, cum, b_ref, c_ref,
    dxl, fp, line_ref, db_ref, dc_ref,
    g_s, dg_s, bt_s, ct_s, colp, dcol, drow,
):
    base = pl.program_id(0) * STEP_HEADS
    nh = cum.shape[0]
    nb = xh.shape[1] // BLOCK
    rows = iota((BLOCK, BLOCK), 0)
    lanes = iota((BLOCK, BLOCK), 1)

    @pl.when(base == 0)
    def _():
        dg_s[...] = jnp.zeros_like(dg_s)
        dcol[...] = jnp.zeros_like(dcol)
        drow[...] = jnp.zeros_like(drow)
        for k in range(nb):
            sl = slice(k * BLOCK, (k + 1) * BLOCK)
            b = b_ref[sl, :]
            c = c_ref[sl, :]
            g_s[k] = jnp.where(rows <= lanes, dot(b, c, 1, 1, HIGHEST), 0.0)
            bt_s[k] = b.T
            ct_s[k] = c.T
            turned_columns(cum, k, colp)

    turned = [pltpu.roll(colp[k], lax.rem(BLOCK - base, BLOCK), 1) for k in range(nb)]
    for hh in range(STEP_HEADS):
        h = base + hh
        c, keep, tail, grow = head_vectors(cum, h, nb)
        for k in range(nb):
            at = slice(k * BLOCK, (k + 1) * BLOCK)
            x = xh[hh, at, :]
            y = yh[hh, at, :]
            decay = jnp.exp(jnp.minimum(c[k] - turned[k][:, hh : hh + 1], 0.0))
            w = g_s[k] * decay
            t = dot(x, y, 1, 1) * decay
            dg_s[k] += t
            z = t * g_s[k]
            cs = (ct_s[k] * grow[k]).astype(BF)
            wy = dot(jnp.concatenate([w.astype(BF), cs], axis=0), y, 1, 0)
            dxl[hh, at, :] = wy[:BLOCK].astype(BF)
            if k > 0:
                fp[hh, nb - 2 + k] = wy[BLOCK:].astype(BF)
            if k < nb - 1:
                fp[hh, k] = dot((bt_s[k] * tail[k]).astype(BF), x, 1, 0).astype(BF)
            line = jnp.sum(z, axis=0, keepdims=True)
            drow[:, at] = jnp.where(iota((nh, BLOCK), 0) == h, line, drow[:, at])
            dcol[k] = jnp.where(lanes == h, jnp.sum(z, axis=1, keepdims=True), dcol[k])

    @pl.when(base == nh - STEP_HEADS)
    def _():
        for k in range(nb):
            sl = slice(k * BLOCK, (k + 1) * BLOCK)
            dg = jnp.where(rows <= lanes, dg_s[k], 0.0)
            db_ref[sl, :] = dot(dg, c_ref[sl, :], 1, 0, HIGHEST)
            dc_ref[sl, :] = dot(dg.T, b_ref[sl, :], 1, 0, HIGHEST)
            line_ref[:, sl] = drow[:, sl] - dcol[k].T[:nh]


def whole(*shape):
    return pl.BlockSpec(shape, lambda h: (0,) * len(shape))


def ssd_local(xh, yh, cum, b, c):
    heads, tok, width = xh.shape
    nb = tok // BLOCK
    per = pl.BlockSpec((STEP_HEADS, tok, width), lambda h: (h, 0, 0))
    sq = pltpu.VMEM((nb, 128, 128), F32)
    return pl.pallas_call(
        ssd_local_kernel,
        grid=(heads // STEP_HEADS,),
        in_specs=[per, per, whole(heads, tok), whole(tok, 128), whole(tok, 128)],
        out_specs=[
            per,
            pl.BlockSpec((STEP_HEADS, 2 * nb - 2, 128, 128), lambda h: (h, 0, 0, 0)),
            whole(heads, tok),
            whole(tok, 128),
            whole(tok, 128),
        ],
        out_shape=[
            jax.ShapeDtypeStruct((heads, tok, width), BF),
            jax.ShapeDtypeStruct((heads, 2 * nb - 2, 128, 128), BF),
            jax.ShapeDtypeStruct((heads, tok), F32),
            jax.ShapeDtypeStruct((tok, 128), F32),
            jax.ShapeDtypeStruct((tok, 128), F32),
        ],
        scratch_shapes=[sq] * 6 + [pltpu.VMEM((heads, tok), F32)],
        compiler_params=pltpu.CompilerParams(vmem_limit_bytes=60 << 20),
        cost_estimate=pl.CostEstimate(
            flops=4 * 10**9, bytes_accessed=10**7, transcendentals=10**6
        ),
        name="ssd_local",
    )(xh, yh, cum, b, c)


def ssd_grad_kernel(
    xh, yh, states, cum, b_ref, c_ref, dxl, fp, line_ref, dbl, dcl,
    dx_ref, da_ref, db_ref, dc_ref,
    dct, dbt, bt_s, ct_s, colp, drow, dxs,
):
    base = pl.program_id(0) * STEP_HEADS
    nh = cum.shape[0]
    nb = xh.shape[1] // BLOCK

    @pl.when(base == 0)
    def _():
        dct[...] = jnp.zeros_like(dct)
        dbt[...] = jnp.zeros_like(dbt)
        drow[...] = line_ref[...]
        for k in range(nb):
            sl = slice(k * BLOCK, (k + 1) * BLOCK)
            bt_s[k] = b_ref[sl, :].T
            ct_s[k] = c_ref[sl, :].T
            turned_columns(cum, k, colp)

    turned = [pltpu.roll(colp[k], lax.rem(BLOCK - base, BLOCK), 1) for k in range(nb)]
    for hh in range(STEP_HEADS):
        h = base + hh
        c, keep, tail, grow = head_vectors(cum, h, nb)
        state = [states[hh, 0:128, :].astype(F32)]
        for k in range(nb - 1):
            state.append(keep[k] * state[k] + fp[hh, k].astype(F32))
        pull = states[hh, 128:256, :].astype(F32)
        for k in reversed(range(nb)):
            at = slice(k * BLOCK, (k + 1) * BLOCK)
            x = xh[hh, at, :]
            y = yh[hh, at, :]
            sb = state[k].astype(BF)
            pb = pull.astype(BF)
            bs = (b_ref[at, :] * turned[k][:, 64 + hh : 65 + hh]).astype(BF)
            dx = dxl[hh, at, :].astype(F32) + dot(bs, pb, 1, 0)
            dxs[pl.ds(k * BLOCK * nh + h, BLOCK, stride=nh), :] = dx
            dcs = dot(sb, y, 1, 1) * grow[k]
            dct[k] += dcs
            dbs = dot(pb, x, 1, 1) * tail[k]
            dbt[k] += dbs
            vs = jnp.sum(dbs * bt_s[k], axis=0, keepdims=True)
            line = jnp.sum(dcs * ct_s[k], axis=0, keepdims=True) - vs
            cross = keep[k] * jnp.sum(state[k] * pull, axis=0, keepdims=True)
            last = jnp.sum(vs + cross, axis=1, keepdims=True)
            line = jnp.where(iota((1, BLOCK), 1) == BLOCK - 1, line + last, line)
            old = drow[:, at]
            drow[:, at] = jnp.where(iota((nh, BLOCK), 0) == h, old + line, old)
            if k > 0:
                pull = keep[k] * pull + fp[hh, nb - 2 + k].astype(F32)

    @pl.when(base == nh - STEP_HEADS)
    def _():
        late = (iota((BLOCK, BLOCK), 0) >= iota((BLOCK, BLOCK), 1)).astype(F32)
        for k in range(nb):
            sl = slice(k * BLOCK, (k + 1) * BLOCK)
            db_ref[sl, :] = dbl[sl, :] + dbt[k].T
            dc_ref[sl, :] = dcl[sl, :] + dct[k].T
            da_ref[:, sl] = dot(drow[:, sl], late, 1, 0, HIGHEST)
            dx_ref[sl] = (
                dxs[k * BLOCK * nh : (k + 1) * BLOCK * nh, :]
                .reshape(BLOCK, nh, 128)
                .astype(BF)
            )


def ssd_grad(xh, yh, states, cum, b, c, local):
    heads, tok, width = xh.shape
    nb = tok // BLOCK
    rows = states.shape[1]
    per = pl.BlockSpec((STEP_HEADS, tok, width), lambda h: (h, 0, 0))
    sq = pltpu.VMEM((nb, 128, 128), F32)
    return pl.pallas_call(
        ssd_grad_kernel,
        grid=(heads // STEP_HEADS,),
        in_specs=[
            per,
            per,
            pl.BlockSpec((STEP_HEADS, rows, 128), lambda h: (h, 0, 0)),
            whole(heads, tok),
            whole(tok, 128),
            whole(tok, 128),
            per,
            pl.BlockSpec((STEP_HEADS, 2 * nb - 2, 128, 128), lambda h: (h, 0, 0, 0)),
            whole(heads, tok),
            whole(tok, 128),
            whole(tok, 128),
        ],
        out_specs=[
            whole(tok, heads, width),
            whole(heads, tok),
            whole(tok, 128),
            whole(tok, 128),
        ],
        out_shape=[
            jax.ShapeDtypeStruct((tok, heads, width), BF),
            jax.ShapeDtypeStruct((heads, tok), F32),
            jax.ShapeDtypeStruct((tok, 128), F32),
            jax.ShapeDtypeStruct((tok, 128), F32),
        ],
        scratch_shapes=[sq] * 5
        + [pltpu.VMEM((heads, tok), F32), pltpu.VMEM((tok * heads, width), F32)],
        compiler_params=pltpu.CompilerParams(vmem_limit_bytes=60 << 20),
        cost_estimate=pl.CostEstimate(
            flops=6 * 10**9, bytes_accessed=10**7, transcendentals=10**6
        ),
        name="ssd_grad",
    )(xh, yh, states, cum, b, c, *local)


def finish_kernel(*refs):
    dqt, parts, (dq, dk, dv) = refs[:5], refs[5:13], refs[13:]
    total = functools.reduce(jnp.add, [r[...].astype(F32) for r in dqt])
    dq[...] = total.T.astype(BF)
    place = lax.axis_index("head")
    for m, r in enumerate(parts):
        h = place ^ m
        for j in range(2):
            to = pl.ds(pl.multiple_of(256 * j + 32 * h, 32), 32)
            dk[to, :] = r[32 * j : 32 * j + 32, :]
            dv[to, :] = r[64 + 32 * j : 96 + 32 * j, :]


def finish(dqt, parts):
    out = jax.ShapeDtypeStruct((512, 128), BF)
    return pl.pallas_call(
        finish_kernel,
        in_specs=[VM] * 13,
        out_specs=[VM, VM, VM],
        out_shape=[out, out, out],
        compiler_params=pltpu.CompilerParams(vmem_limit_bytes=16 << 20),
        name="finish",
    )(*dqt, *parts)


def swap(v, m):
    return lax.ppermute(v, "head", [(i, i ^ m) for i in range(8)])


def turn_rows(v, m):
    return jnp.concatenate([v[j ^ m : (j ^ m) + 1] for j in range(v.shape[0])], axis=0)


def join(a, b):
    top = jnp.maximum(a[0], b[0])
    f, g = jnp.exp2(a[0] - top), jnp.exp2(b[0] - top)
    return jnp.stack([top, f * a[1] + g * b[1], f * a[2] + g * b[2]])


def gather_heads(v):
    out = [v] + [None] * 7
    for m in (2, 6, 4):
        out[m] = swap(v, m)
    for m in (0, 2, 6, 4):
        out[m + 1] = swap(out[m], 1)
    return out


def pair_sums_kernel(*refs):
    for a, b, o in zip(refs[:3], refs[3:6], refs[6:]):
        o[...] = (a[...].astype(F32) + b[...].astype(F32)).astype(BF)


def pair_sums(parts):
    mates = [swap(parts[m + 1], 1) for m in (0, 2, 4, 6)]
    out = jax.ShapeDtypeStruct(parts[0].shape, BF)
    sums = pl.pallas_call(
        pair_sums_kernel,
        in_specs=[VM] * 6,
        out_specs=[VM] * 3,
        out_shape=[out] * 3,
        compiler_params=pltpu.CompilerParams(vmem_limit_bytes=16 << 20),
        name="pair_sums",
    )(*parts[2::2], *mates[1:])
    return [parts[0], mates[0]], sums


def after(value, other):
    return lax.optimization_barrier((value, other))[0]


def per_device(
    ssd_input, log_decay, input_map, output_map, ssd_cotangent,
    queries, key_rows, value_rows, attn_cotangent, pair_order,
):
    tok, heads, width = ssd_input.shape
    b = input_map.reshape(tok, 128)
    c = output_map.reshape(tok, 128)
    send, xh, yh, cum, qd = ssd_send(
        ssd_input, ssd_cotangent, log_decay.T, b, c, key_rows, value_rows,
        queries.reshape(tok, 128), attn_cotangent.reshape(tok, 128),
    )
    recv = lax.all_to_all(send, "seq", 0, 0)
    qds = gather_heads(qd)
    local = ssd_local(xh, yh, cum, b, c)
    turned = scan(after(recv, local[2]))
    states = lax.all_to_all(turned, "seq", 0, 0)
    first, mate = attn_stat(pair_order, after(recv, turned), qds)
    stat = join(first, swap(mate, 1))
    rest = [swap(stat, m) for m in (2, 6, 4)]
    back, *dqt = attn_grad(pair_order, after(recv, states), qds, stat, *rest)
    kept, sums = pair_sums(dqt)
    dx, da, db, dc = ssd_grad(after(xh, (back, *sums)), yh, states, cum, b, c, local)
    back = lax.all_to_all(back, "seq", 0, 0)
    dqt = kept + [swap(sums[i], m) for i, m in ((0, 2), (2, 6), (1, 4))]
    dkv = jnp.sum(after(back, da).astype(F32), axis=0).astype(BF)
    parts = gather_heads(dkv)
    dq, dk, dv = finish(dqt, parts)
    return (
        dx,
        da.T,
        db.reshape(tok, 1, 128),
        dc.reshape(tok, 1, 128),
        dq.reshape(tok, 1, 128),
        dk,
        dv,
    )


def solution(mesh):
    tok = P("seq", "head", None)
    return jax.shard_map(
        per_device,
        mesh=mesh,
        in_specs=(
            tok, P("seq", "head"), tok, tok, tok, tok,
            P("seq", None), P("seq", None), tok, P(),
        ),
        out_specs=(tok, P("seq", "head"), tok, tok, tok, P("seq", None), P("seq", None)),
        check_vma=False,
    )
```

```python
import functools

import jax
import jax.numpy as jnp
from jax import lax
from jax.experimental import pallas as pl
from jax.experimental.pallas import tpu as pltpu
from jax.sharding import PartitionSpec as P

BLOCK = 128
BF = jnp.bfloat16
F32 = jnp.float32
HIGHEST = lax.Precision.HIGHEST
NEG = -1e30
LOG2E = 1.4426950408889634
STATE_ROWS = 256
TOTAL_ROWS = 16


def dot(a, b, ca, cb, precision=None):
    return lax.dot_general(
        a, b, (((ca,), (cb,)), ((), ())), precision=precision, preferred_element_type=F32
    )


def iota(shape, dim):
    return lax.broadcasted_iota(jnp.int32, shape, dim)


def pieces(v, count):
    out = []
    for _ in range(count):
        p = v.astype(BF)
        out.append(p)
        v = v - p.astype(F32)
    return out


def ssd_send_kernel(
    x_ref, y_ref, at_ref, b_ref, c_ref, k_ref, v_ref, q_ref, do_ref,
    send_ref, xh_ref, yh_ref, cum_ref, qd_ref, st, pu, run,
):
    k = pl.program_id(0)
    heads = x_ref.shape[1]

    @pl.when(k == 0)
    def _():
        st[...] = jnp.zeros_like(st)
        pu[...] = jnp.zeros_like(pu)
        run[...] = jnp.zeros_like(run)

    upto = (iota((BLOCK, BLOCK), 0) <= iota((BLOCK, BLOCK), 1)).astype(F32)
    cum = dot(at_ref[...], upto, 1, 0, HIGHEST)
    cum_ref[...] = cum
    total = cum[:, BLOCK - 1 :]
    grow = jnp.exp(cum)
    tail = jnp.exp(total - cum)
    keep = jnp.exp(total)
    before = run[:, :1]
    early = jnp.exp(before)
    run[...] = jnp.broadcast_to(before + total, run.shape)
    bt = b_ref[...].T
    ct = c_ref[...].T
    xt = jnp.swapaxes(x_ref[...], 0, 1)
    yt = jnp.swapaxes(y_ref[...], 0, 1)
    for h in range(heads):
        x = xt[h]
        y = yt[h]
        xh_ref[h] = x
        yh_ref[h] = y
        bs = (bt * tail[h : h + 1, :]).astype(BF)
        cs = (ct * grow[h : h + 1, :]).astype(BF)
        st[h] = keep[h : h + 1, :] * st[h] + dot(bs, x, 1, 0)
        pu[h] = pu[h] + early[h : h + 1, :] * dot(cs, y, 1, 0).astype(BF).astype(F32)

    @pl.when(k == pl.num_programs(0) - 1)
    def _():
        qd_ref[0] = q_ref[...]
        qd_ref[1] = do_ref[...]
        at = pl.multiple_of(lax.axis_index("head") * 32, 32)
        half = k_ref.shape[0] // 2
        subs = [r[pl.ds(at + o, 32), :] for r in (k_ref, v_ref) for o in (0, half)]
        three = pieces(run[...], 3)
        for h in range(heads):
            send_ref[h, 0:128, :] = st[h].astype(BF)
            send_ref[h, 128:256, :] = pu[h].astype(BF)
            for i, s in enumerate(subs):
                send_ref[h, 256 + 32 * i : 288 + 32 * i, :] = s
            rows = iota((TOTAL_ROWS, 128), 0)
            t = jnp.zeros((TOTAL_ROWS, 128), F32)
            for i, p in enumerate(three):
                t = jnp.where(rows == i, p[h : h + 1, :].astype(F32), t)
            send_ref[h, 384:400, :] = t.astype(BF)


def ssd_send(x, y, at, b, c, keys, values, q, do):
    tok, heads, width = x.shape
    nb = tok // BLOCK
    blk = pl.BlockSpec((BLOCK, heads, width), lambda k: (k, 0, 0))
    mat = pl.BlockSpec((BLOCK, 128), lambda k: (k, 0))
    row = pl.BlockSpec((heads, BLOCK), lambda k: (0, k))
    hm = pl.BlockSpec((heads, BLOCK, width), lambda k: (0, k, 0))
    whole = pl.BlockSpec((tok, 128), lambda k: (0, 0))
    rows = STATE_ROWS + 128 + TOTAL_ROWS
    return pl.pallas_call(
        ssd_send_kernel,
        grid_spec=pltpu.PrefetchScalarGridSpec(
            num_scalar_prefetch=0,
            grid=(nb,),
            in_specs=[blk, blk, row, mat, mat, whole, whole, whole, whole],
            out_specs=[
                pl.BlockSpec((heads, rows, 128), lambda k: (0, 0, 0)),
                hm,
                hm,
                row,
                pl.BlockSpec((2, tok, 128), lambda k: (0, 0, 0)),
            ],
            scratch_shapes=[
                pltpu.VMEM((heads, 128, 128), F32),
                pltpu.VMEM((heads, 128, 128), F32),
                pltpu.VMEM((heads, 128), F32),
            ],
        ),
        out_shape=[
            jax.ShapeDtypeStruct((heads, rows, 128), BF),
            jax.ShapeDtypeStruct((heads, tok, width), BF),
            jax.ShapeDtypeStruct((heads, tok, width), BF),
            jax.ShapeDtypeStruct((heads, tok), F32),
            jax.ShapeDtypeStruct((2, tok, 128), BF),
        ],
        compiler_params=pltpu.CompilerParams(vmem_limit_bytes=60 << 20),
        cost_estimate=pl.CostEstimate(
            flops=3 * 10**9, bytes_accessed=10**7, transcendentals=10**5
        ),
        name="ssd_send",
    )(x, y, at, b, c, keys, values, q, do)


VM = pl.BlockSpec(memory_space=pltpu.VMEM)
SM = pl.BlockSpec(memory_space=pltpu.SMEM)
HB = pl.BlockSpec(memory_space=pltpu.HBM)


def scan_kernel(recv, back):
    n = recv.shape[0]
    state = jnp.zeros((128, 128), F32)
    for e in range(n):
        back[e, 0:128, :] = state.astype(BF)
        if e < n - 1:
            t = recv[e, 384:400, :].astype(F32)
            keep = jnp.exp(t[0:1] + t[1:2] + t[2:3])
            state = keep * state + recv[e, 0:128, :].astype(F32)
    pull = jnp.zeros((128, 128), F32)
    for e in reversed(range(n)):
        back[e, 128:256, :] = pull.astype(BF)
        if e > 0:
            t = recv[e, 384:400, :].astype(F32)
            keep = jnp.exp(t[0:1] + t[1:2] + t[2:3])
            pull = keep * pull + recv[e, 128:256, :].astype(F32)


def scan(recv):
    n = recv.shape[0]
    return pl.pallas_call(
        scan_kernel,
        in_specs=[VM],
        out_specs=VM,
        out_shape=jax.ShapeDtypeStruct((n, 256, 128), BF),
        compiler_params=pltpu.CompilerParams(vmem_limit_bytes=20 << 20),
        name="scan",
    )(recv)


def sort_keys(order, inverse, recv, ks, vs):
    for e in range(16):
        inverse[order[e]] = e
    for b in range(32):
        src = inverse[b if b < 16 else 31 - b]
        o = 0 if b < 16 else 32
        ks[32 * b : 32 * b + 32, :] = recv[src, 256 + o : 288 + o, :]
        vs[32 * b : 32 * b + 32, :] = recv[src, 320 + o : 352 + o, :]


def item_at(order, size, i):
    first = order[lax.axis_index("seq")]
    per = size // 32
    n0 = (first + per) // per
    late = (i >= n0).astype(jnp.int32)
    g = i - late * n0
    block = jnp.where(late == 1, 31 - first, first)
    kr = iota((size, 256), 0)
    key_at = (g * per + kr // 32) * 256 + lax.axis_index("head") * 32 + kr % 32
    bias = jnp.where(key_at <= block * 256 + iota((size, 256), 1), 0.0, NEG)
    return pl.multiple_of(g * size, size), pl.multiple_of(late * 256, 256), bias


def attn_stat_kernel(order, recv, *refs):
    qd, (stat, mate, ks, vs, inverse) = refs[:8], refs[8:]
    heads = len(qd)
    scale = LOG2E * 128**-0.5
    sort_keys(order, inverse, recv, ks, vs)
    stat[0] = jnp.full((heads, 512), NEG, F32)
    stat[1:] = jnp.zeros((2, heads, 512), F32)

    def item(i, carry):
        kat, rat, bias = item_at(order, 256, i)
        kg = ks[pl.ds(kat, 256), :]
        vg = vs[pl.ds(kat, 256), :]
        for h in range(heads):
            s = dot(kg, qd[h][0, pl.ds(rat, 256), :], 1, 1) * scale + bias
            dp = dot(vg, qd[h][1, pl.ds(rat, 256), :], 1, 1)
            at = (slice(h, h + 1), pl.ds(rat, 256))
            old = stat[0, *at]
            top = jnp.maximum(old, jnp.max(s, axis=0, keepdims=True))
            p = jnp.exp2(s - top)
            fix = jnp.exp2(old - top)
            stat[0, *at] = top
            stat[1, *at] = fix * stat[1, *at] + jnp.sum(p, axis=0, keepdims=True)
            stat[2, *at] = fix * stat[2, *at] + jnp.sum(p * dp, axis=0, keepdims=True)
        return carry

    lax.fori_loop(0, 5, item, 0)
    for i in range(3):
        mate[i] = turn_rows(stat[i], 1)


def attn_stat(order, recv, qd):
    heads = len(qd)
    return pl.pallas_call(
        attn_stat_kernel,
        in_specs=[SM] + [VM] * 9,
        out_specs=[VM, VM],
        out_shape=[jax.ShapeDtypeStruct((3, heads, 512), F32)] * 2,
        scratch_shapes=[
            pltpu.VMEM((1024, 128), BF),
            pltpu.VMEM((1024, 128), BF),
            pltpu.SMEM((16,), jnp.int32),
        ],
        compiler_params=pltpu.CompilerParams(vmem_limit_bytes=20 << 20),
        cost_estimate=pl.CostEstimate(
            flops=10**8, bytes_accessed=10**5, transcendentals=10**4
        ),
        name="attn_stat",
    )(order, recv, *qd)


def attn_grad_kernel(order, recv, *refs):
    qd, stats, send, dqt = refs[:8], refs[8:12], refs[12], refs[13:21]
    ks, vs, dk, dv, lse, delta, dqs, inverse, dqo, buf, sem = refs[21:]
    heads = len(qd)
    scale = 128**-0.5
    sort_keys(order, inverse, recv, ks, vs)
    tables = [[r[i] for i in range(3)] for r in stats]
    for m, v in zip((2, 6, 4), tables[1:]):
        v[:] = [turn_rows(x, m) for x in v]
    top = functools.reduce(jnp.maximum, [v[0] for v in tables])
    total = jnp.zeros_like(top)
    dsum = jnp.zeros_like(top)
    for v in tables:
        f = jnp.exp2(v[0] - top)
        total = total + f * v[1]
        dsum = dsum + f * v[2]
    lse[...] = top + jnp.log2(total)
    delta[...] = dsum / total
    dk[...] = jnp.zeros_like(dk)
    dv[...] = jnp.zeros_like(dv)
    dqs[...] = jnp.zeros_like(dqs)

    def item(i, carry):
        kat, rat, bias = item_at(order, 512, i)
        kg = ks[pl.ds(kat, 512), :]
        vg = vs[pl.ds(kat, 512), :]
        kt = kg.astype(F32).T.astype(BF)
        dkg = dk[pl.ds(kat, 512), :]
        dvg = dv[pl.ds(kat, 512), :]
        for h in range(heads):
            q = qd[h][0, pl.ds(rat, 256), :]
            do = qd[h][1, pl.ds(rat, 256), :]
            s = dot(kg, q, 1, 1) * (scale * LOG2E) + bias
            dp = dot(vg, do, 1, 1)
            p = jnp.exp2(s - lse[h : h + 1, pl.ds(rat, 256)])
            ds = (p * (dp - delta[h : h + 1, pl.ds(rat, 256)])).astype(BF)
            dvg = dvg + dot(p.astype(BF), do, 1, 0)
            dkg = dkg + dot(ds, q, 1, 0)
            dqs[h, :, pl.ds(rat, 256)] += dot(kt, ds, 1, 0)
        dk[pl.ds(kat, 512), :] = dkg
        dv[pl.ds(kat, 512), :] = dvg
        return carry

    lax.fori_loop(0, 3, item, 0)
    dqo[...] = (dqs[...] * scale).astype(BF)
    moves = [pltpu.make_async_copy(dqo.at[h], dqt[h], sem.at[h]) for h in range(heads)]
    for m in moves:
        m.start()
    for e in range(16):
        b = order[e]
        for j, (r, f) in enumerate(((dk, scale), (dv, 1.0))):
            lo = r[pl.ds(pl.multiple_of(b * 32, 32), 32), :]
            hi = r[pl.ds(pl.multiple_of((31 - b) * 32, 32), 32), :]
            buf[e, 64 * j : 32 + 64 * j, :] = (lo * f).astype(BF)
            buf[e, 32 + 64 * j : 64 + 64 * j, :] = (hi * f).astype(BF)
    moves.append(pltpu.make_async_copy(buf, send, sem.at[heads]))
    moves[-1].start()
    for m in moves:
        m.wait()


def attn_grad(order, recv, qd, *stats):
    heads = len(qd)
    n = recv.shape[0]
    return pl.pallas_call(
        attn_grad_kernel,
        in_specs=[SM] + [VM] * 13,
        out_specs=[HB] * 9,
        out_shape=[pltpu.HBM((n, 128, 128), BF)] + [pltpu.HBM((128, 512), BF)] * 8,
        scratch_shapes=[
            pltpu.VMEM((1024, 128), BF),
            pltpu.VMEM((1024, 128), BF),
            pltpu.VMEM((1024, 128), F32),
            pltpu.VMEM((1024, 128), F32),
            pltpu.VMEM((heads, 512), F32),
            pltpu.VMEM((heads, 512), F32),
            pltpu.VMEM((heads, 128, 512), F32),
            pltpu.SMEM((16,), jnp.int32),
            pltpu.VMEM((heads, 128, 512), BF),
            pltpu.VMEM((n, 128, 128), BF),
            pltpu.SemaphoreType.DMA((heads + 1,)),
        ],
        compiler_params=pltpu.CompilerParams(vmem_limit_bytes=20 << 20),
        cost_estimate=pl.CostEstimate(
            flops=10**8, bytes_accessed=10**5, transcendentals=10**4
        ),
        name="attn_grad",
    )(order, recv, *qd, *stats)


STEP_HEADS = 4


def turned_columns(cum, k, table):
    cm = cum[:, k * BLOCK : (k + 1) * BLOCK]
    tl = jnp.exp(cm[:, BLOCK - 1 :] - cm)
    gap = jnp.zeros((BLOCK // 2 - cm.shape[0], BLOCK), F32)
    table[k] = jnp.concatenate([cm, gap, tl, gap], axis=0).T


def head_vectors(cum, h, nb):
    row = cum[pl.ds(h, 1), :]
    c = [row[:, k * BLOCK : (k + 1) * BLOCK] for k in range(nb)]
    total = [v[:, BLOCK - 1 :] for v in c]
    keep = [jnp.exp(t) for t in total]
    tail = [jnp.exp(t - v) for t, v in zip(total, c)]
    grow = [jnp.exp(v) for v in c]
    return c, keep, tail, grow


def ssd_local_kernel(
    xh, yh, cum, b_ref, c_ref,
    dxl, fp, line_ref, db_ref, dc_ref,
    g_s, dg_s, bt_s, ct_s, colp, dcol, drow,
):
    base = pl.program_id(0) * STEP_HEADS
    nh = cum.shape[0]
    nb = xh.shape[1] // BLOCK
    rows = iota((BLOCK, BLOCK), 0)
    lanes = iota((BLOCK, BLOCK), 1)

    @pl.when(base == 0)
    def _():
        dg_s[...] = jnp.zeros_like(dg_s)
        dcol[...] = jnp.zeros_like(dcol)
        drow[...] = jnp.zeros_like(drow)
        for k in range(nb):
            sl = slice(k * BLOCK, (k + 1) * BLOCK)
            b = b_ref[sl, :]
            c = c_ref[sl, :]
            g_s[k] = jnp.where(rows <= lanes, dot(b, c, 1, 1, HIGHEST), 0.0)
            bt_s[k] = b.T
            ct_s[k] = c.T
            turned_columns(cum, k, colp)

    turned = [pltpu.roll(colp[k], lax.rem(BLOCK - base, BLOCK), 1) for k in range(nb)]
    for hh in range(STEP_HEADS):
        h = base + hh
        c, keep, tail, grow = head_vectors(cum, h, nb)
        for k in range(nb):
            at = slice(k * BLOCK, (k + 1) * BLOCK)
            x = xh[hh, at, :]
            y = yh[hh, at, :]
            decay = jnp.exp(jnp.minimum(c[k] - turned[k][:, hh : hh + 1], 0.0))
            w = g_s[k] * decay
            t = dot(x, y, 1, 1) * decay
            dg_s[k] += t
            z = t * g_s[k]
            cs = (ct_s[k] * grow[k]).astype(BF)
            wy = dot(jnp.concatenate([w.astype(BF), cs], axis=0), y, 1, 0)
            dxl[hh, at, :] = wy[:BLOCK].astype(BF)
            if k > 0:
                fp[hh, nb - 2 + k] = wy[BLOCK:].astype(BF)
            if k < nb - 1:
                fp[hh, k] = dot((bt_s[k] * tail[k]).astype(BF), x, 1, 0).astype(BF)
            line = jnp.sum(z, axis=0, keepdims=True)
            drow[:, at] = jnp.where(iota((nh, BLOCK), 0) == h, line, drow[:, at])
            dcol[k] = jnp.where(lanes == h, jnp.sum(z, axis=1, keepdims=True), dcol[k])

    @pl.when(base == nh - STEP_HEADS)
    def _():
        for k in range(nb):
            sl = slice(k * BLOCK, (k + 1) * BLOCK)
            dg = jnp.where(rows <= lanes, dg_s[k], 0.0)
            db_ref[sl, :] = dot(dg, c_ref[sl, :], 1, 0, HIGHEST)
            dc_ref[sl, :] = dot(dg.T, b_ref[sl, :], 1, 0, HIGHEST)
            line_ref[:, sl] = drow[:, sl] - dcol[k].T[:nh]


def whole(*shape):
    return pl.BlockSpec(shape, lambda h: (0,) * len(shape))


def ssd_local(xh, yh, cum, b, c):
    heads, tok, width = xh.shape
    nb = tok // BLOCK
    per = pl.BlockSpec((STEP_HEADS, tok, width), lambda h: (h, 0, 0))
    sq = pltpu.VMEM((nb, 128, 128), F32)
    return pl.pallas_call(
        ssd_local_kernel,
        grid=(heads // STEP_HEADS,),
        in_specs=[per, per, whole(heads, tok), whole(tok, 128), whole(tok, 128)],
        out_specs=[
            per,
            pl.BlockSpec((STEP_HEADS, 2 * nb - 2, 128, 128), lambda h: (h, 0, 0, 0)),
            whole(heads, tok),
            whole(tok, 128),
            whole(tok, 128),
        ],
        out_shape=[
            jax.ShapeDtypeStruct((heads, tok, width), BF),
            jax.ShapeDtypeStruct((heads, 2 * nb - 2, 128, 128), BF),
            jax.ShapeDtypeStruct((heads, tok), F32),
            jax.ShapeDtypeStruct((tok, 128), F32),
            jax.ShapeDtypeStruct((tok, 128), F32),
        ],
        scratch_shapes=[sq] * 6 + [pltpu.VMEM((heads, tok), F32)],
        compiler_params=pltpu.CompilerParams(vmem_limit_bytes=60 << 20),
        cost_estimate=pl.CostEstimate(
            flops=4 * 10**9, bytes_accessed=10**7, transcendentals=10**6
        ),
        name="ssd_local",
    )(xh, yh, cum, b, c)


def ssd_grad_kernel(
    xh, yh, states, cum, b_ref, c_ref, dxl, fp, line_ref, dbl, dcl,
    dx_ref, da_ref, db_ref, dc_ref,
    dct, dbt, bt_s, ct_s, colp, drow, dxs,
):
    base = pl.program_id(0) * STEP_HEADS
    nh = cum.shape[0]
    nb = xh.shape[1] // BLOCK

    @pl.when(base == 0)
    def _():
        dct[...] = jnp.zeros_like(dct)
        dbt[...] = jnp.zeros_like(dbt)
        drow[...] = line_ref[...]
        for k in range(nb):
            sl = slice(k * BLOCK, (k + 1) * BLOCK)
            bt_s[k] = b_ref[sl, :].T
            ct_s[k] = c_ref[sl, :].T
            turned_columns(cum, k, colp)

    turned = [pltpu.roll(colp[k], lax.rem(BLOCK - base, BLOCK), 1) for k in range(nb)]
    for hh in range(STEP_HEADS):
        h = base + hh
        c, keep, tail, grow = head_vectors(cum, h, nb)
        state = [states[hh, 0:128, :].astype(F32)]
        for k in range(nb - 1):
            state.append(keep[k] * state[k] + fp[hh, k].astype(F32))
        pull = states[hh, 128:256, :].astype(F32)
        for k in reversed(range(nb)):
            at = slice(k * BLOCK, (k + 1) * BLOCK)
            x = xh[hh, at, :]
            y = yh[hh, at, :]
            sb = state[k].astype(BF)
            pb = pull.astype(BF)
            bs = (b_ref[at, :] * turned[k][:, 64 + hh : 65 + hh]).astype(BF)
            dx = dxl[hh, at, :].astype(F32) + dot(bs, pb, 1, 0)
            dxs[pl.ds(k * BLOCK * nh + h, BLOCK, stride=nh), :] = dx
            dcs = dot(sb, y, 1, 1) * grow[k]
            dct[k] += dcs
            dbs = dot(pb, x, 1, 1) * tail[k]
            dbt[k] += dbs
            vs = jnp.sum(dbs * bt_s[k], axis=0, keepdims=True)
            line = jnp.sum(dcs * ct_s[k], axis=0, keepdims=True) - vs
            cross = keep[k] * jnp.sum(state[k] * pull, axis=0, keepdims=True)
            last = jnp.sum(vs + cross, axis=1, keepdims=True)
            line = jnp.where(iota((1, BLOCK), 1) == BLOCK - 1, line + last, line)
            old = drow[:, at]
            drow[:, at] = jnp.where(iota((nh, BLOCK), 0) == h, old + line, old)
            if k > 0:
                pull = keep[k] * pull + fp[hh, nb - 2 + k].astype(F32)

    @pl.when(base == nh - STEP_HEADS)
    def _():
        late = (iota((BLOCK, BLOCK), 0) >= iota((BLOCK, BLOCK), 1)).astype(F32)
        for k in range(nb):
            sl = slice(k * BLOCK, (k + 1) * BLOCK)
            db_ref[sl, :] = dbl[sl, :] + dbt[k].T
            dc_ref[sl, :] = dcl[sl, :] + dct[k].T
            da_ref[:, sl] = dot(drow[:, sl], late, 1, 0, HIGHEST)
            dx_ref[sl] = (
                dxs[k * BLOCK * nh : (k + 1) * BLOCK * nh, :]
                .reshape(BLOCK, nh, 128)
                .astype(BF)
            )


def ssd_grad(xh, yh, states, cum, b, c, local):
    heads, tok, width = xh.shape
    nb = tok // BLOCK
    rows = states.shape[1]
    per = pl.BlockSpec((STEP_HEADS, tok, width), lambda h: (h, 0, 0))
    sq = pltpu.VMEM((nb, 128, 128), F32)
    return pl.pallas_call(
        ssd_grad_kernel,
        grid=(heads // STEP_HEADS,),
        in_specs=[
            per,
            per,
            pl.BlockSpec((STEP_HEADS, rows, 128), lambda h: (h, 0, 0)),
            whole(heads, tok),
            whole(tok, 128),
            whole(tok, 128),
            per,
            pl.BlockSpec((STEP_HEADS, 2 * nb - 2, 128, 128), lambda h: (h, 0, 0, 0)),
            whole(heads, tok),
            whole(tok, 128),
            whole(tok, 128),
        ],
        out_specs=[
            whole(tok, heads, width),
            whole(heads, tok),
            whole(tok, 128),
            whole(tok, 128),
        ],
        out_shape=[
            jax.ShapeDtypeStruct((tok, heads, width), BF),
            jax.ShapeDtypeStruct((heads, tok), F32),
            jax.ShapeDtypeStruct((tok, 128), F32),
            jax.ShapeDtypeStruct((tok, 128), F32),
        ],
        scratch_shapes=[sq] * 5
        + [pltpu.VMEM((heads, tok), F32), pltpu.VMEM((tok * heads, width), F32)],
        compiler_params=pltpu.CompilerParams(vmem_limit_bytes=60 << 20),
        cost_estimate=pl.CostEstimate(
            flops=6 * 10**9, bytes_accessed=10**7, transcendentals=10**6
        ),
        name="ssd_grad",
    )(xh, yh, states, cum, b, c, *local)


def finish_kernel(*refs):
    dqt, parts, (dq, dk, dv) = refs[:5], refs[5:13], refs[13:]
    total = functools.reduce(jnp.add, [r[...].astype(F32) for r in dqt])
    dq[...] = total.T.astype(BF)
    place = lax.axis_index("head")
    for m, r in enumerate(parts):
        h = place ^ m
        for j in range(2):
            to = pl.ds(pl.multiple_of(256 * j + 32 * h, 32), 32)
            dk[to, :] = r[32 * j : 32 * j + 32, :]
            dv[to, :] = r[64 + 32 * j : 96 + 32 * j, :]


def finish(dqt, parts):
    out = jax.ShapeDtypeStruct((512, 128), BF)
    return pl.pallas_call(
        finish_kernel,
        in_specs=[VM] * 13,
        out_specs=[VM, VM, VM],
        out_shape=[out, out, out],
        compiler_params=pltpu.CompilerParams(vmem_limit_bytes=16 << 20),
        name="finish",
    )(*dqt, *parts)


def swap(v, m):
    return lax.ppermute(v, "head", [(i, i ^ m) for i in range(8)])


def turn_rows(v, m):
    return jnp.concatenate([v[j ^ m : (j ^ m) + 1] for j in range(v.shape[0])], axis=0)


def join(a, b):
    top = jnp.maximum(a[0], b[0])
    f, g = jnp.exp2(a[0] - top), jnp.exp2(b[0] - top)
    return jnp.stack([top, f * a[1] + g * b[1], f * a[2] + g * b[2]])


def gather_heads(v, other=None):
    out = [v] + [None] * 7
    for m in (2, 6, 4):
        out[m] = swap(v, m) if other is None else after(swap(v, m), other)
    for m in (0, 2, 6, 4):
        out[m + 1] = swap(out[m], 1)
    return out


def pair_sums_kernel(*refs):
    own, mates, outs, (held, sem) = refs[:3], refs[3:6], refs[6:9], refs[9:]
    moves = [pltpu.make_async_copy(r, held.at[i], sem.at[i]) for i, r in enumerate(own)]
    for m in moves:
        m.start()
    for m in moves:
        m.wait()
    for i in range(3):
        outs[i][...] = (held[i].astype(F32) + mates[i][...].astype(F32)).astype(BF)


def pair_sums(parts):
    mates = [swap(parts[m + 1], 1) for m in (0, 2, 4, 6)]
    out = jax.ShapeDtypeStruct(parts[0].shape, BF)
    sums = pl.pallas_call(
        pair_sums_kernel,
        in_specs=[HB] * 3 + [VM] * 3,
        out_specs=[VM] * 3,
        out_shape=[out] * 3,
        scratch_shapes=[
            pltpu.VMEM((3,) + parts[0].shape, BF),
            pltpu.SemaphoreType.DMA((3,)),
        ],
        compiler_params=pltpu.CompilerParams(vmem_limit_bytes=16 << 20),
        name="pair_sums",
    )(*[pltpu.with_memory_space_constraint(p, pltpu.HBM) for p in parts[2::2]], *mates[1:])
    return [parts[0], mates[0]], sums


def after(value, other):
    return lax.optimization_barrier((value, other))[0]


def per_device(
    ssd_input, log_decay, input_map, output_map, ssd_cotangent,
    queries, key_rows, value_rows, attn_cotangent, pair_order,
):
    tok, heads, width = ssd_input.shape
    b = input_map.reshape(tok, 128)
    c = output_map.reshape(tok, 128)
    send, xh, yh, cum, qd = ssd_send(
        ssd_input, ssd_cotangent, log_decay.T, b, c, key_rows, value_rows,
        queries.reshape(tok, 128), attn_cotangent.reshape(tok, 128),
    )
    recv = lax.all_to_all(send, "seq", 0, 0)
    local = ssd_local(xh, yh, cum, b, c)
    qds = gather_heads(qd, local[2])
    turned = scan(after(recv, qds))
    states = lax.all_to_all(turned, "seq", 0, 0)
    first, mate = attn_stat(pair_order, after(recv, turned), qds)
    stat = join(first, swap(mate, 1))
    rest = [swap(stat, m) for m in (2, 6, 4)]
    back, *dqt = attn_grad(pair_order, recv, qds, stat, *rest)
    back, *dqt = after([back, *dqt], states)
    kept, sums = pair_sums(dqt)
    dx, da, db, dc = ssd_grad(after(xh, (back, *sums)), yh, states, cum, b, c, local)
    back = lax.all_to_all(back, "seq", 0, 0)
    dqt = kept + [swap(sums[i], m) for i, m in ((0, 2), (2, 6), (1, 4))]
    dkv = jnp.sum(after(back, da).astype(F32), axis=0).astype(BF)
    parts = gather_heads(dkv)
    dq, dk, dv = finish(dqt, parts)
    return (
        dx,
        da.T,
        db.reshape(tok, 1, 128),
        dc.reshape(tok, 1, 128),
        dq.reshape(tok, 1, 128),
        dk,
        dv,
    )


def solution(mesh):
    tok = P("seq", "head", None)
    return jax.shard_map(
        per_device,
        mesh=mesh,
        in_specs=(
            tok, P("seq", "head"), tok, tok, tok, tok,
            P("seq", None), P("seq", None), tok, P(),
        ),
        out_specs=(tok, P("seq", "head"), tok, tok, tok, P("seq", None), P("seq", None)),
        check_vma=False,
    )
```

```python
import functools

import jax
import jax.numpy as jnp
from jax import lax
from jax.experimental import pallas as pl
from jax.experimental.pallas import tpu as pltpu
from jax.sharding import PartitionSpec as P

BLOCK = 128
BF = jnp.bfloat16
F32 = jnp.float32
HIGHEST = lax.Precision.HIGHEST
NEG = -1e30
LOG2E = 1.4426950408889634
STATE_ROWS = 256
TOTAL_ROWS = 16


def dot(a, b, ca, cb, precision=None):
    return lax.dot_general(
        a, b, (((ca,), (cb,)), ((), ())), precision=precision, preferred_element_type=F32
    )


def iota(shape, dim):
    return lax.broadcasted_iota(jnp.int32, shape, dim)


def pieces(v, count):
    out = []
    for _ in range(count):
        p = v.astype(BF)
        out.append(p)
        v = v - p.astype(F32)
    return out


def ssd_send_kernel(
    x_ref, y_ref, at_ref, b_ref, c_ref, k_ref, v_ref, q_ref, do_ref,
    send_ref, xh_ref, yh_ref, cum_ref, qd_ref, st, pu, run,
):
    k = pl.program_id(0)
    heads = x_ref.shape[1]

    @pl.when(k == 0)
    def _():
        st[...] = jnp.zeros_like(st)
        pu[...] = jnp.zeros_like(pu)
        run[...] = jnp.zeros_like(run)

    upto = (iota((BLOCK, BLOCK), 0) <= iota((BLOCK, BLOCK), 1)).astype(F32)
    cum = dot(at_ref[...], upto, 1, 0, HIGHEST)
    cum_ref[...] = cum
    total = cum[:, BLOCK - 1 :]
    grow = jnp.exp(cum)
    tail = jnp.exp(total - cum)
    keep = jnp.exp(total)
    before = run[:, :1]
    early = jnp.exp(before)
    run[...] = jnp.broadcast_to(before + total, run.shape)
    bt = b_ref[...].T
    ct = c_ref[...].T
    xt = jnp.swapaxes(x_ref[...], 0, 1)
    yt = jnp.swapaxes(y_ref[...], 0, 1)
    for h in range(heads):
        x = xt[h]
        y = yt[h]
        xh_ref[h] = x
        yh_ref[h] = y
        bs = (bt * tail[h : h + 1, :]).astype(BF)
        cs = (ct * grow[h : h + 1, :]).astype(BF)
        st[h] = keep[h : h + 1, :] * st[h] + dot(bs, x, 1, 0)
        pu[h] = pu[h] + early[h : h + 1, :] * dot(cs, y, 1, 0).astype(BF).astype(F32)

    @pl.when(k == pl.num_programs(0) - 1)
    def _():
        qd_ref[0] = q_ref[...]
        qd_ref[1] = do_ref[...]
        at = pl.multiple_of(lax.axis_index("head") * 32, 32)
        half = k_ref.shape[0] // 2
        subs = [r[pl.ds(at + o, 32), :] for r in (k_ref, v_ref) for o in (0, half)]
        three = pieces(run[...], 3)
        for h in range(heads):
            send_ref[h, 0:128, :] = st[h].astype(BF)
            send_ref[h, 128:256, :] = pu[h].astype(BF)
            for i, s in enumerate(subs):
                send_ref[h, 256 + 32 * i : 288 + 32 * i, :] = s
            rows = iota((TOTAL_ROWS, 128), 0)
            t = jnp.zeros((TOTAL_ROWS, 128), F32)
            for i, p in enumerate(three):
                t = jnp.where(rows == i, p[h : h + 1, :].astype(F32), t)
            send_ref[h, 384:400, :] = t.astype(BF)


def ssd_send(x, y, at, b, c, keys, values, q, do):
    tok, heads, width = x.shape
    nb = tok // BLOCK
    blk = pl.BlockSpec((BLOCK, heads, width), lambda k: (k, 0, 0))
    mat = pl.BlockSpec((BLOCK, 128), lambda k: (k, 0))
    row = pl.BlockSpec((heads, BLOCK), lambda k: (0, k))
    hm = pl.BlockSpec((heads, BLOCK, width), lambda k: (0, k, 0))
    whole = pl.BlockSpec((tok, 128), lambda k: (0, 0))
    rows = STATE_ROWS + 128 + TOTAL_ROWS
    return pl.pallas_call(
        ssd_send_kernel,
        grid_spec=pltpu.PrefetchScalarGridSpec(
            num_scalar_prefetch=0,
            grid=(nb,),
            in_specs=[blk, blk, row, mat, mat, whole, whole, whole, whole],
            out_specs=[
                pl.BlockSpec((heads, rows, 128), lambda k: (0, 0, 0)),
                hm,
                hm,
                row,
                pl.BlockSpec((2, tok, 128), lambda k: (0, 0, 0)),
            ],
            scratch_shapes=[
                pltpu.VMEM((heads, 128, 128), F32),
                pltpu.VMEM((heads, 128, 128), F32),
                pltpu.VMEM((heads, 128), F32),
            ],
        ),
        out_shape=[
            jax.ShapeDtypeStruct((heads, rows, 128), BF),
            jax.ShapeDtypeStruct((heads, tok, width), BF),
            jax.ShapeDtypeStruct((heads, tok, width), BF),
            jax.ShapeDtypeStruct((heads, tok), F32),
            jax.ShapeDtypeStruct((2, tok, 128), BF),
        ],
        compiler_params=pltpu.CompilerParams(vmem_limit_bytes=60 << 20),
        cost_estimate=pl.CostEstimate(
            flops=3 * 10**9, bytes_accessed=10**7, transcendentals=10**5
        ),
        name="ssd_send",
    )(x, y, at, b, c, keys, values, q, do)


VM = pl.BlockSpec(memory_space=pltpu.VMEM)
SM = pl.BlockSpec(memory_space=pltpu.SMEM)
HB = pl.BlockSpec(memory_space=pltpu.HBM)


def scan_kernel(recv, back):
    n = recv.shape[0]
    state = jnp.zeros((128, 128), F32)
    for e in range(n):
        back[e, 0:128, :] = state.astype(BF)
        if e < n - 1:
            t = recv[e, 384:400, :].astype(F32)
            keep = jnp.exp(t[0:1] + t[1:2] + t[2:3])
            state = keep * state + recv[e, 0:128, :].astype(F32)
    pull = jnp.zeros((128, 128), F32)
    for e in reversed(range(n)):
        back[e, 128:256, :] = pull.astype(BF)
        if e > 0:
            t = recv[e, 384:400, :].astype(F32)
            keep = jnp.exp(t[0:1] + t[1:2] + t[2:3])
            pull = keep * pull + recv[e, 128:256, :].astype(F32)


def scan(recv):
    n = recv.shape[0]
    return pl.pallas_call(
        scan_kernel,
        in_specs=[VM],
        out_specs=VM,
        out_shape=jax.ShapeDtypeStruct((n, 256, 128), BF),
        compiler_params=pltpu.CompilerParams(vmem_limit_bytes=20 << 20),
        name="scan",
    )(recv)


def sort_keys(order, inverse, recv, ks, vs):
    for e in range(16):
        inverse[order[e]] = e
    for b in range(32):
        src = inverse[b if b < 16 else 31 - b]
        o = 0 if b < 16 else 32
        ks[32 * b : 32 * b + 32, :] = recv[src, 256 + o : 288 + o, :]
        vs[32 * b : 32 * b + 32, :] = recv[src, 320 + o : 352 + o, :]


def item_at(order, size, i):
    first = order[lax.axis_index("seq")]
    per = size // 32
    n0 = (first + per) // per
    late = (i >= n0).astype(jnp.int32)
    g = i - late * n0
    block = jnp.where(late == 1, 31 - first, first)
    kr = iota((size, 256), 0)
    key_at = (g * per + kr // 32) * 256 + lax.axis_index("head") * 32 + kr % 32
    bias = jnp.where(key_at <= block * 256 + iota((size, 256), 1), 0.0, NEG)
    return pl.multiple_of(g * size, size), pl.multiple_of(late * 256, 256), bias


def attn_stat_kernel(order, recv, *refs):
    qd, (stat, mate, ks, vs, inverse) = refs[:8], refs[8:]
    heads = len(qd)
    scale = LOG2E * 128**-0.5
    sort_keys(order, inverse, recv, ks, vs)
    stat[0] = jnp.full((heads, 512), NEG, F32)
    stat[1:] = jnp.zeros((2, heads, 512), F32)

    def item(i, carry):
        kat, rat, bias = item_at(order, 256, i)
        kg = ks[pl.ds(kat, 256), :]
        vg = vs[pl.ds(kat, 256), :]
        for h in range(heads):
            s = dot(kg, qd[h][0, pl.ds(rat, 256), :], 1, 1) * scale + bias
            dp = dot(vg, qd[h][1, pl.ds(rat, 256), :], 1, 1)
            at = (slice(h, h + 1), pl.ds(rat, 256))
            old = stat[0, *at]
            top = jnp.maximum(old, jnp.max(s, axis=0, keepdims=True))
            p = jnp.exp2(s - top)
            fix = jnp.exp2(old - top)
            stat[0, *at] = top
            stat[1, *at] = fix * stat[1, *at] + jnp.sum(p, axis=0, keepdims=True)
            stat[2, *at] = fix * stat[2, *at] + jnp.sum(p * dp, axis=0, keepdims=True)
        return carry

    lax.fori_loop(0, 5, item, 0)
    for i in range(3):
        mate[i] = turn_rows(stat[i], 1)


def attn_stat(order, recv, qd):
    heads = len(qd)
    return pl.pallas_call(
        attn_stat_kernel,
        in_specs=[SM] + [VM] * 9,
        out_specs=[VM, VM],
        out_shape=[jax.ShapeDtypeStruct((3, heads, 512), F32)] * 2,
        scratch_shapes=[
            pltpu.VMEM((1024, 128), BF),
            pltpu.VMEM((1024, 128), BF),
            pltpu.SMEM((16,), jnp.int32),
        ],
        compiler_params=pltpu.CompilerParams(vmem_limit_bytes=20 << 20),
        cost_estimate=pl.CostEstimate(
            flops=10**8, bytes_accessed=10**5, transcendentals=10**4
        ),
        name="attn_stat",
    )(order, recv, *qd)


def attn_grad_kernel(order, recv, *refs):
    qd, stats, send, dqt = refs[:8], refs[8:12], refs[12], refs[13:21]
    ks, vs, dk, dv, lse, delta, dqs, inverse, dqo, buf, sem = refs[21:]
    heads = len(qd)
    scale = 128**-0.5
    sort_keys(order, inverse, recv, ks, vs)
    tables = [[r[i] for i in range(3)] for r in stats]
    for m, v in zip((2, 6, 4), tables[1:]):
        v[:] = [turn_rows(x, m) for x in v]
    top = functools.reduce(jnp.maximum, [v[0] for v in tables])
    total = jnp.zeros_like(top)
    dsum = jnp.zeros_like(top)
    for v in tables:
        f = jnp.exp2(v[0] - top)
        total = total + f * v[1]
        dsum = dsum + f * v[2]
    lse[...] = top + jnp.log2(total)
    delta[...] = dsum / total
    dk[...] = jnp.zeros_like(dk)
    dv[...] = jnp.zeros_like(dv)
    dqs[...] = jnp.zeros_like(dqs)

    def item(i, carry):
        kat, rat, bias = item_at(order, 512, i)
        kg = ks[pl.ds(kat, 512), :]
        vg = vs[pl.ds(kat, 512), :]
        kt = kg.astype(F32).T.astype(BF)
        dkg = dk[pl.ds(kat, 512), :]
        dvg = dv[pl.ds(kat, 512), :]
        for h in range(heads):
            q = qd[h][0, pl.ds(rat, 256), :]
            do = qd[h][1, pl.ds(rat, 256), :]
            s = dot(kg, q, 1, 1) * (scale * LOG2E) + bias
            dp = dot(vg, do, 1, 1)
            p = jnp.exp2(s - lse[h : h + 1, pl.ds(rat, 256)])
            ds = (p * (dp - delta[h : h + 1, pl.ds(rat, 256)])).astype(BF)
            dvg = dvg + dot(p.astype(BF), do, 1, 0)
            dkg = dkg + dot(ds, q, 1, 0)
            dqs[h, :, pl.ds(rat, 256)] += dot(kt, ds, 1, 0)
        dk[pl.ds(kat, 512), :] = dkg
        dv[pl.ds(kat, 512), :] = dvg
        return carry

    lax.fori_loop(0, 3, item, 0)
    dqo[...] = (dqs[...] * scale).astype(BF)
    moves = [pltpu.make_async_copy(dqo.at[h], dqt[h], sem.at[h]) for h in range(heads)]
    for m in moves:
        m.start()
    for e in range(16):
        b = order[e]
        for j, (r, f) in enumerate(((dk, scale), (dv, 1.0))):
            lo = r[pl.ds(pl.multiple_of(b * 32, 32), 32), :]
            hi = r[pl.ds(pl.multiple_of((31 - b) * 32, 32), 32), :]
            buf[e, 64 * j : 32 + 64 * j, :] = (lo * f).astype(BF)
            buf[e, 32 + 64 * j : 64 + 64 * j, :] = (hi * f).astype(BF)
    moves.append(pltpu.make_async_copy(buf, send, sem.at[heads]))
    moves[-1].start()
    for m in moves:
        m.wait()


def attn_grad(order, recv, qd, *stats):
    heads = len(qd)
    n = recv.shape[0]
    return pl.pallas_call(
        attn_grad_kernel,
        in_specs=[SM] + [VM] * 13,
        out_specs=[HB] * 9,
        out_shape=[pltpu.HBM((n, 128, 128), BF)] + [pltpu.HBM((128, 512), BF)] * 8,
        scratch_shapes=[
            pltpu.VMEM((1024, 128), BF),
            pltpu.VMEM((1024, 128), BF),
            pltpu.VMEM((1024, 128), F32),
            pltpu.VMEM((1024, 128), F32),
            pltpu.VMEM((heads, 512), F32),
            pltpu.VMEM((heads, 512), F32),
            pltpu.VMEM((heads, 128, 512), F32),
            pltpu.SMEM((16,), jnp.int32),
            pltpu.VMEM((heads, 128, 512), BF),
            pltpu.VMEM((n, 128, 128), BF),
            pltpu.SemaphoreType.DMA((heads + 1,)),
        ],
        compiler_params=pltpu.CompilerParams(vmem_limit_bytes=20 << 20),
        cost_estimate=pl.CostEstimate(
            flops=10**8, bytes_accessed=10**5, transcendentals=10**4
        ),
        name="attn_grad",
    )(order, recv, *qd, *stats)


STEP_HEADS = 4


def turned_columns(cum, k, table):
    cm = cum[:, k * BLOCK : (k + 1) * BLOCK]
    tl = jnp.exp(cm[:, BLOCK - 1 :] - cm)
    gap = jnp.zeros((BLOCK // 2 - cm.shape[0], BLOCK), F32)
    table[k] = jnp.concatenate([cm, gap, tl, gap], axis=0).T


def head_vectors(cum, h, nb):
    row = cum[pl.ds(h, 1), :]
    c = [row[:, k * BLOCK : (k + 1) * BLOCK] for k in range(nb)]
    total = [v[:, BLOCK - 1 :] for v in c]
    keep = [jnp.exp(t) for t in total]
    tail = [jnp.exp(t - v) for t, v in zip(total, c)]
    grow = [jnp.exp(v) for v in c]
    return c, keep, tail, grow


def ssd_local_kernel(
    xh, yh, cum, b_ref, c_ref,
    dxl, fp, line_ref, db_ref, dc_ref,
    g_s, dg_s, bt_s, ct_s, colp, dcol, drow,
):
    base = pl.program_id(0) * STEP_HEADS
    nh = cum.shape[0]
    nb = xh.shape[1] // BLOCK
    rows = iota((BLOCK, BLOCK), 0)
    lanes = iota((BLOCK, BLOCK), 1)

    @pl.when(base == 0)
    def _():
        dg_s[...] = jnp.zeros_like(dg_s)
        dcol[...] = jnp.zeros_like(dcol)
        drow[...] = jnp.zeros_like(drow)
        for k in range(nb):
            sl = slice(k * BLOCK, (k + 1) * BLOCK)
            b = b_ref[sl, :]
            c = c_ref[sl, :]
            g_s[k] = jnp.where(rows <= lanes, dot(b, c, 1, 1, HIGHEST), 0.0)
            bt_s[k] = b.T
            ct_s[k] = c.T
            turned_columns(cum, k, colp)

    turned = [pltpu.roll(colp[k], lax.rem(BLOCK - base, BLOCK), 1) for k in range(nb)]
    for hh in range(STEP_HEADS):
        h = base + hh
        c, keep, tail, grow = head_vectors(cum, h, nb)
        for k in range(nb):
            at = slice(k * BLOCK, (k + 1) * BLOCK)
            x = xh[hh, at, :]
            y = yh[hh, at, :]
            decay = jnp.exp(jnp.minimum(c[k] - turned[k][:, hh : hh + 1], 0.0))
            w = g_s[k] * decay
            t = dot(x, y, 1, 1) * decay
            dg_s[k] += t
            z = t * g_s[k]
            cs = (ct_s[k] * grow[k]).astype(BF)
            wy = dot(jnp.concatenate([w.astype(BF), cs], axis=0), y, 1, 0)
            dxl[hh, at, :] = wy[:BLOCK].astype(BF)
            if k > 0:
                fp[hh, nb - 2 + k] = wy[BLOCK:].astype(BF)
            if k < nb - 1:
                fp[hh, k] = dot((bt_s[k] * tail[k]).astype(BF), x, 1, 0).astype(BF)
            line = jnp.sum(z, axis=0, keepdims=True)
            drow[:, at] = jnp.where(iota((nh, BLOCK), 0) == h, line, drow[:, at])
            dcol[k] = jnp.where(lanes == h, jnp.sum(z, axis=1, keepdims=True), dcol[k])

    @pl.when(base == nh - STEP_HEADS)
    def _():
        for k in range(nb):
            sl = slice(k * BLOCK, (k + 1) * BLOCK)
            dg = jnp.where(rows <= lanes, dg_s[k], 0.0)
            db_ref[sl, :] = dot(dg, c_ref[sl, :], 1, 0, HIGHEST)
            dc_ref[sl, :] = dot(dg.T, b_ref[sl, :], 1, 0, HIGHEST)
            line_ref[:, sl] = drow[:, sl] - dcol[k].T[:nh]


def whole(*shape):
    return pl.BlockSpec(shape, lambda h: (0,) * len(shape))


def ssd_local(xh, yh, cum, b, c):
    heads, tok, width = xh.shape
    nb = tok // BLOCK
    per = pl.BlockSpec((STEP_HEADS, tok, width), lambda h: (h, 0, 0))
    sq = pltpu.VMEM((nb, 128, 128), F32)
    return pl.pallas_call(
        ssd_local_kernel,
        grid=(heads // STEP_HEADS,),
        in_specs=[per, per, whole(heads, tok), whole(tok, 128), whole(tok, 128)],
        out_specs=[
            per,
            pl.BlockSpec((STEP_HEADS, 2 * nb - 2, 128, 128), lambda h: (h, 0, 0, 0)),
            whole(heads, tok),
            whole(tok, 128),
            whole(tok, 128),
        ],
        out_shape=[
            jax.ShapeDtypeStruct((heads, tok, width), BF),
            jax.ShapeDtypeStruct((heads, 2 * nb - 2, 128, 128), BF),
            jax.ShapeDtypeStruct((heads, tok), F32),
            jax.ShapeDtypeStruct((tok, 128), F32),
            jax.ShapeDtypeStruct((tok, 128), F32),
        ],
        scratch_shapes=[sq] * 6 + [pltpu.VMEM((heads, tok), F32)],
        compiler_params=pltpu.CompilerParams(vmem_limit_bytes=60 << 20),
        cost_estimate=pl.CostEstimate(
            flops=4 * 10**9, bytes_accessed=10**7, transcendentals=10**6
        ),
        name="ssd_local",
    )(xh, yh, cum, b, c)


def ssd_grad_kernel(
    xh, yh, states, cum, b_ref, c_ref, dxl, fp, line_ref, dbl, dcl,
    dx_ref, da_ref, db_ref, dc_ref,
    dct, dbt, bt_s, ct_s, colp, drow, dxs,
):
    base = pl.program_id(0) * STEP_HEADS
    nh = cum.shape[0]
    nb = xh.shape[1] // BLOCK

    @pl.when(base == 0)
    def _():
        dct[...] = jnp.zeros_like(dct)
        dbt[...] = jnp.zeros_like(dbt)
        drow[...] = line_ref[...]
        for k in range(nb):
            sl = slice(k * BLOCK, (k + 1) * BLOCK)
            bt_s[k] = b_ref[sl, :].T
            ct_s[k] = c_ref[sl, :].T
            turned_columns(cum, k, colp)

    turned = [pltpu.roll(colp[k], lax.rem(BLOCK - base, BLOCK), 1) for k in range(nb)]
    for hh in range(STEP_HEADS):
        h = base + hh
        c, keep, tail, grow = head_vectors(cum, h, nb)
        state = [states[hh, 0:128, :].astype(F32)]
        for k in range(nb - 1):
            state.append(keep[k] * state[k] + fp[hh, k].astype(F32))
        pull = states[hh, 128:256, :].astype(F32)
        for k in reversed(range(nb)):
            at = slice(k * BLOCK, (k + 1) * BLOCK)
            x = xh[hh, at, :]
            y = yh[hh, at, :]
            sb = state[k].astype(BF)
            pb = pull.astype(BF)
            bs = (b_ref[at, :] * turned[k][:, 64 + hh : 65 + hh]).astype(BF)
            dx = dxl[hh, at, :].astype(F32) + dot(bs, pb, 1, 0)
            dxs[h, at, :] = dx.astype(BF)
            dcs = dot(sb, y, 1, 1) * grow[k]
            dct[k] += dcs
            dbs = dot(pb, x, 1, 1) * tail[k]
            dbt[k] += dbs
            vs = jnp.sum(dbs * bt_s[k], axis=0, keepdims=True)
            line = jnp.sum(dcs * ct_s[k], axis=0, keepdims=True) - vs
            cross = keep[k] * jnp.sum(state[k] * pull, axis=0, keepdims=True)
            last = jnp.sum(vs + cross, axis=1, keepdims=True)
            line = jnp.where(iota((1, BLOCK), 1) == BLOCK - 1, line + last, line)
            old = drow[:, at]
            drow[:, at] = jnp.where(iota((nh, BLOCK), 0) == h, old + line, old)
            if k > 0:
                pull = keep[k] * pull + fp[hh, nb - 2 + k].astype(F32)

    @pl.when(base == nh - STEP_HEADS)
    def _():
        late = (iota((BLOCK, BLOCK), 0) >= iota((BLOCK, BLOCK), 1)).astype(F32)
        for k in range(nb):
            sl = slice(k * BLOCK, (k + 1) * BLOCK)
            db_ref[sl, :] = dbl[sl, :] + dbt[k].T
            dc_ref[sl, :] = dcl[sl, :] + dct[k].T
            da_ref[:, sl] = dot(drow[:, sl], late, 1, 0, HIGHEST)
            dx_ref[sl] = jnp.swapaxes(dxs[:, sl, :], 0, 1)


def ssd_grad(xh, yh, states, cum, b, c, local):
    heads, tok, width = xh.shape
    nb = tok // BLOCK
    rows = states.shape[1]
    per = pl.BlockSpec((STEP_HEADS, tok, width), lambda h: (h, 0, 0))
    sq = pltpu.VMEM((nb, 128, 128), F32)
    return pl.pallas_call(
        ssd_grad_kernel,
        grid=(heads // STEP_HEADS,),
        in_specs=[
            per,
            per,
            pl.BlockSpec((STEP_HEADS, rows, 128), lambda h: (h, 0, 0)),
            whole(heads, tok),
            whole(tok, 128),
            whole(tok, 128),
            per,
            pl.BlockSpec((STEP_HEADS, 2 * nb - 2, 128, 128), lambda h: (h, 0, 0, 0)),
            whole(heads, tok),
            whole(tok, 128),
            whole(tok, 128),
        ],
        out_specs=[
            whole(tok, heads, width),
            whole(heads, tok),
            whole(tok, 128),
            whole(tok, 128),
        ],
        out_shape=[
            jax.ShapeDtypeStruct((tok, heads, width), BF),
            jax.ShapeDtypeStruct((heads, tok), F32),
            jax.ShapeDtypeStruct((tok, 128), F32),
            jax.ShapeDtypeStruct((tok, 128), F32),
        ],
        scratch_shapes=[sq] * 5
        + [pltpu.VMEM((heads, tok), F32), pltpu.VMEM((heads, tok, width), BF)],
        compiler_params=pltpu.CompilerParams(vmem_limit_bytes=60 << 20),
        cost_estimate=pl.CostEstimate(
            flops=6 * 10**9, bytes_accessed=10**7, transcendentals=10**6
        ),
        name="ssd_grad",
    )(xh, yh, states, cum, b, c, *local)


def finish_kernel(*refs):
    dqt, parts, (dq, dk, dv) = refs[:5], refs[5:13], refs[13:]
    total = functools.reduce(jnp.add, [r[...].astype(F32) for r in dqt])
    dq[...] = total.T.astype(BF)
    place = lax.axis_index("head")
    for m, r in enumerate(parts):
        h = place ^ m
        for j in range(2):
            to = pl.ds(pl.multiple_of(256 * j + 32 * h, 32), 32)
            dk[to, :] = r[32 * j : 32 * j + 32, :]
            dv[to, :] = r[64 + 32 * j : 96 + 32 * j, :]


def finish(dqt, parts):
    out = jax.ShapeDtypeStruct((512, 128), BF)
    return pl.pallas_call(
        finish_kernel,
        in_specs=[VM] * 13,
        out_specs=[VM, VM, VM],
        out_shape=[out, out, out],
        compiler_params=pltpu.CompilerParams(vmem_limit_bytes=16 << 20),
        name="finish",
    )(*dqt, *parts)


def swap(v, m):
    return lax.ppermute(v, "head", [(i, i ^ m) for i in range(8)])


def turn_rows(v, m):
    return jnp.concatenate([v[j ^ m : (j ^ m) + 1] for j in range(v.shape[0])], axis=0)


def join(a, b):
    top = jnp.maximum(a[0], b[0])
    f, g = jnp.exp2(a[0] - top), jnp.exp2(b[0] - top)
    return jnp.stack([top, f * a[1] + g * b[1], f * a[2] + g * b[2]])


def gather_heads(v, other=None):
    out = [v if other is None else after(v, other)] + [None] * 7
    for m in (2, 6, 4):
        out[m] = swap(v, m) if other is None else after(swap(v, m), other)
    for m in (0, 2, 6, 4):
        out[m + 1] = swap(out[m], 1)
    return out


def pair_sums_kernel(*refs):
    own, mates, outs, (held, sem) = refs[:3], refs[3:6], refs[6:9], refs[9:]
    moves = [pltpu.make_async_copy(r, held.at[i], sem.at[i]) for i, r in enumerate(own)]
    for m in moves:
        m.start()
    for m in moves:
        m.wait()
    for i in range(3):
        outs[i][...] = (held[i].astype(F32) + mates[i][...].astype(F32)).astype(BF)


def pair_sums(parts):
    mates = [swap(parts[m + 1], 1) for m in (0, 2, 4, 6)]
    out = jax.ShapeDtypeStruct(parts[0].shape, BF)
    sums = pl.pallas_call(
        pair_sums_kernel,
        in_specs=[HB] * 3 + [VM] * 3,
        out_specs=[VM] * 3,
        out_shape=[out] * 3,
        scratch_shapes=[
            pltpu.VMEM((3,) + parts[0].shape, BF),
            pltpu.SemaphoreType.DMA((3,)),
        ],
        compiler_params=pltpu.CompilerParams(vmem_limit_bytes=16 << 20),
        name="pair_sums",
    )(*[pltpu.with_memory_space_constraint(p, pltpu.HBM) for p in parts[2::2]], *mates[1:])
    return [parts[0], mates[0]], sums


def after(value, other):
    return lax.optimization_barrier((value, other))[0]


def per_device(
    ssd_input, log_decay, input_map, output_map, ssd_cotangent,
    queries, key_rows, value_rows, attn_cotangent, pair_order,
):
    tok, heads, width = ssd_input.shape
    b = input_map.reshape(tok, 128)
    c = output_map.reshape(tok, 128)
    send, xh, yh, cum, qd = ssd_send(
        ssd_input, ssd_cotangent, log_decay.T, b, c, key_rows, value_rows,
        queries.reshape(tok, 128), attn_cotangent.reshape(tok, 128),
    )
    recv = lax.all_to_all(send, "seq", 0, 0)
    local = ssd_local(xh, yh, cum, b, c)
    qds = gather_heads(qd, local[2])
    turned = scan(after(recv, qds))
    states = lax.all_to_all(turned, "seq", 0, 0)
    first, mate = attn_stat(pair_order, after(recv, turned), qds)
    stat = join(first, swap(mate, 1))
    rest = [swap(stat, m) for m in (2, 6, 4)]
    back, *dqt = attn_grad(pair_order, recv, qds, stat, *rest)
    back, *dqt = after([back, *dqt], states)
    kept, sums = pair_sums(dqt)
    dx, da, db, dc = ssd_grad(after(xh, (back, *sums)), yh, states, cum, b, c, local)
    back = lax.all_to_all(back, "seq", 0, 0)
    dqt = kept + [swap(sums[i], m) for i, m in ((0, 2), (2, 6), (1, 4))]
    dkv = jnp.sum(after(back, da).astype(F32), axis=0).astype(BF)
    parts = gather_heads(dkv)
    dq, dk, dv = finish(dqt, parts)
    return (
        dx,
        da.T,
        db.reshape(tok, 1, 128),
        dc.reshape(tok, 1, 128),
        dq.reshape(tok, 1, 128),
        dk,
        dv,
    )


def solution(mesh):
    tok = P("seq", "head", None)
    return jax.shard_map(
        per_device,
        mesh=mesh,
        in_specs=(
            tok, P("seq", "head"), tok, tok, tok, tok,
            P("seq", None), P("seq", None), tok, P(),
        ),
        out_specs=(tok, P("seq", "head"), tok, tok, tok, P("seq", None), P("seq", None)),
        check_vma=False,
    )
```
